128 devices in a mesh: wide: 16 (over y, z), narrow: 8 (over x, core).
Axes of the slice: x: 4, y: 4, z: 4, core: 2. Of those that a mesh axis runs over, the one named last changes fastest.
Arguments:
- queries: bfloat16 [32, 128, 2304], P('wide'), may hold values from -112 to 112
- new_kv: bfloat16 [32, 2, 128, 2304], P('wide', None, 'narrow'), may hold values from -4 to 4
- cache_pool: bfloat16 [32, 32, 2, 128, 2304], P('wide', 'narrow'), may hold values from -4 to 4
- page_table: int32 [32, 32], P('wide'), may hold values from 0 to 31, as said below
- cached_len: int32 [32], P('wide'), may hold values from 0 to 4096, as said below
- residual: bfloat16 [4096, 2304], P('wide'), may hold values from -0.1796875 to 0.1796875
- norm_gain: float32 [2304], replicated, may hold values from 0.1 to 1.9
- expert_ids: int32 [4096, 2], P('wide'), may hold values from 0 to 7, all different within a row; in each aligned block of 256 rows (0 to 255, 256 to 511, ...) at most 80 rows name the same one
- route_weight: float32 [4096, 2], P('wide'), may hold values from 0.1 to 1
- w_gate_up: bfloat16 [8, 2304, 2, 5760], P(None, 'narrow', None, 'wide'), may hold values from -0.125 to 0.125
- w_down: bfloat16 [8, 5760, 2304], P(None, 'wide', 'narrow'), may hold values from -0.078125 to 0.078125
Outputs:
- layer_out: bfloat16 [4096, 2304], P('wide', 'narrow')
The draws below stay inside these ranges and needn't reach their ends.
Inputs may be any that keep to these rules, and one draw needn't show every extreme that they name: `page_table`: for each request the 32 entries are distinct, and entry j lies in (j % 8) * 4 to (j % 8) * 4 + 3. `cached_len`: some request has exactly 4096 cached tokens. `expert_ids`: A token's two experts differ; among the 256 tokens of one index of wide no expert is named more than 80 times.
All inputs are finite; a program needn't handle non-finite values.
Results may differ from the reference program's by a relative error of at most 0.035.
Values may be sent and summed in bfloat16 or wider, within the bound.
No kernel may reach another device: no remote copies, remote signals or barrier semaphores. Data moves between devices by JAX's collectives and lax.ppermute only.
A program may use at most 192 MiB of HBM per device.

```python
import math
import jax
import jax.numpy as jnp
import numpy as np
from jax import lax

D = 2304
HEADS = 36
HD = 64
FF = 5760
E = 8
NEWTOK = 128
PAGE = 128
PG_DEV = 4
REQS = 32
TOKENS = 4096
TOKW = 256
MAXPG = 32
CAP = 80
N_WIDE = 16
N_NARROW = 8


def joint_draw(key):
    folded = jax.random.fold_in(key, 29)
    query_key, pair_key = jax.random.split(folded)
    queries = jnp.clip(jax.random.normal(query_key, (REQS, NEWTOK, D), jnp.float32), -4.0, 4.0)
    new_kv = jnp.clip(jax.random.normal(pair_key, (REQS, 2, NEWTOK, D), jnp.float32), -4.0, 4.0)
    return (queries, new_kv)


def draw_queries(key, part):
    return joint_draw(key)[0].astype(jnp.bfloat16)


def draw_new_kv(key, part):
    return joint_draw(key)[1].astype(jnp.bfloat16)


def draw_page_table(key, part):
    groups = MAXPG // PG_DEV
    scores = jax.random.randint(jax.random.fold_in(key, 31), (REQS, groups, PG_DEV), 0, 1 << 20)
    distinct = scores * PG_DEV + jnp.arange(PG_DEV, dtype=jnp.int32)[None, None, :]
    ranking = jnp.argsort(distinct, axis=2).astype(jnp.int32)
    slot_ids = jnp.arange(groups, dtype=jnp.int32)[None, :, None] * PG_DEV + ranking
    return jnp.transpose(slot_ids, (0, 2, 1)).reshape(REQS, MAXPG)


def draw_cached_len(key, part):
    longest = PAGE * MAXPG
    first_key, second_key = jax.random.split(jax.random.fold_in(key, 37))
    attempts = jax.random.randint(first_key, (REQS, 3), 0, longest + 1)
    lengths = jnp.min(attempts, axis=1)
    chosen = jax.random.randint(second_key, (), 0, REQS)
    return jnp.where(jnp.arange(REQS, dtype=jnp.int32) == chosen, longest, lengths).astype(jnp.int32)


def shard_levels(stream_key, extent, shards, smallest, top_value):
    level, own = 1.0, jax.random.fold_in(stream_key, 6)
    for dim, parts in shards:
        heights = jnp.exp(jax.random.uniform(jax.random.fold_in(own, dim), (parts,), jnp.float32, smallest / len(shards), top_value / len(shards)))
        level = level * jnp.repeat(heights, extent[dim] // parts).reshape([-1 if axis == dim else 1 for axis in range(len(extent))])
    return level


def shared_out(own_key, own, number, rows, amount, top, limit, lean):
    order = jax.random.permutation(own_key, amount)
    heavy_load, usual = load_shares(amount, rows * top, limit, lean, True), load_shares(amount, rows * top, limit, lean, False)
    places = jnp.arange(amount)

    def named(sizes, offset_by):
        used = int((sizes > 0).sum())
        fixed = max(1, used // 4)
        moved = fixed + (places - fixed + offset_by * (used - fixed)) % max(1, amount - fixed)
        return jnp.zeros((amount,), jnp.int32).at[order[jnp.where(places < fixed, places, moved)]].set(jnp.asarray(sizes, jnp.int32))

    sizes = jnp.where(number % 4 == 0, named(heavy_load, number // 4), named(usual, number - number // 4 - 1))
    mixed = jax.random.permutation(jax.random.fold_in(own, 3), amount)
    donor, receiver = mixed[0:amount // 2 * 2:2], mixed[1:amount // 2 * 2:2]
    slack = jnp.minimum(sizes[donor] - 1, limit - sizes[receiver]) // 2
    slack = jnp.where((donor == order[0]) | (receiver == order[0]) | (sizes[receiver] == 0), 0, jnp.maximum(slack, 0))
    moved = jax.random.randint(jax.random.fold_in(own, 4), (amount // 2,), 0, 1 << 20) % (slack + 1)
    sizes = sizes.at[donor].add(-moved).at[receiver].add(moved)
    labels = jnp.searchsorted(jnp.cumsum(sizes), jnp.arange(rows * top), side="right").astype(jnp.int32)
    table = labels.reshape(top, rows).T
    table = table[jax.random.permutation(jax.random.fold_in(own, 1), rows)]
    offset_by = jax.random.randint(jax.random.fold_in(own, 2), (rows, 1), 0, top)
    return jnp.take_along_axis(table, (jnp.arange(top)[None, :] + offset_by) % top, axis=1)


def load_shares(amount, total, reach, lean, full):
    portions = [(1 << 20) // math.isqrt(grade ** lean) + 1 for grade in range(1, amount + 1)]
    largest = reach if full else min(reach, max(-(-total // amount), total * portions[0] // sum(portions)))
    least = 1 if total - largest >= amount - 1 else 0
    holding, surplus = [largest] + [least] * (amount - 1), total - largest - least * (amount - 1)
    while surplus > 0:
        free = [i for i in range(1, amount) if holding[i] < largest] or [i for i in range(1, amount) if holding[i] < reach]
        pool, budget = sum([portions[i] for i in free]), surplus
        for i in free:
            more = min(reach - holding[i], max(1, budget * portions[i] // pool), surplus)
            holding[i] = holding[i] + more
            surplus = surplus - more
    return np.array(holding)


def centred(own_key, dims, width, limit, shards=(), kind=jnp.bfloat16):
    drawn = width * jax.random.normal(own_key, dims, jnp.float32)
    if shards:
        drawn = drawn * shard_levels(own_key, dims, shards, -0.22, 0.18)
    return jnp.clip(drawn, -limit, limit).astype(kind)


def setup_inputs(seed: int = 0) -> dict:
    key_list = jax.random.split(jax.random.key(seed), 12)
    queries = draw_queries(jax.random.fold_in(key_list[11], 71), 0)
    new_kv = draw_new_kv(jax.random.fold_in(key_list[11], 71), 0)
    cache_pool = centred(key_list[2], (REQS, MAXPG, 2, PAGE, D), 1.0, 4.0, ((0, 16), (1, 8)))
    page_table = draw_page_table(jax.random.fold_in(key_list[11], 71), 0)
    cached_len = draw_cached_len(jax.random.fold_in(key_list[11], 71), 0)
    residual = centred(key_list[5], (TOKENS, D), 0.03, 0.1796875, ((0, 16),))
    norm_gain = jnp.clip(1.0 + 0.18 * jax.random.normal(key_list[6], (D,), jnp.float32), 0.1, 1.9)
    expert_ids_keys = jax.random.split(jax.random.fold_in(key_list[7], 1), TOKENS // TOKW)
    expert_ids_turns = jax.random.permutation(jax.random.fold_in(key_list[7], 3), TOKENS // TOKW)
    expert_ids = jax.vmap(lambda own, number: shared_out(jax.random.fold_in(key_list[7], 2), own, number, TOKW, E, 2, CAP, 1))(expert_ids_keys, expert_ids_turns).reshape((TOKENS, 2))
    route_weight = jnp.clip(0.1 + 0.9 * jax.random.uniform(key_list[8], (TOKENS, 2), jnp.float32) ** shard_levels(key_list[8], (TOKENS, 2), ((0, 16),), -0.2, 0.2), 0.1, 1.0)
    w_gate_up = centred(key_list[9], (E, D, 2, FF), D ** -0.5, 0.125, ((1, 8), (3, 16)))
    w_down = centred(key_list[10], (E, FF, D), FF ** -0.5, 0.078125, ((1, 16), (2, 8)))
    return {"queries": queries, "new_kv": new_kv, "cache_pool": cache_pool, "page_table": page_table, "cached_len": cached_len, "residual": residual, "norm_gain": norm_gain, "expert_ids": expert_ids, "route_weight": route_weight, "w_gate_up": w_gate_up, "w_down": w_down}


NEG_FILL = -1e+30
SCORE_SCALE = 0.125
EPSILON = 1e-05

def attend_one(inputs):
    query_rows, new_pair, page_rows, table_row, length_one = inputs
    groups = N_NARROW
    local_new = NEWTOK // groups
    ordered = jnp.take(page_rows, table_row.astype(jnp.int32), axis=0)
    cache_keys = ordered[:, 0].astype(jnp.float32).reshape(PG_DEV, groups, PAGE, HEADS, HD)
    cache_vals = ordered[:, 1].astype(jnp.float32).reshape(PG_DEV, groups, PAGE, HEADS, HD)
    new_keys = new_pair[0].astype(jnp.float32).reshape(groups, local_new, HEADS, HD)
    new_vals = new_pair[1].astype(jnp.float32).reshape(groups, local_new, HEADS, HD)
    query_heads = query_rows.astype(jnp.float32).reshape(NEWTOK, HEADS, HD)
    cache_scores = jnp.einsum('qhd,inphd->hqinp', query_heads, cache_keys) * SCORE_SCALE
    new_scores = jnp.einsum('qhd,nchd->hqnc', query_heads, new_keys) * SCORE_SCALE
    page_index = jnp.arange(PG_DEV, dtype=jnp.int32)[:, None, None] * groups + jnp.arange(groups, dtype=jnp.int32)[None, :, None]
    cache_pos = page_index * PAGE + jnp.arange(PAGE, dtype=jnp.int32)[None, None, :]
    cache_valid = cache_pos < length_one
    new_pos = jnp.arange(NEWTOK, dtype=jnp.int32).reshape(groups, local_new)
    new_valid = new_pos[None, :, :] <= jnp.arange(NEWTOK, dtype=jnp.int32)[:, None, None]
    cache_scores = jnp.where(cache_valid[None, None], cache_scores, NEG_FILL)
    new_scores = jnp.where(new_valid[None], new_scores, NEG_FILL)
    score_top = jnp.maximum(lax.optimization_barrier(jnp.max(cache_scores, axis=(2, 3, 4))), lax.optimization_barrier(jnp.max(new_scores, axis=(2, 3))))
    cache_weights = jnp.where(cache_valid[None, None], jnp.exp(cache_scores - score_top[:, :, None, None, None]), 0.0)
    new_weights = jnp.where(new_valid[None], jnp.exp(new_scores - score_top[:, :, None, None]), 0.0)
    denominator = lax.optimization_barrier(jnp.sum(cache_weights, axis=(2, 4))) + lax.optimization_barrier(jnp.sum(new_weights, axis=3))
    cache_round = lax.optimization_barrier(cache_weights.astype(jnp.bfloat16)).astype(jnp.float32)
    new_round = lax.optimization_barrier(new_weights.astype(jnp.bfloat16)).astype(jnp.float32)
    numerator = jnp.einsum('hqinp,inphd->nqhd', cache_round, cache_vals) + jnp.einsum('hqnc,nchd->nqhd', new_round, new_vals)
    numerator = lax.optimization_barrier(numerator.astype(jnp.bfloat16)).astype(jnp.float32)
    denominator = lax.optimization_barrier(denominator.astype(jnp.bfloat16)).astype(jnp.float32)
    total_num = lax.optimization_barrier(jnp.sum(numerator, axis=0))
    total_den = lax.optimization_barrier(jnp.sum(denominator, axis=2))
    return (total_num / jnp.transpose(total_den)[:, :, None]).reshape(NEWTOK, D)

def reference(queries, new_kv, cache_pool, page_table, cached_len, residual, norm_gain, expert_ids, route_weight, w_gate_up, w_down):
    attention = lax.map(attend_one, (queries, new_kv, cache_pool, page_table, cached_len))
    hidden = residual.astype(jnp.float32) + attention.reshape(TOKENS, D)
    spread = lax.optimization_barrier(jnp.mean(hidden * hidden, axis=1, keepdims=True))
    normed = (hidden * lax.rsqrt(spread + EPSILON) * norm_gain).astype(jnp.bfloat16)
    block_ids = expert_ids.reshape(N_WIDE, TOKW * 2).astype(jnp.int32)
    onehot = (block_ids[:, :, None] == jnp.arange(E, dtype=jnp.int32)[None, None, :]).astype(jnp.int32)
    earlier = jnp.cumsum(onehot, axis=1) - onehot
    position = lax.optimization_barrier(jnp.sum(earlier * onehot, axis=2)).astype(jnp.int32)
    slot_ids = (block_ids * CAP + position).astype(jnp.int32)
    source_rows = jnp.repeat(normed.reshape(N_WIDE, TOKW, D), 2, axis=1)
    block_index = jnp.arange(N_WIDE, dtype=jnp.int32)[:, None]
    dispatched = jnp.zeros((N_WIDE, E * CAP, D), jnp.bfloat16).at[block_index, slot_ids].set(source_rows)
    grouped = dispatched.reshape(N_WIDE, E, CAP, D)
    gate_table = w_gate_up.reshape(E, D, 2 * FF)
    width_part = D // N_NARROW
    gate_up = jnp.zeros((N_WIDE, E, CAP, 2 * FF), jnp.float32)
    for group_index in range(N_NARROW):
        offset = group_index * width_part
        partial_term = jnp.einsum('wecd,edf->wecf', grouped[..., offset:offset + width_part].astype(jnp.float32), gate_table[:, offset:offset + width_part].astype(jnp.float32))
        gate_up = gate_up + lax.optimization_barrier(partial_term.astype(jnp.bfloat16)).astype(jnp.float32)
    activated = (jax.nn.silu(gate_up[..., :FF]) * gate_up[..., FF:]).astype(jnp.bfloat16)
    unit_part = FF // N_WIDE
    expert_out = jnp.zeros((N_WIDE, E, CAP, D), jnp.float32)
    for group_index in range(N_WIDE):
        offset = group_index * unit_part
        partial_term = jnp.einsum('wecf,efd->wecd', activated[..., offset:offset + unit_part].astype(jnp.float32), w_down[:, offset:offset + unit_part].astype(jnp.float32))
        expert_out = expert_out + lax.optimization_barrier(partial_term.astype(jnp.bfloat16)).astype(jnp.float32)
    flat_out = expert_out.reshape(N_WIDE, E * CAP, D)
    picked = jnp.take_along_axis(flat_out, slot_ids[:, :, None], axis=1).reshape(N_WIDE, TOKW, 2, D)
    mixing = route_weight.reshape(N_WIDE, TOKW, 2)
    mixed = mixing[:, :, 0:1] * picked[:, :, 0] + mixing[:, :, 1:2] * picked[:, :, 1]
    return (hidden + mixed.reshape(TOKENS, D)).astype(jnp.bfloat16)
```

```python
import functools

import jax
import jax.numpy as jnp
from jax import lax
from jax.experimental import pallas as pl
from jax.experimental.pallas import tpu as pltpu
from jax.sharding import PartitionSpec as P

HD = 64
CAP = 80
NEG_FILL = -(2.0**100)
SCORE_SCALE = 0.125
EPSILON = 1e-05
STAT_ROWS = 16
RING = 4


F32 = jnp.float32
BF16 = jnp.bfloat16


def nt_dot(a, b):
    return lax.dot_general(a, b, (((1,), (1,)), ((), ())), preferred_element_type=F32)


def tn_dot(a, b):
    return lax.dot_general(a, b, (((0,), (0,)), ((), ())), preferred_element_type=F32)


def attend_kernel(limit, place, q_ref, k_ref, v_ref, nk_ref, nv_ref, out_ref, top_sc, den_sc, *, share):
    req, group = pl.program_id(0), pl.program_id(1)
    new_len = q_ref.shape[1]
    pages, page_len = k_ref.shape[1], k_ref.shape[3]
    local_new = nk_ref.shape[2]
    pairs = q_ref.shape[2] // 128
    lane_at = pl.multiple_of(req * new_len, new_len)
    col = lax.broadcasted_iota(jnp.int32, (new_len, 128), 1)
    row = lax.broadcasted_iota(jnp.int32, (128, new_len), 0)
    page_row = lax.broadcasted_iota(jnp.int32, (page_len, 2 * new_len), 0)
    new_row = lax.broadcasted_iota(jnp.int32, (local_new, 2 * new_len), 0) + place[0] * local_new
    new_col = lax.broadcasted_iota(jnp.int32, (local_new, 2 * new_len), 1) % new_len
    new_valid = new_row <= new_col

    @pl.when((req == 0) & (group == 0))
    def _():
        top_sc[...] = jnp.zeros_like(top_sc)
        den_sc[...] = jnp.zeros_like(den_sc)

    for pair in range(pairs):
        at = slice(pair * 128, pair * 128 + 128)
        q = q_ref[0, :, at].astype(F32) * SCORE_SCALE
        both = jnp.concatenate([jnp.where(col < HD, q, 0.0), jnp.where(col < HD, 0.0, q)], axis=0).astype(BF16)
        parts = []
        for page in range(pages):
            s = nt_dot(k_ref[0, page, 0, :, at], both)
            parts.append(jnp.where(page_row < limit[req, page], s, NEG_FILL))
        parts.append(jnp.where(new_valid, nt_dot(nk_ref[0, 0, :, at], both), NEG_FILL))
        top = functools.reduce(jnp.maximum, [jnp.max(s, axis=0, keepdims=True) for s in parts])
        top = top.astype(BF16).astype(F32)
        weights = [jnp.exp(s - top) for s in parts]
        den = functools.reduce(jnp.add, [jnp.sum(w, axis=0, keepdims=True) for w in weights])
        low = jnp.concatenate([w.astype(BF16) for w in weights[:-1]], axis=0)
        values = jnp.concatenate([v_ref[0, page, 0, :, at] for page in range(pages)], axis=0)
        num = tn_dot(values, low) + tn_dot(nv_ref[0, 0, :, at], weights[-1].astype(BF16))
        num = jnp.where(row < HD, num[:, :new_len], num[:, new_len:]).astype(BF16)
        for piece in range(4):
            index = (group * pairs + pair) * 4 + piece
            dest = index // (share // 32)
            offset = pl.multiple_of((index - dest * (share // 32)) * 32, 32)
            out_ref[dest, pl.ds(offset, 32), pl.ds(lane_at, new_len)] = num[piece * 32 : piece * 32 + 32]
        head = (group * pairs + pair) * 2
        for half in range(2):
            lanes = slice(half * new_len, half * new_len + new_len)
            top_sc[head + half, :, pl.ds(lane_at, new_len)] = top[:, lanes]
            den_sc[head + half, :, pl.ds(lane_at, new_len)] = den[:, lanes]

    @pl.when((req == pl.num_programs(0) - 1) & (group == pl.num_programs(1) - 1))
    def _():
        for dest in range(out_ref.shape[0]):
            first = dest * share // HD
            stats = jnp.concatenate([top_sc[first : first + 8, 0, :], den_sc[first : first + 8, 0, :]], axis=0)
            out_ref[dest, share : share + STAT_ROWS, :] = stats.astype(BF16)


def attend(limit, place, queries, cache_pool, new_kv, dests):
    req_here, new_len, width = queries.shape
    pages, page_len = cache_pool.shape[1], cache_pool.shape[3]
    local_new = new_kv.shape[2]
    share = width // dests
    groups = 3
    block = width // groups
    heads = width // HD
    keys = pages * page_len + local_new
    return pl.pallas_call(
        functools.partial(attend_kernel, share=share),
        grid_spec=pltpu.PrefetchScalarGridSpec(
            num_scalar_prefetch=2,
            grid=(req_here, groups),
            in_specs=[
                pl.BlockSpec((1, new_len, block), lambda r, g, *_: (r, 0, g)),
                pl.BlockSpec((1, pages, 1, page_len, block), lambda r, g, *_: (r, 0, 0, 0, g)),
                pl.BlockSpec((1, pages, 1, page_len, block), lambda r, g, *_: (r, 0, 1, 0, g)),
                pl.BlockSpec((1, 1, local_new, block), lambda r, g, *_: (r, 0, 0, g)),
                pl.BlockSpec((1, 1, local_new, block), lambda r, g, *_: (r, 1, 0, g)),
            ],
            out_specs=pl.BlockSpec((dests, share + STAT_ROWS, req_here * new_len), lambda r, g, *_: (0, 0, 0)),
            scratch_shapes=[pltpu.VMEM((heads + 12, 1, req_here * new_len), F32)] * 2,
        ),
        out_shape=jax.ShapeDtypeStruct((dests, share + STAT_ROWS, req_here * new_len), BF16),
        cost_estimate=pl.CostEstimate(
            flops=4 * req_here * new_len * width * keys,
            bytes_accessed=cache_pool.size * 2 + queries.size * 2,
            transcendentals=req_here * heads * new_len * keys,
        ),
        name="attend",
    )(limit, place, queries, cache_pool, cache_pool, new_kv, new_kv)


def join_kernel(place, recv_ref, res_ref, gain_ref, slot_ref, placed_ref, hidden_ref, spread_sc, *, share):
    groups = recv_ref.shape[0]
    tokens = recv_ref.shape[2]
    slots = placed_ref.shape[0] * placed_ref.shape[1]
    padded = placed_ref.shape[2]
    tops = [recv_ref[g, share : share + 8, :].astype(F32) for g in range(groups)]
    top = functools.reduce(jnp.maximum, tops)
    scales = [jnp.exp(t - top) for t in tops]
    den = functools.reduce(jnp.add, [s * recv_ref[g, share + 8 : share + 16, :].astype(F32) for g, s in enumerate(scales)])
    offset = pl.multiple_of(place[0] % 2 * (HD // 2), HD // 2)
    total = res_ref[...]
    for g in range(groups):
        factor = scales[g] / den
        for head in range(5):
            spread_sc[g, head * HD : head * HD + HD, :] = jnp.broadcast_to(factor[head : head + 1, :], (HD, tokens))
        total = total + recv_ref[g, :share, :].astype(F32) * spread_sc[g, pl.ds(offset, share), :]
    hidden_ref[...] = total
    square = jnp.sum(total * total, axis=0, keepdims=True)
    high = square.astype(BF16).astype(F32)
    row = lax.broadcasted_iota(jnp.int32, (padded - share, tokens), 0)
    tail = jnp.where(row == 0, high, jnp.where(row == 1, square - high, 0.0)).astype(BF16)
    rows = jnp.concatenate([(total * gain_ref[...]).astype(BF16), tail], axis=0)
    at = lax.broadcasted_iota(jnp.int32, (slots, tokens), 0)
    picks = (at == slot_ref[0:1, :]) | (at == slot_ref[1:2, :])
    placed = nt_dot(jnp.where(picks, 1.0, 0.0).astype(BF16), rows)
    placed_ref[...] = placed.astype(BF16).reshape(placed_ref.shape)


def join(place, recv, residual, gain, slots, experts):
    groups, rows, tokens = recv.shape
    share = rows - STAT_ROWS
    padded = -(-(share + 2) // 128) * 128
    whole = lambda *shape: pl.BlockSpec(shape, lambda i, *_: (0,) * len(shape))
    return pl.pallas_call(
        functools.partial(join_kernel, share=share),
        grid_spec=pltpu.PrefetchScalarGridSpec(
            num_scalar_prefetch=1,
            grid=(1,),
            in_specs=[
                whole(groups, rows, tokens),
                whole(share, tokens),
                whole(share, 1),
                whole(2, tokens),
            ],
            out_specs=[whole(experts, CAP, padded), whole(share, tokens)],
            scratch_shapes=[pltpu.VMEM((groups, 5 * HD, tokens), F32)],
        ),
        out_shape=[
            jax.ShapeDtypeStruct((experts, CAP, padded), BF16),
            jax.ShapeDtypeStruct((share, tokens), F32),
        ],
        cost_estimate=pl.CostEstimate(
            flops=2 * experts * CAP * padded * tokens, bytes_accessed=recv.size * 2 + experts * CAP * padded * 2, transcendentals=0
        ),
        name="join",
    )(place, recv, residual, gain, slots)


def norm_kernel(recv_ref, out_ref, *, share):
    groups, rows, _ = recv_ref.shape
    blocks = [recv_ref[g].astype(F32) for g in range(groups)]
    square = functools.reduce(jnp.add, [b[:, share : share + 1] + b[:, share + 1 : share + 2] for b in blocks])
    scale = lax.rsqrt(square / (groups * share) + EPSILON)
    out_ref[...] = jnp.concatenate([b[:, :share] * scale for b in blocks], axis=1).astype(BF16)


def norm_rows(recv, share):
    groups, rows, _ = recv.shape
    return pl.pallas_call(
        functools.partial(norm_kernel, share=share),
        out_shape=jax.ShapeDtypeStruct((rows, groups * share), BF16),
        cost_estimate=pl.CostEstimate(flops=0, bytes_accessed=recv.size * 4, transcendentals=0),
        name="norm_rows",
    )(recv)


def expert_kernel(*refs, count):
    rows, (gate_up_ref, down_ref), outs = refs[:count], refs[count : count + 2], refs[count + 2 :]
    half = gate_up_ref.shape[1] // 2
    for x_ref, o_ref in zip(rows, outs):
        both = jnp.dot(x_ref[...], gate_up_ref[...], preferred_element_type=F32)
        gate, up = both[:, :half], both[:, half:]
        act = (gate / (1.0 + jnp.exp(-gate)) * up).astype(BF16)
        o_ref[...] = nt_dot(act, down_ref[...]).astype(BF16)


def expert(blocks, gate_up, down):
    width = down.shape[0]
    total = sum(b.shape[0] for b in blocks)
    return pl.pallas_call(
        functools.partial(expert_kernel, count=len(blocks)),
        out_shape=[jax.ShapeDtypeStruct(b.shape, BF16) for b in blocks],
        cost_estimate=pl.CostEstimate(
            flops=2 * total * width * (gate_up.shape[1] + down.shape[1]),
            bytes_accessed=4 * total * width + 2 * gate_up.size + 2 * down.size,
            transcendentals=total * down.shape[1],
        ),
        name="expert",
    )(*blocks, gate_up, down)


def mix_kernel(rows_ref, slot_ref, weight_ref, hidden_ref, out_ref):
    tokens = out_ref.shape[0]
    slots = rows_ref.shape[0]
    at = lax.broadcasted_iota(jnp.int32, (tokens, slots), 1)
    table = jnp.where(at == slot_ref[:, 0:1], weight_ref[:, 0:1], 0.0)
    table = table + jnp.where(at == slot_ref[:, 1:2], weight_ref[:, 1:2], 0.0)
    high = table.astype(BF16)
    low = (table - high.astype(F32)).astype(BF16)
    rows = rows_ref[...]
    mixed = jnp.dot(high, rows, preferred_element_type=F32) + jnp.dot(low, rows, preferred_element_type=F32)
    out_ref[...] = (hidden_ref[...] + mixed).astype(BF16)


def mix(rows, slots, weights, hidden):
    return pl.pallas_call(
        mix_kernel,
        out_shape=jax.ShapeDtypeStruct(hidden.shape, BF16),
        cost_estimate=pl.CostEstimate(flops=4 * hidden.size * rows.shape[0], bytes_accessed=rows.size * 2 + hidden.size * 6, transcendentals=0),
        name="mix",
    )(rows, slots, weights, hidden)


def ring_pairs(axis, step):
    pairs = []
    for index in range(RING * RING):
        y, z = divmod(index, RING)
        if axis == "y":
            y = (y + step) % RING
        else:
            z = (z + step) % RING
        pairs.append((index, y * RING + z))
    return pairs


def shift(x, axis, step):
    return lax.ppermute(x, "wide", ring_pairs(axis, step))


def local(
    queries,
    new_kv,
    cache_pool,
    page_table,
    cached_len,
    residual,
    norm_gain,
    expert_ids,
    route_weight,
    w_gate_up,
    w_down,
):
    narrow_count = lax.axis_size("narrow")
    narrow_pos = lax.axis_index("narrow").astype(jnp.int32)
    req_here, new_len, width = queries.shape
    slot_count, page_len = cache_pool.shape[1], cache_pool.shape[3]
    table_len = page_table.shape[1]
    token_rows = expert_ids.shape[0]
    expert_count = w_gate_up.shape[0]
    units = w_down.shape[1]
    share = width // narrow_count

    gate_up_all = lax.all_to_all(w_gate_up, "narrow", 0, 0, tiled=True)
    down_all = lax.all_to_all(jnp.transpose(w_down, (0, 2, 1)), "narrow", 0, 0, tiled=True)

    own_slots = narrow_pos * slot_count + jnp.arange(slot_count, dtype=jnp.int32)
    matches = page_table[:, None, :] == own_slots[None, :, None]
    logical = jnp.sum(jnp.where(matches, jnp.arange(table_len, dtype=jnp.int32)[None, None, :], 0), axis=2)
    limit = cached_len[:, None] - logical * page_len
    place = narrow_pos.reshape(1)
    sums = attend(limit, place, queries, cache_pool, new_kv, narrow_count)
    sums = lax.all_to_all(sums, "narrow", 0, 0, tiled=True)

    flat_ids = expert_ids.reshape(token_rows * 2)
    onehot = (flat_ids[:, None] == jnp.arange(expert_count, dtype=jnp.int32)[None, :]).astype(BF16)
    order = jnp.arange(token_rows * 2, dtype=jnp.int32)
    earlier = jnp.dot((order[:, None] > order[None, :]).astype(BF16), onehot, preferred_element_type=F32)
    position = jnp.sum(earlier * onehot.astype(F32), axis=1).astype(jnp.int32)
    slots = (flat_ids * CAP + position).reshape(token_rows, 2)

    res_share = lax.dynamic_slice_in_dim(residual, narrow_pos * share, share, 1).astype(F32).T
    gain_share = lax.dynamic_slice_in_dim(norm_gain, narrow_pos * share, share, 0)[:, None]
    placed, hidden = join(place, sums, res_share, gain_share, slots.T, expert_count)
    placed = lax.all_to_all(placed, "narrow", 0, 0, tiled=True)
    rows = norm_rows(placed, share)

    half = CAP // 2

    def gather(block, axis, cut):
        before, after = shift(block, axis, 1), shift(block, axis, -1)
        far = shift(before[:cut], axis, 1), shift(after[cut:], axis, -1)
        return before, after, far

    pieces = []
    for first, second, block in (("z", "y", rows[:half]), ("y", "z", rows[half:])):
        before, after, far = gather(block, first, 24)
        four = jnp.concatenate([block, before, after, *far], axis=0)
        pieces.append((four, *gather(four, second, 2 * half)))
    gate_up = jnp.pad(gate_up_all.reshape(width, 2, units), ((0, 0), (0, 0), (0, -units % 128)))
    gate_up = gate_up.reshape(width, -1)
    down = jnp.pad(down_all.reshape(width, units), ((0, 0), (0, -units % 128)))
    near = expert([pieces[0][0], pieces[0][1], pieces[0][2], pieces[1][0], pieces[1][1], pieces[1][2]], gate_up, down)
    far = expert([*pieces[0][3], *pieces[1][3]], gate_up, down)

    def scatter(own, before, after, far_before, far_after, axis):
        cut = far_before.shape[0]
        via = shift(far_before, axis, 1), shift(far_after, axis, -1)
        up = jnp.concatenate([(after[:cut].astype(F32) + via[0].astype(F32)).astype(BF16), after[cut:]], axis=0)
        dn = jnp.concatenate([before[:cut], (before[cut:].astype(F32) + via[1].astype(F32)).astype(BF16)], axis=0)
        got = shift(up, axis, 1), shift(dn, axis, -1)
        return own.astype(F32) + got[0].astype(F32) + got[1].astype(F32)

    halves = []
    for color, (first, second) in enumerate((("z", "y"), ("y", "z"))):
        own, before, after = near[3 * color : 3 * color + 3]
        four = scatter(own, before, after, far[2 * color], far[2 * color + 1], second).astype(BF16)
        parts = [four[i * half : (i + 1) * half] for i in range(3)]
        halves.append(scatter(*parts, four[3 * half : 3 * half + 24], four[3 * half + 24 :], first).astype(BF16))
    out_rows = jnp.concatenate(halves, axis=0)
    out_rows = jnp.transpose(out_rows.reshape(CAP, narrow_count, share), (1, 0, 2))
    out_rows = lax.all_to_all(out_rows, "narrow", 0, 0, tiled=True)
    return mix(out_rows.reshape(expert_count * CAP, share), slots, route_weight, hidden.T)


def solution(mesh):
    return jax.shard_map(
        local,
        mesh=mesh,
        in_specs=(
            P("wide", None, None),
            P("wide", None, "narrow", None),
            P("wide", "narrow", None, None, None),
            P("wide", None),
            P("wide"),
            P("wide", None),
            P(),
            P("wide", None),
            P("wide", None),
            P(None, "narrow", None, "wide"),
            P(None, "wide", "narrow"),
        ),
        out_specs=P("wide", "narrow"),
        check_vma=False,
    )
```

```python
import functools

import jax
import jax.numpy as jnp
from jax import lax
from jax.experimental import pallas as pl
from jax.experimental.pallas import tpu as pltpu
from jax.sharding import PartitionSpec as P

HD = 64
CAP = 80
NEG_FILL = -(2.0**100)
SCORE_SCALE = 0.125
EPSILON = 1e-05
STAT_ROWS = 16
RING = 4
STEPS = (2, 1, -1)


F32 = jnp.float32
BF16 = jnp.bfloat16


def nt_dot(a, b):
    return lax.dot_general(a, b, (((1,), (1,)), ((), ())), preferred_element_type=F32)


def tn_dot(a, b):
    return lax.dot_general(a, b, (((0,), (0,)), ((), ())), preferred_element_type=F32)


def attend_kernel(table, length, place, q_ref, k_ref, v_ref, nk_ref, nv_ref, out_ref, top_sc, den_sc, *, share):
    groups = out_ref.shape[0]
    req, group = pl.program_id(0), pl.program_id(1)
    new_len = q_ref.shape[1]
    pages, page_len = k_ref.shape[1], k_ref.shape[3]
    local_new = nk_ref.shape[2]
    pairs = q_ref.shape[2] // 128
    lane_at = pl.multiple_of(req * new_len, new_len)
    col = lax.broadcasted_iota(jnp.int32, (new_len, 128), 1)
    row = lax.broadcasted_iota(jnp.int32, (128, new_len), 0)
    page_row = lax.broadcasted_iota(jnp.int32, (page_len, 2 * new_len), 0)
    new_row = lax.broadcasted_iota(jnp.int32, (local_new, 2 * new_len), 0) + place[0] * local_new
    new_col = lax.broadcasted_iota(jnp.int32, (local_new, 2 * new_len), 1) % new_len
    new_valid = new_row <= new_col
    logical = [place[0] + i * groups for i in range(pages)]
    places = [table[req, j] - place[0] * pages for j in logical]
    limits = [length[req] - j * page_len for j in logical]

    @pl.when((req == 0) & (group == 0))
    def _():
        top_sc[...] = jnp.zeros_like(top_sc)
        den_sc[...] = jnp.zeros_like(den_sc)

    for pair in range(pairs):
        at = slice(pair * 128, pair * 128 + 128)
        q = q_ref[0, :, at].astype(F32) * SCORE_SCALE
        both = jnp.concatenate([jnp.where(col < HD, q, 0.0), jnp.where(col < HD, 0.0, q)], axis=0).astype(BF16)
        parts = [
            jnp.where(page_row < limits[i], nt_dot(k_ref[0, places[i], 0, :, at], both), NEG_FILL) for i in range(pages)
        ]
        parts.append(jnp.where(new_valid, nt_dot(nk_ref[0, 0, :, at], both), NEG_FILL))
        top = functools.reduce(jnp.maximum, [jnp.max(s, axis=0, keepdims=True) for s in parts])
        top = top.astype(BF16).astype(F32)
        weights = [jnp.exp(s - top) for s in parts]
        den = functools.reduce(jnp.add, [jnp.sum(w, axis=0, keepdims=True) for w in weights])
        low = jnp.concatenate([w.astype(BF16) for w in weights[:-1]], axis=0)
        values = jnp.concatenate([v_ref[0, places[i], 0, :, at] for i in range(pages)], axis=0)
        num = tn_dot(values, low) + tn_dot(nv_ref[0, 0, :, at], weights[-1].astype(BF16))
        num = jnp.where(row < HD, num[:, :new_len], num[:, new_len:]).astype(BF16)
        for piece in range(4):
            index = (group * pairs + pair) * 4 + piece
            dest = index // (share // 32)
            offset = pl.multiple_of((index - dest * (share // 32)) * 32, 32)
            out_ref[dest, pl.ds(offset, 32), pl.ds(lane_at, new_len)] = num[piece * 32 : piece * 32 + 32]
        head = (group * pairs + pair) * 2
        for half in range(2):
            lanes = slice(half * new_len, half * new_len + new_len)
            top_sc[head + half, :, pl.ds(lane_at, new_len)] = top[:, lanes]
            den_sc[head + half, :, pl.ds(lane_at, new_len)] = den[:, lanes]

    @pl.when((req == pl.num_programs(0) - 1) & (group == pl.num_programs(1) - 1))
    def _():
        for dest in range(out_ref.shape[0]):
            first = dest * share // HD
            stats = jnp.concatenate([top_sc[first : first + 8, 0, :], den_sc[first : first + 8, 0, :]], axis=0)
            out_ref[dest, share : share + STAT_ROWS, :] = stats.astype(BF16)


def attend(table, length, place, queries, cache_pool, new_kv, dests):
    req_here, new_len, width = queries.shape
    pages, page_len = cache_pool.shape[1], cache_pool.shape[3]
    local_new = new_kv.shape[2]
    share = width // dests
    groups = 3
    block = width // groups
    heads = width // HD
    keys = pages * page_len + local_new
    return pl.pallas_call(
        functools.partial(attend_kernel, share=share),
        grid_spec=pltpu.PrefetchScalarGridSpec(
            num_scalar_prefetch=3,
            grid=(req_here, groups),
            in_specs=[
                pl.BlockSpec((1, new_len, block), lambda r, g, *_: (r, 0, g)),
                pl.BlockSpec((1, pages, 1, page_len, block), lambda r, g, *_: (r, 0, 0, 0, g)),
                pl.BlockSpec((1, pages, 1, page_len, block), lambda r, g, *_: (r, 0, 1, 0, g)),
                pl.BlockSpec((1, 1, local_new, block), lambda r, g, *_: (r, 0, 0, g)),
                pl.BlockSpec((1, 1, local_new, block), lambda r, g, *_: (r, 1, 0, g)),
            ],
            out_specs=pl.BlockSpec((dests, share + STAT_ROWS, req_here * new_len), lambda r, g, *_: (0, 0, 0)),
            scratch_shapes=[pltpu.VMEM((heads + 12, 1, req_here * new_len), F32)] * 2,
        ),
        out_shape=jax.ShapeDtypeStruct((dests, share + STAT_ROWS, req_here * new_len), BF16),
        cost_estimate=pl.CostEstimate(
            flops=4 * req_here * new_len * width * keys,
            bytes_accessed=cache_pool.size * 2 + queries.size * 2,
            transcendentals=req_here * heads * new_len * keys,
        ),
        compiler_params=pltpu.CompilerParams(vmem_limit_bytes=20 << 20),
        name="attend",
    )(table, length, place, queries, cache_pool, cache_pool, new_kv, new_kv)


def join_kernel(place, recv_ref, res_ref, gain_ref, slot_ref, placed_ref, hidden_ref, spread_sc, *, share):
    groups = recv_ref.shape[0]
    tokens = recv_ref.shape[2]
    slots = placed_ref.shape[0] * placed_ref.shape[1]
    padded = placed_ref.shape[2]
    tops = [recv_ref[g, share : share + 8, :].astype(F32) for g in range(groups)]
    top = functools.reduce(jnp.maximum, tops)
    scales = [jnp.exp(t - top) for t in tops]
    den = functools.reduce(jnp.add, [s * recv_ref[g, share + 8 : share + 16, :].astype(F32) for g, s in enumerate(scales)])
    offset = pl.multiple_of(place[0] % 2 * (HD // 2), HD // 2)
    total = res_ref[...]
    for g in range(groups):
        factor = scales[g] / den
        for head in range(5):
            spread_sc[g, head * HD : head * HD + HD, :] = jnp.broadcast_to(factor[head : head + 1, :], (HD, tokens))
        total = total + recv_ref[g, :share, :].astype(F32) * spread_sc[g, pl.ds(offset, share), :]
    hidden_ref[...] = total
    square = jnp.sum(total * total, axis=0, keepdims=True)
    high = square.astype(BF16).astype(F32)
    row = lax.broadcasted_iota(jnp.int32, (padded - share, tokens), 0)
    tail = jnp.where(row == 0, high, jnp.where(row == 1, square - high, 0.0)).astype(BF16)
    rows = jnp.concatenate([(total * gain_ref[...]).astype(BF16), tail], axis=0)
    at = lax.broadcasted_iota(jnp.int32, (slots, tokens), 0)
    picks = (at == slot_ref[0:1, :]) | (at == slot_ref[1:2, :])
    placed = nt_dot(jnp.where(picks, 1.0, 0.0).astype(BF16), rows)
    placed_ref[...] = placed.astype(BF16).reshape(placed_ref.shape)


def join(place, recv, residual, gain, slots, experts):
    groups, rows, tokens = recv.shape
    share = rows - STAT_ROWS
    padded = -(-(share + 2) // 128) * 128
    whole = lambda *shape: pl.BlockSpec(shape, lambda i, *_: (0,) * len(shape))
    return pl.pallas_call(
        functools.partial(join_kernel, share=share),
        grid_spec=pltpu.PrefetchScalarGridSpec(
            num_scalar_prefetch=1,
            grid=(1,),
            in_specs=[
                whole(groups, rows, tokens),
                whole(share, tokens),
                whole(share, 1),
                whole(2, tokens),
            ],
            out_specs=[whole(experts, CAP, padded), whole(share, tokens)],
            scratch_shapes=[pltpu.VMEM((groups, 5 * HD, tokens), F32)],
        ),
        out_shape=[
            jax.ShapeDtypeStruct((experts, CAP, padded), BF16),
            jax.ShapeDtypeStruct((share, tokens), F32),
        ],
        cost_estimate=pl.CostEstimate(
            flops=2 * experts * CAP * padded * tokens, bytes_accessed=recv.size * 2 + experts * CAP * padded * 2, transcendentals=0
        ),
        compiler_params=pltpu.CompilerParams(vmem_limit_bytes=10 << 20),
        name="join",
    )(place, recv, residual, gain, slots)


def norm_kernel(recv_ref, out_ref, *, share):
    groups, rows, _ = recv_ref.shape
    blocks = [recv_ref[g].astype(F32) for g in range(groups)]
    square = functools.reduce(jnp.add, [b[:, share : share + 1] + b[:, share + 1 : share + 2] for b in blocks])
    scale = lax.rsqrt(square / (groups * share) + EPSILON)
    out_ref[...] = jnp.concatenate([b[:, :share] * scale for b in blocks], axis=1).astype(BF16)


def norm_rows(recv, share):
    groups, rows, _ = recv.shape
    return pl.pallas_call(
        functools.partial(norm_kernel, share=share),
        out_shape=jax.ShapeDtypeStruct((rows, groups * share), BF16),
        cost_estimate=pl.CostEstimate(flops=0, bytes_accessed=recv.size * 4, transcendentals=0),
        compiler_params=pltpu.CompilerParams(vmem_limit_bytes=4 << 20),
        name="norm_rows",
    )(recv)


def stack_kernel(*refs):
    out_ref = refs[-1]
    for i, ref in enumerate(refs[:-1]):
        out_ref[i] = ref[...]


def stack(blocks):
    rows, width = blocks[0].shape
    return pl.pallas_call(
        stack_kernel,
        out_shape=jax.ShapeDtypeStruct((len(blocks), rows, width), BF16),
        cost_estimate=pl.CostEstimate(flops=0, bytes_accessed=4 * len(blocks) * rows * width, transcendentals=0),
        compiler_params=pltpu.CompilerParams(vmem_limit_bytes=4 << 20),
        name="stack",
    )(*blocks).reshape(len(blocks) * rows, width)


def expert_kernel(*refs, count):
    blocks, gate_up_ref, down_ref = refs[:count], refs[count], refs[count + 1]
    outs, (x_sc, both_sc, y_sc, sems) = refs[count + 2 : 2 * count + 2], refs[2 * count + 2 :]
    rows = blocks[0].shape[0]
    half = gate_up_ref.shape[1] // 2
    tile = 256
    loads = [pltpu.make_async_copy(b, x_sc.at[i // 2, pl.ds(i % 2 * rows, rows)], sems.at[i]) for i, b in enumerate(blocks)]
    stores = [pltpu.make_async_copy(y_sc.at[i // 2, pl.ds(i % 2 * rows, rows)], o, sems.at[count + i]) for i, o in enumerate(outs)]
    for load in loads:
        load.start()
    for step in range(count // 2):
        loads[2 * step].wait()
        loads[2 * step + 1].wait()

        @pl.loop(0, gate_up_ref.shape[1] // tile)
        def _(j):
            lanes = pl.ds(pl.multiple_of(j * tile, tile), tile)
            both_sc[:, lanes] = jnp.dot(x_sc[step], gate_up_ref[:, lanes], preferred_element_type=F32)

        gate, up = both_sc[:, :half], both_sc[:, half:]
        act = (gate / (1.0 + jnp.exp(-gate)) * up).astype(BF16)

        @pl.loop(0, down_ref.shape[0] // tile)
        def _(j):
            lanes = pl.ds(pl.multiple_of(j * tile, tile), tile)
            y_sc[step, :, lanes] = nt_dot(act, down_ref[lanes, :]).astype(BF16)

        stores[2 * step].start()
        stores[2 * step + 1].start()
    for copy in stores:
        copy.wait()


def expert(blocks, gate_up, down):
    rows, width = blocks[0].shape
    count = len(blocks)
    total = count * rows
    held = pl.BlockSpec(memory_space=pltpu.VMEM)
    anywhere = pl.BlockSpec(memory_space=pl.ANY)
    return pl.pallas_call(
        functools.partial(expert_kernel, count=count),
        in_specs=[anywhere] * count + [held, held],
        out_specs=[anywhere] * count,
        out_shape=[jax.ShapeDtypeStruct((rows, width), BF16)] * count,
        scratch_shapes=[
            pltpu.VMEM((count // 2, 2 * rows, width), BF16),
            pltpu.VMEM((2 * rows, gate_up.shape[1]), F32),
            pltpu.VMEM((count // 2, 2 * rows, width), BF16),
            pltpu.SemaphoreType.DMA((2 * count,)),
        ],
        cost_estimate=pl.CostEstimate(
            flops=2 * total * width * (gate_up.shape[1] + down.shape[1]),
            bytes_accessed=4 * total * width + 2 * gate_up.size + 2 * down.size,
            transcendentals=total * down.shape[1],
        ),
        compiler_params=pltpu.CompilerParams(vmem_limit_bytes=30 << 20),
        name="expert",
    )(*blocks, gate_up, down)


def total_of(refs):
    return functools.reduce(jnp.add, [ref[...].astype(F32) for ref in refs])


def add_kernel(*refs):
    outs = refs[4:]
    rows = outs[0].shape[0]
    for i, out in enumerate(outs):
        at = slice(i * rows, i * rows + rows)
        out[...] = functools.reduce(jnp.add, [ref[at, :].astype(F32) for ref in refs[:4]]).astype(BF16)


def add_blocks(blocks):
    rows, width = blocks[0].shape
    return pl.pallas_call(
        add_kernel,
        out_shape=[jax.ShapeDtypeStruct((rows // 4, width), BF16)] * 4,
        cost_estimate=pl.CostEstimate(flops=0, bytes_accessed=10 * rows * width, transcendentals=0),
        compiler_params=pltpu.CompilerParams(vmem_limit_bytes=8 << 20),
        name="add_blocks",
    )(*blocks)


def finish_kernel(*refs):
    out_ref = refs[-1]
    groups, _, share = out_ref.shape
    both = jnp.concatenate([total_of(refs[:4]), total_of(refs[4:8])], axis=0).astype(BF16)
    for g in range(groups):
        out_ref[g] = both[:, g * share : (g + 1) * share]


def finish(blocks, groups):
    rows, width = blocks[0].shape
    return pl.pallas_call(
        finish_kernel,
        out_shape=jax.ShapeDtypeStruct((groups, 2 * rows, width // groups), BF16),
        cost_estimate=pl.CostEstimate(flops=0, bytes_accessed=20 * rows * width, transcendentals=0),
        compiler_params=pltpu.CompilerParams(vmem_limit_bytes=8 << 20),
        name="finish",
    )(*blocks)


def mix_kernel(rows_ref, slot_ref, weight_ref, hidden_ref, out_ref):
    tokens = out_ref.shape[1]
    slots = rows_ref.shape[0]
    at = lax.broadcasted_iota(jnp.int32, (slots, tokens), 0)
    table = jnp.where(at == slot_ref[0:1, :], weight_ref[0:1, :], 0.0)
    table = table + jnp.where(at == slot_ref[1:2, :], weight_ref[1:2, :], 0.0)
    high = table.astype(BF16)
    low = (table - high.astype(F32)).astype(BF16)
    rows = rows_ref[...]
    out_ref[...] = (hidden_ref[...] + (tn_dot(rows, high) + tn_dot(rows, low))).astype(BF16)


def mix(rows, slots, weights, hidden):
    return pl.pallas_call(
        mix_kernel,
        out_shape=jax.ShapeDtypeStruct(hidden.shape, BF16),
        cost_estimate=pl.CostEstimate(flops=4 * hidden.size * rows.shape[0], bytes_accessed=rows.size * 2 + hidden.size * 6, transcendentals=0),
        compiler_params=pltpu.CompilerParams(vmem_limit_bytes=6 << 20),
        name="mix",
    )(rows, slots, weights, hidden)


def ring_pairs(axis, step):
    pairs = []
    for index in range(RING * RING):
        y, z = divmod(index, RING)
        if axis == "y":
            y = (y + step) % RING
        else:
            z = (z + step) % RING
        pairs.append((index, y * RING + z))
    return pairs


def shift(x, axis, step):
    return lax.ppermute(x, "wide", ring_pairs(axis, step))


def local(
    queries,
    new_kv,
    cache_pool,
    page_table,
    cached_len,
    residual,
    norm_gain,
    expert_ids,
    route_weight,
    w_gate_up,
    w_down,
):
    narrow_count = lax.axis_size("narrow")
    narrow_pos = lax.axis_index("narrow").astype(jnp.int32)
    req_here, new_len, width = queries.shape
    token_rows = expert_ids.shape[0]
    expert_count = w_gate_up.shape[0]
    units = w_down.shape[1]
    share = width // narrow_count

    down_all = lax.all_to_all(jnp.transpose(w_down, (0, 2, 1)), "narrow", 0, 0, tiled=True)

    place = narrow_pos.reshape(1)
    sums = attend(page_table, cached_len, place, queries, cache_pool, new_kv, narrow_count)
    sums, down_all = lax.optimization_barrier((sums, down_all))
    sums = lax.all_to_all(sums, "narrow", 0, 0, tiled=True)

    flat_ids = expert_ids.reshape(token_rows * 2)
    onehot = (flat_ids[:, None] == jnp.arange(expert_count, dtype=jnp.int32)[None, :]).astype(BF16)
    order = jnp.arange(token_rows * 2, dtype=jnp.int32)
    earlier = jnp.dot((order[:, None] > order[None, :]).astype(BF16), onehot, preferred_element_type=F32)
    position = jnp.sum(earlier * onehot.astype(F32), axis=1).astype(jnp.int32)
    slots = (flat_ids * CAP + position).reshape(token_rows, 2)

    res_share = lax.dynamic_slice_in_dim(residual, narrow_pos * share, share, 1).astype(F32).T
    gain_share = lax.dynamic_slice_in_dim(norm_gain, narrow_pos * share, share, 0)[:, None]
    placed, hidden = join(place, sums, res_share, gain_share, slots.T, expert_count)
    placed = lax.all_to_all(placed, "narrow", 0, 0, tiled=True)
    w_gate_up, placed = lax.optimization_barrier((w_gate_up, placed))
    gate_up_all = lax.all_to_all(w_gate_up, "narrow", 0, 0, tiled=True)
    rows = norm_rows(placed, share)

    half = CAP // 2

    def around(block, axis):
        return [block, *(shift(block, axis, step) for step in STEPS)]

    four = [stack(around(block, axis)) for block, axis in ((rows[:half], "z"), (rows[half:], "y"))]
    near = [around(four[0], "y"), around(four[1], "z")]
    gate_up = jnp.pad(gate_up_all.reshape(width, 2, units), ((0, 0), (0, 0), (0, -units % 128)))
    gate_up = gate_up.reshape(width, -1)
    down = jnp.pad(down_all.reshape(width, units), ((0, 0), (0, -units % 128)))
    outs = expert([block for pair in zip(*near) for block in pair], gate_up, down)

    def back(blocks, axis):
        return [blocks[0], *(shift(block, axis, -step) for block, step in zip(blocks[1:], STEPS))]

    four = [add_blocks(back(outs[0::2], "y")), add_blocks(back(outs[1::2], "z"))]
    out_rows = finish([*back(four[0], "z"), *back(four[1], "y")], narrow_count)
    out_rows = lax.all_to_all(out_rows, "narrow", 0, 0, tiled=True)
    return mix(out_rows.reshape(expert_count * CAP, share), slots.T, route_weight.T, hidden).T


def solution(mesh):
    return jax.shard_map(
        local,
        mesh=mesh,
        in_specs=(
            P("wide", None, None),
            P("wide", None, "narrow", None),
            P("wide", "narrow", None, None, None),
            P("wide", None),
            P("wide"),
            P("wide", None),
            P(),
            P("wide", None),
            P("wide", None),
            P(None, "narrow", None, "wide"),
            P(None, "wide", "narrow"),
        ),
        out_specs=P("wide", "narrow"),
        check_vma=False,
    )
```

```python
import functools

import jax
import jax.numpy as jnp
from jax import lax
from jax.experimental import pallas as pl
from jax.experimental.pallas import tpu as pltpu
from jax.sharding import PartitionSpec as P


HD = 64
CAP = 80
NEG_FILL = -(2.0**100)
SCORE_SCALE = 0.125
EPSILON = 1e-05
STAT_ROWS = 16
RING = 4
STEPS = (2, 1, -1)


F32 = jnp.float32
BF16 = jnp.bfloat16


def nt_dot(a, b):
    return lax.dot_general(a, b, (((1,), (1,)), ((), ())), preferred_element_type=F32)


def tn_dot(a, b):
    return lax.dot_general(a, b, (((0,), (0,)), ((), ())), preferred_element_type=F32)


def attend_kernel(table, length, place, q_ref, k_ref, v_ref, nk_ref, nv_ref, out_ref, top_sc, den_sc, *, share):
    groups = out_ref.shape[0]
    req, group = pl.program_id(0), pl.program_id(1)
    new_len = q_ref.shape[1]
    pages, page_len = k_ref.shape[1], k_ref.shape[3]
    local_new = nk_ref.shape[2]
    pairs = q_ref.shape[2] // 128
    lane_at = pl.multiple_of(req * new_len, new_len)
    col = lax.broadcasted_iota(jnp.int32, (new_len, 128), 1)
    row = lax.broadcasted_iota(jnp.int32, (128, new_len), 0)
    page_row = lax.broadcasted_iota(jnp.int32, (page_len, 2 * new_len), 0)
    new_row = lax.broadcasted_iota(jnp.int32, (local_new, 2 * new_len), 0) + place[0] * local_new
    new_col = lax.broadcasted_iota(jnp.int32, (local_new, 2 * new_len), 1) % new_len
    new_valid = new_row <= new_col
    logical = [place[0] + i * groups for i in range(pages)]
    places = [table[req, j] - place[0] * pages for j in logical]
    limits = [length[req] - j * page_len for j in logical]

    @pl.when((req == 0) & (group == 0))
    def _():
        top_sc[...] = jnp.zeros_like(top_sc)
        den_sc[...] = jnp.zeros_like(den_sc)

    for pair in range(pairs):
        at = slice(pair * 128, pair * 128 + 128)
        q = q_ref[0, :, at].astype(F32) * SCORE_SCALE
        both = jnp.concatenate([jnp.where(col < HD, q, 0.0), jnp.where(col < HD, 0.0, q)], axis=0).astype(BF16)
        parts = [
            jnp.where(page_row < limits[i], nt_dot(k_ref[0, places[i], 0, :, at], both), NEG_FILL) for i in range(pages)
        ]
        parts.append(jnp.where(new_valid, nt_dot(nk_ref[0, 0, :, at], both), NEG_FILL))
        top = functools.reduce(jnp.maximum, [jnp.max(s, axis=0, keepdims=True) for s in parts])
        top = top.astype(BF16).astype(F32)
        weights = [jnp.exp(s - top) for s in parts]
        den = functools.reduce(jnp.add, [jnp.sum(w, axis=0, keepdims=True) for w in weights])
        low = jnp.concatenate([w.astype(BF16) for w in weights[:-1]], axis=0)
        values = jnp.concatenate([v_ref[0, places[i], 0, :, at] for i in range(pages)], axis=0)
        num = tn_dot(values, low) + tn_dot(nv_ref[0, 0, :, at], weights[-1].astype(BF16))
        num = jnp.where(row < HD, num[:, :new_len], num[:, new_len:]).astype(BF16)
        for piece in range(4):
            index = (group * pairs + pair) * 4 + piece
            dest = index // (share // 32)
            offset = pl.multiple_of((index - dest * (share // 32)) * 32, 32)
            out_ref[dest, pl.ds(offset, 32), pl.ds(lane_at, new_len)] = num[piece * 32 : piece * 32 + 32]
        head = (group * pairs + pair) * 2
        for half in range(2):
            lanes = slice(half * new_len, half * new_len + new_len)
            top_sc[head + half, :, pl.ds(lane_at, new_len)] = top[:, lanes]
            den_sc[head + half, :, pl.ds(lane_at, new_len)] = den[:, lanes]

    @pl.when((req == pl.num_programs(0) - 1) & (group == pl.num_programs(1) - 1))
    def _():
        for dest in range(out_ref.shape[0]):
            first = dest * share // HD
            stats = jnp.concatenate([top_sc[first : first + 8, 0, :], den_sc[first : first + 8, 0, :]], axis=0)
            out_ref[dest, share : share + STAT_ROWS, :] = stats.astype(BF16)


def attend(table, length, place, queries, cache_pool, new_kv, dests):
    req_here, new_len, width = queries.shape
    pages, page_len = cache_pool.shape[1], cache_pool.shape[3]
    local_new = new_kv.shape[2]
    share = width // dests
    groups = 3
    block = width // groups
    heads = width // HD
    keys = pages * page_len + local_new
    return pl.pallas_call(
        functools.partial(attend_kernel, share=share),
        grid_spec=pltpu.PrefetchScalarGridSpec(
            num_scalar_prefetch=3,
            grid=(req_here, groups),
            in_specs=[
                pl.BlockSpec((1, new_len, block), lambda r, g, *_: (r, 0, g)),
                pl.BlockSpec((1, pages, 1, page_len, block), lambda r, g, *_: (r, 0, 0, 0, g)),
                pl.BlockSpec((1, pages, 1, page_len, block), lambda r, g, *_: (r, 0, 1, 0, g)),
                pl.BlockSpec((1, 1, local_new, block), lambda r, g, *_: (r, 0, 0, g)),
                pl.BlockSpec((1, 1, local_new, block), lambda r, g, *_: (r, 1, 0, g)),
            ],
            out_specs=pl.BlockSpec((dests, share + STAT_ROWS, req_here * new_len), lambda r, g, *_: (0, 0, 0)),
            scratch_shapes=[pltpu.VMEM((heads + 12, 1, req_here * new_len), F32)] * 2,
        ),
        out_shape=jax.ShapeDtypeStruct((dests, share + STAT_ROWS, req_here * new_len), BF16),
        cost_estimate=pl.CostEstimate(
            flops=4 * req_here * new_len * width * keys,
            bytes_accessed=cache_pool.size * 2 + queries.size * 2,
            transcendentals=req_here * heads * new_len * keys,
        ),
        compiler_params=pltpu.CompilerParams(vmem_limit_bytes=60 << 20),
        name="attend",
    )(table, length, place, queries, cache_pool, cache_pool, new_kv, new_kv)


def join_kernel(place, recv_ref, res_ref, gain_ref, slot_ref, placed_ref, hidden_ref, spread_sc, *, share):
    groups = recv_ref.shape[0]
    tokens = recv_ref.shape[2]
    slots = placed_ref.shape[0] * placed_ref.shape[1]
    padded = placed_ref.shape[2]
    tops = [recv_ref[g, share : share + 8, :].astype(F32) for g in range(groups)]
    top = functools.reduce(jnp.maximum, tops)
    scales = [jnp.exp(t - top) for t in tops]
    den = functools.reduce(jnp.add, [s * recv_ref[g, share + 8 : share + 16, :].astype(F32) for g, s in enumerate(scales)])
    offset = pl.multiple_of(place[0] % 2 * (HD // 2), HD // 2)
    total = res_ref[...]
    for g in range(groups):
        factor = scales[g] / den
        for head in range(5):
            spread_sc[g, head * HD : head * HD + HD, :] = jnp.broadcast_to(factor[head : head + 1, :], (HD, tokens))
        total = total + recv_ref[g, :share, :].astype(F32) * spread_sc[g, pl.ds(offset, share), :]
    hidden_ref[...] = total
    square = jnp.sum(total * total, axis=0, keepdims=True)
    high = square.astype(BF16).astype(F32)
    row = lax.broadcasted_iota(jnp.int32, (padded - share, tokens), 0)
    tail = jnp.where(row == 0, high, jnp.where(row == 1, square - high, 0.0)).astype(BF16)
    rows = jnp.concatenate([(total * gain_ref[...]).astype(BF16), tail], axis=0)
    at = lax.broadcasted_iota(jnp.int32, (slots, tokens), 0)
    picks = (at == slot_ref[0:1, :]) | (at == slot_ref[1:2, :])
    placed = nt_dot(jnp.where(picks, 1.0, 0.0).astype(BF16), rows)
    placed_ref[...] = placed.astype(BF16).reshape(placed_ref.shape)


def join(place, recv, residual, gain, slots, experts):
    groups, rows, tokens = recv.shape
    share = rows - STAT_ROWS
    padded = -(-(share + 2) // 128) * 128
    whole = lambda *shape: pl.BlockSpec(shape, lambda i, *_: (0,) * len(shape))
    return pl.pallas_call(
        functools.partial(join_kernel, share=share),
        grid_spec=pltpu.PrefetchScalarGridSpec(
            num_scalar_prefetch=1,
            grid=(1,),
            in_specs=[
                whole(groups, rows, tokens),
                whole(share, tokens),
                whole(share, 1),
                whole(2, tokens),
            ],
            out_specs=[whole(experts, CAP, padded), whole(share, tokens)],
            scratch_shapes=[pltpu.VMEM((groups, 5 * HD, tokens), F32)],
        ),
        out_shape=[
            jax.ShapeDtypeStruct((experts, CAP, padded), BF16),
            jax.ShapeDtypeStruct((share, tokens), F32),
        ],
        cost_estimate=pl.CostEstimate(
            flops=2 * experts * CAP * padded * tokens, bytes_accessed=recv.size * 2 + experts * CAP * padded * 2, transcendentals=0
        ),
        compiler_params=pltpu.CompilerParams(vmem_limit_bytes=10 << 20),
        name="join",
    )(place, recv, residual, gain, slots)


def norm_kernel(recv_ref, out_ref, *, share):
    groups, _, _ = recv_ref.shape
    blocks = [recv_ref[g].astype(F32) for g in range(groups)]
    square = functools.reduce(jnp.add, [b[:, share : share + 1] + b[:, share + 1 : share + 2] for b in blocks])
    scale = lax.rsqrt(square / (groups * share) + EPSILON)
    out_ref[...] = jnp.concatenate([b[:, :share] * scale for b in blocks], axis=1).astype(BF16)


def norm_rows(recv, share):
    groups, rows, _ = recv.shape
    return pl.pallas_call(
        functools.partial(norm_kernel, share=share),
        out_shape=jax.ShapeDtypeStruct((rows, groups * share), BF16),
        cost_estimate=pl.CostEstimate(flops=0, bytes_accessed=recv.size * 4, transcendentals=0),
        compiler_params=pltpu.CompilerParams(vmem_limit_bytes=4 << 20),
        name="norm_rows",
    )(recv)


def stack_kernel(*refs):
    blocks, outs = refs[:4], refs[4:]
    for i, ref in enumerate(blocks):
        outs[i // 2][i % 2] = ref[...]


def stack(blocks):
    rows, width = blocks[0].shape
    pairs = pl.pallas_call(
        stack_kernel,
        out_shape=[jax.ShapeDtypeStruct((2, rows, width), BF16)] * 2,
        cost_estimate=pl.CostEstimate(flops=0, bytes_accessed=16 * rows * width, transcendentals=0),
        compiler_params=pltpu.CompilerParams(vmem_limit_bytes=4 << 20),
        name="stack",
    )(*blocks)
    return [pair.reshape(2 * rows, width) for pair in pairs]


def expert_kernel(*refs, count):
    blocks, gate_up_ref, down_ref = refs[:count], refs[count], refs[count + 1]
    outs, (x_sc, weight_sc, both_sc, y_sc, sems) = refs[count + 2 : 2 * count + 2], refs[2 * count + 2 :]
    rows = blocks[0].shape[0]
    groups, _, units = gate_up_ref.shape
    share = x_sc.shape[1] // groups
    half = weight_sc.shape[1] // 2
    tile = 256
    loads = [pltpu.make_async_copy(b, x_sc.at[pl.ds(i * rows, rows)], sems.at[i]) for i, b in enumerate(blocks)]
    stores = [pltpu.make_async_copy(y_sc.at[pl.ds(i * rows, rows)], o, sems.at[count + i]) for i, o in enumerate(outs)]
    for load in loads:
        load.start()
    for g in range(groups):
        weight_sc[g * share : g * share + share, :units] = gate_up_ref[g, :share]
        weight_sc[g * share : g * share + share, half : half + units] = gate_up_ref[g, share:]
    for load in loads:
        load.wait()

    @pl.loop(0, 2 * half // tile)
    def _(j):
        lanes = pl.ds(pl.multiple_of(j * tile, tile), tile)
        both_sc[:, lanes] = jnp.dot(x_sc[...], weight_sc[:, lanes], preferred_element_type=F32)

    gate, up = both_sc[:, :units], both_sc[:, half : half + units]
    act = (gate / (1.0 + jnp.exp(-gate)) * up).astype(BF16)

    @pl.loop(0, down_ref.shape[0] // tile)
    def _(j):
        lanes = pl.ds(pl.multiple_of(j * tile, tile), tile)
        y_sc[:, lanes] = nt_dot(act, down_ref[lanes, :]).astype(BF16)

    for copy in stores:
        copy.start()
    for copy in stores:
        copy.wait()


def expert(blocks, gate_up, down):
    rows, width = blocks[0].shape
    units = down.shape[1]
    count = len(blocks)
    total = count * rows
    packed = 2 * (-(-units // 128) * 128)
    held = pl.BlockSpec(memory_space=pltpu.VMEM)
    anywhere = pl.BlockSpec(memory_space=pl.ANY)
    return pl.pallas_call(
        functools.partial(expert_kernel, count=count),
        in_specs=[anywhere] * count + [held] * 2,
        out_specs=[anywhere] * count,
        out_shape=[jax.ShapeDtypeStruct((rows, width), BF16)] * count,
        scratch_shapes=[
            pltpu.VMEM((total, width), BF16),
            pltpu.VMEM((width, packed), BF16),
            pltpu.VMEM((total, packed), F32),
            pltpu.VMEM((total, width), BF16),
            pltpu.SemaphoreType.DMA((2 * count,)),
        ],
        cost_estimate=pl.CostEstimate(
            flops=6 * total * width * units,
            bytes_accessed=4 * total * width + 6 * width * units,
            transcendentals=total * units,
        ),
        compiler_params=pltpu.CompilerParams(vmem_limit_bytes=26 << 20),
        name="expert",
    )(*blocks, gate_up, down)


def total_of(refs):
    return functools.reduce(jnp.add, [ref[...].astype(F32) for ref in refs])


def add_kernel(*refs):
    outs = refs[6:]
    rows = outs[0].shape[0]
    for i, out in enumerate(outs):
        at = slice(i % 2 * rows, i % 2 * rows + rows)
        some = refs[:3] if i < 2 else refs[3:6]
        out[...] = functools.reduce(jnp.add, [ref[at, :].astype(F32) for ref in some]).astype(BF16)


def add_blocks(low, high):
    rows, width = low[0].shape
    return pl.pallas_call(
        add_kernel,
        out_shape=[jax.ShapeDtypeStruct((rows // 2, width), BF16)] * 4,
        cost_estimate=pl.CostEstimate(flops=0, bytes_accessed=16 * rows * width, transcendentals=0),
        compiler_params=pltpu.CompilerParams(vmem_limit_bytes=8 << 20),
        name="add_blocks",
    )(*low, *high)


def finish_kernel(*refs):
    out_ref = refs[-1]
    groups, _, share = out_ref.shape
    both = jnp.concatenate([total_of(refs[:4]), total_of(refs[4:8])], axis=0).astype(BF16)
    for g in range(groups):
        out_ref[g] = both[:, g * share : (g + 1) * share]


def finish(blocks, groups):
    rows, width = blocks[0].shape
    return pl.pallas_call(
        finish_kernel,
        out_shape=jax.ShapeDtypeStruct((groups, 2 * rows, width // groups), BF16),
        cost_estimate=pl.CostEstimate(flops=0, bytes_accessed=20 * rows * width, transcendentals=0),
        compiler_params=pltpu.CompilerParams(vmem_limit_bytes=8 << 20),
        name="finish",
    )(*blocks)


def mix_kernel(rows_ref, slot_ref, weight_ref, hidden_ref, out_ref):
    tokens = out_ref.shape[1]
    slots = rows_ref.shape[0]
    at = lax.broadcasted_iota(jnp.int32, (slots, tokens), 0)
    table = jnp.where(at == slot_ref[0:1, :], weight_ref[0:1, :], 0.0)
    table = table + jnp.where(at == slot_ref[1:2, :], weight_ref[1:2, :], 0.0)
    high = table.astype(BF16)
    low = (table - high.astype(F32)).astype(BF16)
    rows = rows_ref[...]
    out_ref[...] = (hidden_ref[...] + (tn_dot(rows, high) + tn_dot(rows, low))).astype(BF16)


def mix(rows, slots, weights, hidden):
    return pl.pallas_call(
        mix_kernel,
        out_shape=jax.ShapeDtypeStruct(hidden.shape, BF16),
        cost_estimate=pl.CostEstimate(flops=4 * hidden.size * rows.shape[0], bytes_accessed=rows.size * 2 + hidden.size * 6, transcendentals=0),
        compiler_params=pltpu.CompilerParams(vmem_limit_bytes=6 << 20),
        name="mix",
    )(rows, slots, weights, hidden)


def ring_pairs(axis, step):
    pairs = []
    for index in range(RING * RING):
        y, z = divmod(index, RING)
        if axis == "y":
            y = (y + step) % RING
        else:
            z = (z + step) % RING
        pairs.append((index, y * RING + z))
    return pairs


def shift(x, axis, step):
    return lax.ppermute(x, "wide", ring_pairs(axis, step))


def local(
    queries,
    new_kv,
    cache_pool,
    page_table,
    cached_len,
    residual,
    norm_gain,
    expert_ids,
    route_weight,
    w_gate_up,
    w_down,
):
    narrow_count = lax.axis_size("narrow")
    narrow_pos = lax.axis_index("narrow").astype(jnp.int32)
    _, _, width = queries.shape
    token_rows = expert_ids.shape[0]
    expert_count = w_gate_up.shape[0]
    units = w_down.shape[1]
    share = width // narrow_count

    def exchange(x):
        return lax.all_to_all(x, "narrow", 0, 0, tiled=True)

    down_all = exchange(jnp.transpose(w_down, (0, 2, 1)))
    place = narrow_pos.reshape(1)
    sums = attend(page_table, cached_len, place, queries, cache_pool, new_kv, narrow_count)
    sums, down_all, w_gate_up = lax.optimization_barrier((sums, down_all, w_gate_up))
    later = jnp.concatenate([w_gate_up[:, :, 0], w_gate_up[:, :, 1]], axis=1)
    sums = exchange(sums)

    flat_ids = expert_ids.reshape(token_rows * 2)
    onehot = (flat_ids[:, None] == jnp.arange(expert_count, dtype=jnp.int32)[None, :]).astype(BF16)
    order = jnp.arange(token_rows * 2, dtype=jnp.int32)
    earlier = jnp.dot((order[:, None] > order[None, :]).astype(BF16), onehot, preferred_element_type=F32)
    position = jnp.sum(earlier * onehot.astype(F32), axis=1).astype(jnp.int32)
    slots = (flat_ids * CAP + position).reshape(token_rows, 2)

    res_share = lax.dynamic_slice_in_dim(residual, narrow_pos * share, share, 1).astype(F32).T
    gain_share = lax.dynamic_slice_in_dim(norm_gain, narrow_pos * share, share, 0)[:, None]
    placed, hidden = join(place, sums, res_share, gain_share, slots.T, expert_count)
    placed = exchange(placed)
    later, placed = lax.optimization_barrier((later, placed))
    later = exchange(later)
    down_all = down_all.reshape(width, units)
    rows = norm_rows(placed, share)

    half = CAP // 2

    def around(block, axis):
        return [block, *(shift(block, axis, step) for step in STEPS)]

    near, far = [], []
    for first, second, block in (("z", "y", rows[:half]), ("y", "z", rows[half:])):
        low, high = stack(around(block, first))
        before_low, after_high = shift(low, second, 1), shift(high, second, -1)
        before_high, after_low = shift(high, second, 1), shift(low, second, -1)
        near += [low, high, before_low, before_high, after_low, after_high]
        far += [shift(before_low, second, 1), shift(after_high, second, -1)]
    near = list(expert(near, later, down_all))
    near[0], *far = lax.optimization_barrier((near[0], *far))
    far = expert(far, later, down_all)

    def back(blocks, axis):
        return [blocks[0], *(shift(block, axis, -step) for block, step in zip(blocks[1:], STEPS))]

    def joined(a, b):
        return (a.astype(F32) + b.astype(F32)).astype(BF16)

    four = []
    for color, second in enumerate(("y", "z")):
        low, high, before_low, before_high, after_low, after_high = near[6 * color : 6 * color + 6]
        got_low = shift(before_low, second, -1)
        got_high = shift(after_high, second, 1)
        via_low, via_high = shift(far[2 * color], second, 1), shift(far[2 * color + 1], second, -1)
        more_low, more_high = shift(joined(after_low, via_low), second, 1), shift(joined(before_high, via_high), second, -1)
        four.append(add_blocks([low, got_low, more_low], [high, got_high, more_high]))
    out_rows = finish([*back(four[0], "z"), *back(four[1], "y")], narrow_count)
    out_rows = exchange(out_rows)
    return mix(out_rows.reshape(expert_count * CAP, share), slots.T, route_weight.T, hidden).T


def solution(mesh):
    return jax.shard_map(
        local,
        mesh=mesh,
        in_specs=(
            P("wide", None, None),
            P("wide", None, "narrow", None),
            P("wide", "narrow", None, None, None),
            P("wide", None),
            P("wide"),
            P("wide", None),
            P(),
            P("wide", None),
            P("wide", None),
            P(None, "narrow", None, "wide"),
            P(None, "wide", "narrow"),
        ),
        out_specs=P("wide", "narrow"),
        check_vma=False,
    )
```

```python
import functools

import jax
import jax.numpy as jnp
from jax import lax
from jax.experimental import pallas as pl
from jax.experimental.pallas import tpu as pltpu
from jax.sharding import PartitionSpec as P


HD = 64
CAP = 80
NEG_FILL = -(2.0**100)
SCORE_SCALE = 0.125
EPSILON = 1e-05
STAT_ROWS = 16
RING = 4
STEPS = (2, 1, -1)


F32 = jnp.float32
BF16 = jnp.bfloat16


def nt_dot(a, b):
    return lax.dot_general(a, b, (((1,), (1,)), ((), ())), preferred_element_type=F32)


def tn_dot(a, b):
    return lax.dot_general(a, b, (((0,), (0,)), ((), ())), preferred_element_type=F32)


def attend_kernel(table, length, place, q_ref, k_ref, v_ref, nk_ref, nv_ref, out_ref, top_sc, den_sc, *, share):
    groups = out_ref.shape[0]
    req, group = pl.program_id(0), pl.program_id(1)
    new_len = q_ref.shape[1]
    pages, page_len = k_ref.shape[1], k_ref.shape[3]
    local_new = nk_ref.shape[2]
    pairs = q_ref.shape[2] // 128
    lane_at = pl.multiple_of(req * new_len, new_len)
    col = lax.broadcasted_iota(jnp.int32, (new_len, 128), 1)
    row = lax.broadcasted_iota(jnp.int32, (128, new_len), 0)
    page_row = lax.broadcasted_iota(jnp.int32, (page_len, 2 * new_len), 0)
    new_row = lax.broadcasted_iota(jnp.int32, (local_new, 2 * new_len), 0) + place[0] * local_new
    new_col = lax.broadcasted_iota(jnp.int32, (local_new, 2 * new_len), 1) % new_len
    new_valid = new_row <= new_col
    logical = [place[0] + i * groups for i in range(pages)]
    places = [table[req, j] - place[0] * pages for j in logical]
    limits = [length[req] - j * page_len for j in logical]

    @pl.when((req == 0) & (group == 0))
    def _():
        top_sc[...] = jnp.zeros_like(top_sc)
        den_sc[...] = jnp.zeros_like(den_sc)

    for pair in range(pairs):
        at = slice(pair * 128, pair * 128 + 128)
        q = q_ref[0, :, at].astype(F32) * SCORE_SCALE
        both = jnp.concatenate([jnp.where(col < HD, q, 0.0), jnp.where(col < HD, 0.0, q)], axis=0).astype(BF16)
        parts = [
            jnp.where(page_row < limits[i], nt_dot(k_ref[0, places[i], 0, :, at], both), NEG_FILL) for i in range(pages)
        ]
        parts.append(jnp.where(new_valid, nt_dot(nk_ref[0, 0, :, at], both), NEG_FILL))
        top = functools.reduce(jnp.maximum, [jnp.max(s, axis=0, keepdims=True) for s in parts])
        top = top.astype(BF16).astype(F32)
        weights = [jnp.exp(s - top) for s in parts]
        den = functools.reduce(jnp.add, [jnp.sum(w, axis=0, keepdims=True) for w in weights])
        low = jnp.concatenate([w.astype(BF16) for w in weights[:-1]], axis=0)
        values = jnp.concatenate([v_ref[0, places[i], 0, :, at] for i in range(pages)], axis=0)
        num = tn_dot(values, low) + tn_dot(nv_ref[0, 0, :, at], weights[-1].astype(BF16))
        num = jnp.where(row < HD, num[:, :new_len], num[:, new_len:]).astype(BF16)
        for piece in range(4):
            index = (group * pairs + pair) * 4 + piece
            dest = index // (share // 32)
            offset = pl.multiple_of((index - dest * (share // 32)) * 32, 32)
            out_ref[dest, pl.ds(offset, 32), pl.ds(lane_at, new_len)] = num[piece * 32 : piece * 32 + 32]
        head = (group * pairs + pair) * 2
        for half in range(2):
            lanes = slice(half * new_len, half * new_len + new_len)
            top_sc[head + half, :, pl.ds(lane_at, new_len)] = top[:, lanes]
            den_sc[head + half, :, pl.ds(lane_at, new_len)] = den[:, lanes]

    @pl.when((req == pl.num_programs(0) - 1) & (group == pl.num_programs(1) - 1))
    def _():
        for dest in range(out_ref.shape[0]):
            first = dest * share // HD
            stats = jnp.concatenate([top_sc[first : first + 8, 0, :], den_sc[first : first + 8, 0, :]], axis=0)
            out_ref[dest, share : share + STAT_ROWS, :] = stats.astype(BF16)


def attend(table, length, place, queries, cache_pool, new_kv, dests):
    req_here, new_len, width = queries.shape
    pages, page_len = cache_pool.shape[1], cache_pool.shape[3]
    local_new = new_kv.shape[2]
    share = width // dests
    groups = 3
    block = width // groups
    heads = width // HD
    keys = pages * page_len + local_new
    return pl.pallas_call(
        functools.partial(attend_kernel, share=share),
        grid_spec=pltpu.PrefetchScalarGridSpec(
            num_scalar_prefetch=3,
            grid=(req_here, groups),
            in_specs=[
                pl.BlockSpec((1, new_len, block), lambda r, g, *_: (r, 0, g)),
                pl.BlockSpec((1, pages, 1, page_len, block), lambda r, g, *_: (r, 0, 0, 0, g)),
                pl.BlockSpec((1, pages, 1, page_len, block), lambda r, g, *_: (r, 0, 1, 0, g)),
                pl.BlockSpec((1, 1, local_new, block), lambda r, g, *_: (r, 0, 0, g)),
                pl.BlockSpec((1, 1, local_new, block), lambda r, g, *_: (r, 1, 0, g)),
            ],
            out_specs=pl.BlockSpec((dests, share + STAT_ROWS, req_here * new_len), lambda r, g, *_: (0, 0, 0)),
            scratch_shapes=[pltpu.VMEM((heads + 12, 1, req_here * new_len), F32)] * 2,
        ),
        out_shape=jax.ShapeDtypeStruct((dests, share + STAT_ROWS, req_here * new_len), BF16),
        cost_estimate=pl.CostEstimate(
            flops=4 * req_here * new_len * width * keys,
            bytes_accessed=cache_pool.size * 2 + queries.size * 2,
            transcendentals=req_here * heads * new_len * keys,
        ),
        compiler_params=pltpu.CompilerParams(vmem_limit_bytes=60 << 20),
        name="attend",
    )(table, length, place, queries, cache_pool, cache_pool, new_kv, new_kv)


def join_kernel(place, recv_ref, res_ref, gain_ref, slot_ref, placed_ref, hidden_ref, spread_sc, *, share):
    groups = recv_ref.shape[0]
    tokens = recv_ref.shape[2]
    slots = placed_ref.shape[0] * placed_ref.shape[1]
    padded = placed_ref.shape[2]
    tops = [recv_ref[g, share : share + 8, :].astype(F32) for g in range(groups)]
    top = functools.reduce(jnp.maximum, tops)
    scales = [jnp.exp(t - top) for t in tops]
    den = functools.reduce(jnp.add, [s * recv_ref[g, share + 8 : share + 16, :].astype(F32) for g, s in enumerate(scales)])
    offset = pl.multiple_of(place[0] % 2 * (HD // 2), HD // 2)
    total = res_ref[...]
    for g in range(groups):
        factor = scales[g] / den
        for head in range(5):
            spread_sc[g, head * HD : head * HD + HD, :] = jnp.broadcast_to(factor[head : head + 1, :], (HD, tokens))
        total = total + recv_ref[g, :share, :].astype(F32) * spread_sc[g, pl.ds(offset, share), :]
    hidden_ref[...] = total
    square = jnp.sum(total * total, axis=0, keepdims=True)
    high = square.astype(BF16).astype(F32)
    row = lax.broadcasted_iota(jnp.int32, (padded - share, tokens), 0)
    tail = jnp.where(row == 0, high, jnp.where(row == 1, square - high, 0.0)).astype(BF16)
    rows = jnp.concatenate([(total * gain_ref[...]).astype(BF16), tail], axis=0)
    at = lax.broadcasted_iota(jnp.int32, (slots, tokens), 0)
    picks = (at == slot_ref[0:1, :]) | (at == slot_ref[1:2, :])
    placed = nt_dot(jnp.where(picks, 1.0, 0.0).astype(BF16), rows)
    placed_ref[...] = placed.astype(BF16).reshape(placed_ref.shape)


def join(place, recv, residual, gain, slots, experts):
    groups, rows, tokens = recv.shape
    share = rows - STAT_ROWS
    padded = -(-(share + 2) // 128) * 128
    whole = lambda *shape: pl.BlockSpec(shape, lambda i, *_: (0,) * len(shape))
    return pl.pallas_call(
        functools.partial(join_kernel, share=share),
        grid_spec=pltpu.PrefetchScalarGridSpec(
            num_scalar_prefetch=1,
            grid=(1,),
            in_specs=[
                whole(groups, rows, tokens),
                whole(share, tokens),
                whole(share, 1),
                whole(2, tokens),
            ],
            out_specs=[whole(experts, CAP, padded), whole(share, tokens)],
            scratch_shapes=[pltpu.VMEM((groups, 5 * HD, tokens), F32)],
        ),
        out_shape=[
            jax.ShapeDtypeStruct((experts, CAP, padded), BF16),
            jax.ShapeDtypeStruct((share, tokens), F32),
        ],
        cost_estimate=pl.CostEstimate(
            flops=2 * experts * CAP * padded * tokens, bytes_accessed=recv.size * 2 + experts * CAP * padded * 2, transcendentals=0
        ),
        compiler_params=pltpu.CompilerParams(vmem_limit_bytes=10 << 20),
        name="join",
    )(place, recv, residual, gain, slots)


def norm_kernel(recv_ref, out_ref, *, share):
    groups, _, _ = recv_ref.shape
    blocks = [recv_ref[g].astype(F32) for g in range(groups)]
    square = functools.reduce(jnp.add, [b[:, share : share + 1] + b[:, share + 1 : share + 2] for b in blocks])
    scale = lax.rsqrt(square / (groups * share) + EPSILON)
    out_ref[...] = jnp.concatenate([b[:, :share] * scale for b in blocks], axis=1).astype(BF16)


def norm_rows(recv, share):
    groups, rows, _ = recv.shape
    return pl.pallas_call(
        functools.partial(norm_kernel, share=share),
        out_shape=jax.ShapeDtypeStruct((rows, groups * share), BF16),
        cost_estimate=pl.CostEstimate(flops=0, bytes_accessed=recv.size * 4, transcendentals=0),
        compiler_params=pltpu.CompilerParams(vmem_limit_bytes=4 << 20),
        name="norm_rows",
    )(recv)


def stack_kernel(*refs):
    blocks, outs = refs[:4], refs[4:]
    for i, ref in enumerate(blocks):
        outs[i // 2][i % 2] = ref[...]


def stack(blocks):
    rows, width = blocks[0].shape
    pairs = pl.pallas_call(
        stack_kernel,
        out_shape=[jax.ShapeDtypeStruct((2, rows, width), BF16)] * 2,
        cost_estimate=pl.CostEstimate(flops=0, bytes_accessed=16 * rows * width, transcendentals=0),
        compiler_params=pltpu.CompilerParams(vmem_limit_bytes=4 << 20),
        name="stack",
    )(*blocks)
    return [pair.reshape(2 * rows, width) for pair in pairs]


def expert_kernel(*refs, count):
    blocks, gate_up_hbm, down_hbm = refs[:count], refs[count], refs[count + 1]
    outs, (x_sc, gate_up_ref, down_ref, weight_sc, both_sc, y_sc, sems) = refs[count + 2 : 2 * count + 2], refs[2 * count + 2 :]
    rows = blocks[0].shape[0]
    groups, _, units = gate_up_ref.shape
    share = x_sc.shape[1] // groups
    half = weight_sc.shape[1] // 2
    tile = 256
    loads = [pltpu.make_async_copy(b, x_sc.at[pl.ds(i * rows, rows)], sems.at[i]) for i, b in enumerate(blocks)]
    stores = [pltpu.make_async_copy(y_sc.at[pl.ds(i * rows, rows)], o, sems.at[count + i]) for i, o in enumerate(outs)]
    parts = [pltpu.make_async_copy(gate_up_hbm.at[g], gate_up_ref.at[g], sems.at[2 * count + g]) for g in range(groups)]
    down_load = pltpu.make_async_copy(down_hbm, down_ref, sems.at[2 * count + groups])
    for load in (*parts, *loads, down_load):
        load.start()
    for g in range(groups):
        parts[g].wait()
        weight_sc[g * share : g * share + share, :units] = gate_up_ref[g, :share]
        weight_sc[g * share : g * share + share, half : half + units] = gate_up_ref[g, share:]
    for load in loads:
        load.wait()

    @pl.loop(0, 2 * half // tile)
    def _(j):
        lanes = pl.ds(pl.multiple_of(j * tile, tile), tile)
        both_sc[:, lanes] = jnp.dot(x_sc[...], weight_sc[:, lanes], preferred_element_type=F32)

    gate, up = both_sc[:, :units], both_sc[:, half : half + units]
    act = (gate / (1.0 + jnp.exp(-gate)) * up).astype(BF16)
    down_load.wait()

    @pl.loop(0, down_ref.shape[0] // tile)
    def _(j):
        lanes = pl.ds(pl.multiple_of(j * tile, tile), tile)
        y_sc[:, lanes] = nt_dot(act, down_ref[lanes, :]).astype(BF16)

    for copy in stores:
        copy.start()
    for copy in stores:
        copy.wait()


def expert(blocks, gate_up, down):
    rows, width = blocks[0].shape
    units = down.shape[1]
    count = len(blocks)
    total = count * rows
    packed = 2 * (-(-units // 128) * 128)
    anywhere = pl.BlockSpec(memory_space=pltpu.HBM)
    return pl.pallas_call(
        functools.partial(expert_kernel, count=count),
        in_specs=[anywhere] * (count + 2),
        out_specs=[anywhere] * count,
        out_shape=[jax.ShapeDtypeStruct((rows, width), BF16)] * count,
        scratch_shapes=[
            pltpu.VMEM((total, width), BF16),
            pltpu.VMEM(gate_up.shape, BF16),
            pltpu.VMEM(down.shape, BF16),
            pltpu.VMEM((width, packed), BF16),
            pltpu.VMEM((total, packed), F32),
            pltpu.VMEM((total, width), BF16),
            pltpu.SemaphoreType.DMA((2 * count + gate_up.shape[0] + 1,)),
        ],
        cost_estimate=pl.CostEstimate(
            flops=6 * total * width * units,
            bytes_accessed=4 * total * width + 6 * width * units,
            transcendentals=total * units,
        ),
        compiler_params=pltpu.CompilerParams(vmem_limit_bytes=60 << 20),
        name="expert",
    )(*blocks, gate_up, down)


def total_of(refs):
    return functools.reduce(jnp.add, [ref[...].astype(F32) for ref in refs])


def add_kernel(*refs):
    outs = refs[6:]
    rows = outs[0].shape[0]
    for i, out in enumerate(outs):
        at = slice(i % 2 * rows, i % 2 * rows + rows)
        some = refs[:3] if i < 2 else refs[3:6]
        out[...] = functools.reduce(jnp.add, [ref[at, :].astype(F32) for ref in some]).astype(BF16)


def add_blocks(low, high):
    rows, width = low[0].shape
    return pl.pallas_call(
        add_kernel,
        out_shape=[jax.ShapeDtypeStruct((rows // 2, width), BF16)] * 4,
        cost_estimate=pl.CostEstimate(flops=0, bytes_accessed=16 * rows * width, transcendentals=0),
        compiler_params=pltpu.CompilerParams(vmem_limit_bytes=8 << 20),
        name="add_blocks",
    )(*low, *high)


def finish_kernel(*refs):
    out_ref = refs[-1]
    groups, _, share = out_ref.shape
    both = jnp.concatenate([total_of(refs[:4]), total_of(refs[4:8])], axis=0).astype(BF16)
    for g in range(groups):
        out_ref[g] = both[:, g * share : (g + 1) * share]


def finish(blocks, groups):
    rows, width = blocks[0].shape
    return pl.pallas_call(
        finish_kernel,
        out_shape=jax.ShapeDtypeStruct((groups, 2 * rows, width // groups), BF16),
        cost_estimate=pl.CostEstimate(flops=0, bytes_accessed=20 * rows * width, transcendentals=0),
        compiler_params=pltpu.CompilerParams(vmem_limit_bytes=8 << 20),
        name="finish",
    )(*blocks)


def mix_kernel(rows_ref, slot_ref, weight_ref, hidden_ref, out_ref):
    tokens = out_ref.shape[1]
    slots = rows_ref.shape[0]
    at = lax.broadcasted_iota(jnp.int32, (slots, tokens), 0)
    table = jnp.where(at == slot_ref[0:1, :], weight_ref[0:1, :], 0.0)
    table = table + jnp.where(at == slot_ref[1:2, :], weight_ref[1:2, :], 0.0)
    high = table.astype(BF16)
    low = (table - high.astype(F32)).astype(BF16)
    rows = rows_ref[...]
    out_ref[...] = (hidden_ref[...] + (tn_dot(rows, high) + tn_dot(rows, low))).astype(BF16)


def mix(rows, slots, weights, hidden):
    return pl.pallas_call(
        mix_kernel,
        out_shape=jax.ShapeDtypeStruct(hidden.shape, BF16),
        cost_estimate=pl.CostEstimate(flops=4 * hidden.size * rows.shape[0], bytes_accessed=rows.size * 2 + hidden.size * 6, transcendentals=0),
        compiler_params=pltpu.CompilerParams(vmem_limit_bytes=6 << 20),
        name="mix",
    )(rows, slots, weights, hidden)


def ring_pairs(axis, step):
    pairs = []
    for index in range(RING * RING):
        y, z = divmod(index, RING)
        if axis == "y":
            y = (y + step) % RING
        else:
            z = (z + step) % RING
        pairs.append((index, y * RING + z))
    return pairs


def shift(x, axis, step):
    return lax.ppermute(x, "wide", ring_pairs(axis, step))


def local(
    queries,
    new_kv,
    cache_pool,
    page_table,
    cached_len,
    residual,
    norm_gain,
    expert_ids,
    route_weight,
    w_gate_up,
    w_down,
):
    narrow_count = lax.axis_size("narrow")
    narrow_pos = lax.axis_index("narrow").astype(jnp.int32)
    _, _, width = queries.shape
    token_rows = expert_ids.shape[0]
    expert_count = w_gate_up.shape[0]
    units = w_down.shape[1]
    share = width // narrow_count

    def exchange(x):
        return lax.all_to_all(x, "narrow", 0, 0, tiled=True)

    down_all = exchange(jnp.transpose(w_down, (0, 2, 1)))
    place = narrow_pos.reshape(1)
    sums = attend(page_table, cached_len, place, queries, cache_pool, new_kv, narrow_count)
    sums, down_all, w_gate_up = lax.optimization_barrier((sums, down_all, w_gate_up))
    later = jnp.concatenate([w_gate_up[:, :, 0], w_gate_up[:, :, 1]], axis=1)
    sums = exchange(sums)

    flat_ids = expert_ids.reshape(token_rows * 2)
    onehot = (flat_ids[:, None] == jnp.arange(expert_count, dtype=jnp.int32)[None, :]).astype(BF16)
    order = jnp.arange(token_rows * 2, dtype=jnp.int32)
    earlier = jnp.dot((order[:, None] > order[None, :]).astype(BF16), onehot, preferred_element_type=F32)
    position = jnp.sum(earlier * onehot.astype(F32), axis=1).astype(jnp.int32)
    slots = (flat_ids * CAP + position).reshape(token_rows, 2)

    res_share = lax.dynamic_slice_in_dim(residual, narrow_pos * share, share, 1).astype(F32).T
    gain_share = lax.dynamic_slice_in_dim(norm_gain, narrow_pos * share, share, 0)[:, None]
    placed, hidden = join(place, sums, res_share, gain_share, slots.T, expert_count)
    placed = exchange(placed)
    later, placed = lax.optimization_barrier((later, placed))
    later = exchange(later)
    down_all = down_all.reshape(width, units)
    rows = norm_rows(placed, share)

    half = CAP // 2

    def around(block, axis):
        return [block, *(shift(block, axis, step) for step in STEPS)]

    early, late = [], []
    for first, second, block in (("z", "y", rows[:half]), ("y", "z", rows[half:])):
        low, high = stack(around(block, first))
        before_low, after_high = shift(low, second, 1), shift(high, second, -1)
        before_high, after_low = shift(high, second, 1), shift(low, second, -1)
        far_low, far_high = shift(before_low, second, 1), shift(after_high, second, -1)
        early += [before_low, after_high, far_low, far_high]
        late += [low, high, after_low, before_high]
    early = list(expert(early, later, down_all))
    early[0], *late = lax.optimization_barrier((early[0], *late))
    late = expert(late, later, down_all)

    def back(blocks, axis):
        return [blocks[0], *(shift(block, axis, -step) for block, step in zip(blocks[1:], STEPS))]

    def joined(a, b):
        return (a.astype(F32) + b.astype(F32)).astype(BF16)

    four = []
    for color, second in enumerate(("y", "z")):
        before_low, after_high, far_low, far_high = early[4 * color : 4 * color + 4]
        low, high, after_low, before_high = late[4 * color : 4 * color + 4]
        got = []
        for block, step in zip((far_low, far_high, before_low, after_high), (1, -1, -1, 1)):
            got.append(shift(block, second, step))
        more_low, more_high = shift(joined(after_low, got[0]), second, 1), shift(joined(before_high, got[1]), second, -1)
        four.append(add_blocks([low, got[2], more_low], [high, got[3], more_high]))
    out_rows = finish([*back(four[0], "z"), *back(four[1], "y")], narrow_count)
    out_rows = exchange(out_rows)
    return mix(out_rows.reshape(expert_count * CAP, share), slots.T, route_weight.T, hidden).T


def solution(mesh):
    return jax.shard_map(
        local,
        mesh=mesh,
        in_specs=(
            P("wide", None, None),
            P("wide", None, "narrow", None),
            P("wide", "narrow", None, None, None),
            P("wide", None),
            P("wide"),
            P("wide", None),
            P(),
            P("wide", None),
            P("wide", None),
            P(None, "narrow", None, "wide"),
            P(None, "wide", "narrow"),
        ),
        out_specs=P("wide", "narrow"),
        check_vma=False,
    )
```

```python
import functools

import jax
import jax.numpy as jnp
from jax import lax
from jax.experimental import pallas as pl
from jax.experimental.pallas import tpu as pltpu
from jax.sharding import PartitionSpec as P


HD = 64
CAP = 80
NEG_FILL = -(2.0**100)
SCORE_SCALE = 0.125
EPSILON = 1e-05
STAT_ROWS = 16
RING = 4
STEPS = (2, 1, -1)


F32 = jnp.float32
BF16 = jnp.bfloat16


def nt_dot(a, b):
    return lax.dot_general(a, b, (((1,), (1,)), ((), ())), preferred_element_type=F32)


def tn_dot(a, b):
    return lax.dot_general(a, b, (((0,), (0,)), ((), ())), preferred_element_type=F32)


def attend_kernel(table, length, place, q_ref, k_ref, v_ref, nk_ref, nv_ref, keep_ref, send_ref, sum_sc, top_sc, den_sc, *, share):
    groups = 2 * keep_ref.shape[0]
    req, group = pl.program_id(0), pl.program_id(1)
    new_len = q_ref.shape[1]
    pages, page_len = k_ref.shape[1], k_ref.shape[3]
    local_new = nk_ref.shape[2]
    pairs = q_ref.shape[2] // 128
    lane_at = pl.multiple_of(req * new_len, new_len)
    col = lax.broadcasted_iota(jnp.int32, (new_len, 128), 1)
    row = lax.broadcasted_iota(jnp.int32, (128, new_len), 0)
    page_row = lax.broadcasted_iota(jnp.int32, (page_len, 2 * new_len), 0)
    new_row = lax.broadcasted_iota(jnp.int32, (local_new, 2 * new_len), 0) + place[0] * local_new
    new_col = lax.broadcasted_iota(jnp.int32, (local_new, 2 * new_len), 1) % new_len
    new_valid = new_row <= new_col
    logical = [place[0] + i * groups for i in range(pages)]
    places = [table[req, j] - place[0] * pages for j in logical]
    limits = [length[req] - j * page_len for j in logical]

    @pl.when((req == 0) & (group == 0))
    def _():
        top_sc[...] = jnp.zeros_like(top_sc)
        den_sc[...] = jnp.zeros_like(den_sc)

    for pair in range(pairs):
        at = slice(pair * 128, pair * 128 + 128)
        q = q_ref[0, :, at].astype(F32) * SCORE_SCALE
        both = jnp.concatenate([jnp.where(col < HD, q, 0.0), jnp.where(col < HD, 0.0, q)], axis=0).astype(BF16)
        parts = [
            jnp.where(page_row < limits[i], nt_dot(k_ref[0, places[i], 0, :, at], both), NEG_FILL) for i in range(pages)
        ]
        parts.append(jnp.where(new_valid, nt_dot(nk_ref[0, 0, :, at], both), NEG_FILL))
        top = functools.reduce(jnp.maximum, [jnp.max(s, axis=0, keepdims=True) for s in parts])
        top = top.astype(BF16).astype(F32)
        weights = [jnp.exp(s - top) for s in parts]
        den = functools.reduce(jnp.add, [jnp.sum(w, axis=0, keepdims=True) for w in weights])
        low = jnp.concatenate([w.astype(BF16) for w in weights[:-1]], axis=0)
        values = jnp.concatenate([v_ref[0, places[i], 0, :, at] for i in range(pages)], axis=0)
        num = tn_dot(values, low) + tn_dot(nv_ref[0, 0, :, at], weights[-1].astype(BF16))
        num = jnp.where(row < HD, num[:, :new_len], num[:, new_len:]).astype(BF16)
        for piece in range(4):
            index = (group * pairs + pair) * 4 + piece
            dest = index // (share // 32)
            offset = pl.multiple_of((index - dest * (share // 32)) * 32, 32)
            side = (dest + place[0]) % 2
            sum_sc[side, dest // 2, pl.ds(offset, 32), pl.ds(lane_at, new_len)] = num[piece * 32 : piece * 32 + 32]
        head = (group * pairs + pair) * 2
        for half in range(2):
            lanes = slice(half * new_len, half * new_len + new_len)
            top_sc[head + half, :, pl.ds(lane_at, new_len)] = top[:, lanes]
            den_sc[head + half, :, pl.ds(lane_at, new_len)] = den[:, lanes]

    @pl.when((req == pl.num_programs(0) - 1) & (group == pl.num_programs(1) - 1))
    def _():
        for dest in range(groups):
            first = dest * share // HD
            stats = jnp.concatenate([top_sc[first : first + 8, 0, :], den_sc[first : first + 8, 0, :]], axis=0)
            sum_sc[(dest + place[0]) % 2, dest // 2, share : share + STAT_ROWS, :] = stats.astype(BF16)
        keep_ref[...] = sum_sc[0]
        send_ref[...] = sum_sc[1]


def attend(table, length, place, queries, cache_pool, new_kv, dests):
    req_here, new_len, width = queries.shape
    pages, page_len = cache_pool.shape[1], cache_pool.shape[3]
    local_new = new_kv.shape[2]
    share = width // dests
    groups = 3
    block = width // groups
    heads = width // HD
    keys = pages * page_len + local_new
    return pl.pallas_call(
        functools.partial(attend_kernel, share=share),
        grid_spec=pltpu.PrefetchScalarGridSpec(
            num_scalar_prefetch=3,
            grid=(req_here, groups),
            in_specs=[
                pl.BlockSpec((1, new_len, block), lambda r, g, *_: (r, 0, g)),
                pl.BlockSpec((1, pages, 1, page_len, block), lambda r, g, *_: (r, 0, 0, 0, g)),
                pl.BlockSpec((1, pages, 1, page_len, block), lambda r, g, *_: (r, 0, 1, 0, g)),
                pl.BlockSpec((1, 1, local_new, block), lambda r, g, *_: (r, 0, 0, g)),
                pl.BlockSpec((1, 1, local_new, block), lambda r, g, *_: (r, 1, 0, g)),
            ],
            out_specs=[pl.BlockSpec((dests // 2, share + STAT_ROWS, req_here * new_len), lambda r, g, *_: (0, 0, 0))] * 2,
            scratch_shapes=[pltpu.VMEM((2, dests // 2, share + STAT_ROWS, req_here * new_len), BF16)]
            + [pltpu.VMEM((heads + 12, 1, req_here * new_len), F32)] * 2,
        ),
        out_shape=[jax.ShapeDtypeStruct((dests // 2, share + STAT_ROWS, req_here * new_len), BF16)] * 2,
        cost_estimate=pl.CostEstimate(
            flops=4 * req_here * new_len * width * keys,
            bytes_accessed=cache_pool.size * 2 + queries.size * 2,
            transcendentals=req_here * heads * new_len * keys,
        ),
        compiler_params=pltpu.CompilerParams(vmem_limit_bytes=60 << 20),
        name="attend",
    )(table, length, place, queries, cache_pool, cache_pool, new_kv, new_kv)


def merge_kernel(place, own_ref, other_ref, out_ref, spread_sc, *, share):
    tokens = own_ref.shape[2]
    offset = pl.multiple_of(place[0] % 2 * (HD // 2), HD // 2)
    both = (own_ref, other_ref)
    for dest in range(own_ref.shape[0]):
        tops = [ref[dest, share : share + 8, :].astype(F32) for ref in both]
        top = jnp.maximum(*tops)
        scales = [jnp.exp(t - top) for t in tops]
        den = functools.reduce(jnp.add, [s * ref[dest, share + 8 : share + 16, :].astype(F32) for s, ref in zip(scales, both)])
        total = None
        for side, ref in enumerate(both):
            for head in range(5):
                spread_sc[side, head * HD : head * HD + HD, :] = jnp.broadcast_to(scales[side][head : head + 1, :], (HD, tokens))
            term = ref[dest, :share, :].astype(F32) * spread_sc[side, pl.ds(offset, share), :]
            total = term if total is None else total + term
        out_ref[dest, :share, :] = total.astype(BF16)
        out_ref[dest, share:, :] = jnp.concatenate([top, den], axis=0).astype(BF16)


def merge(place, own, other):
    dests, rows, tokens = own.shape
    whole = pl.BlockSpec((dests, rows, tokens), lambda i, *_: (0, 0, 0))
    return pl.pallas_call(
        functools.partial(merge_kernel, share=rows - STAT_ROWS),
        grid_spec=pltpu.PrefetchScalarGridSpec(
            num_scalar_prefetch=1,
            grid=(1,),
            in_specs=[whole, whole],
            out_specs=whole,
            scratch_shapes=[pltpu.VMEM((2, 5 * HD, tokens), F32)],
        ),
        out_shape=jax.ShapeDtypeStruct(own.shape, BF16),
        cost_estimate=pl.CostEstimate(flops=4 * own.size, bytes_accessed=6 * own.size, transcendentals=0),
        compiler_params=pltpu.CompilerParams(vmem_limit_bytes=10 << 20),
        name="merge",
    )(place, own, other)


def join_kernel(place, recv_ref, res_ref, gain_ref, slot_ref, placed_ref, hidden_ref, spread_sc, *, share):
    groups = recv_ref.shape[0]
    tokens = recv_ref.shape[2]
    slots = placed_ref.shape[0] * placed_ref.shape[1]
    padded = placed_ref.shape[2]
    tops = [recv_ref[g, share : share + 8, :].astype(F32) for g in range(groups)]
    top = functools.reduce(jnp.maximum, tops)
    scales = [jnp.exp(t - top) for t in tops]
    den = functools.reduce(jnp.add, [s * recv_ref[g, share + 8 : share + 16, :].astype(F32) for g, s in enumerate(scales)])
    offset = pl.multiple_of(place[0] % 2 * (HD // 2), HD // 2)
    total = res_ref[...]
    for g in range(groups):
        factor = scales[g] / den
        for head in range(5):
            spread_sc[g, head * HD : head * HD + HD, :] = jnp.broadcast_to(factor[head : head + 1, :], (HD, tokens))
        total = total + recv_ref[g, :share, :].astype(F32) * spread_sc[g, pl.ds(offset, share), :]
    hidden_ref[...] = total
    square = jnp.sum(total * total, axis=0, keepdims=True)
    high = square.astype(BF16).astype(F32)
    row = lax.broadcasted_iota(jnp.int32, (padded - share, tokens), 0)
    tail = jnp.where(row == 0, high, jnp.where(row == 1, square - high, 0.0)).astype(BF16)
    rows = jnp.concatenate([(total * gain_ref[...]).astype(BF16), tail], axis=0)
    at = lax.broadcasted_iota(jnp.int32, (slots, tokens), 0)
    picks = (at == slot_ref[0:1, :]) | (at == slot_ref[1:2, :])
    placed = nt_dot(jnp.where(picks, 1.0, 0.0).astype(BF16), rows)
    placed_ref[...] = placed.astype(BF16).reshape(placed_ref.shape)


def join(place, recv, residual, gain, slots, experts):
    groups, rows, tokens = recv.shape
    share = rows - STAT_ROWS
    padded = -(-(share + 2) // 128) * 128
    whole = lambda *shape: pl.BlockSpec(shape, lambda i, *_: (0,) * len(shape))
    return pl.pallas_call(
        functools.partial(join_kernel, share=share),
        grid_spec=pltpu.PrefetchScalarGridSpec(
            num_scalar_prefetch=1,
            grid=(1,),
            in_specs=[
                whole(groups, rows, tokens),
                whole(share, tokens),
                whole(share, 1),
                whole(2, tokens),
            ],
            out_specs=[whole(experts, CAP, padded), whole(share, tokens)],
            scratch_shapes=[pltpu.VMEM((groups, 5 * HD, tokens), F32)],
        ),
        out_shape=[
            jax.ShapeDtypeStruct((experts, CAP, padded), BF16),
            jax.ShapeDtypeStruct((share, tokens), F32),
        ],
        cost_estimate=pl.CostEstimate(
            flops=2 * experts * CAP * padded * tokens, bytes_accessed=recv.size * 2 + experts * CAP * padded * 2, transcendentals=0
        ),
        compiler_params=pltpu.CompilerParams(vmem_limit_bytes=10 << 20),
        name="join",
    )(place, recv, residual, gain, slots)


def norm_kernel(recv_ref, out_ref, *, share):
    groups, _, _ = recv_ref.shape
    blocks = [recv_ref[g].astype(F32) for g in range(groups)]
    square = functools.reduce(jnp.add, [b[:, share : share + 1] + b[:, share + 1 : share + 2] for b in blocks])
    scale = lax.rsqrt(square / (groups * share) + EPSILON)
    out_ref[...] = jnp.concatenate([b[:, :share] * scale for b in blocks], axis=1).astype(BF16)


def norm_rows(recv, share):
    groups, rows, _ = recv.shape
    return pl.pallas_call(
        functools.partial(norm_kernel, share=share),
        out_shape=jax.ShapeDtypeStruct((rows, groups * share), BF16),
        cost_estimate=pl.CostEstimate(flops=0, bytes_accessed=recv.size * 4, transcendentals=0),
        compiler_params=pltpu.CompilerParams(vmem_limit_bytes=4 << 20),
        name="norm_rows",
    )(recv)


def stack_kernel(*refs):
    blocks, outs = refs[:4], refs[4:]
    for i, ref in enumerate(blocks):
        outs[i // 2][i % 2] = ref[...]


def stack(blocks):
    rows, width = blocks[0].shape
    pairs = pl.pallas_call(
        stack_kernel,
        out_shape=[jax.ShapeDtypeStruct((2, rows, width), BF16)] * 2,
        cost_estimate=pl.CostEstimate(flops=0, bytes_accessed=16 * rows * width, transcendentals=0),
        compiler_params=pltpu.CompilerParams(vmem_limit_bytes=4 << 20),
        name="stack",
    )(*blocks)
    return [pair.reshape(2 * rows, width) for pair in pairs]


def expert_kernel(*refs, count):
    blocks, gate_up_hbm, down_hbm = refs[:count], refs[count], refs[count + 1]
    outs, (x_sc, gate_up_sc, down_sc, both_sc, y_sc, sems) = refs[count + 2 : -6], refs[-6:]
    rows, out_rows, units = blocks[0].shape[0], outs[0].shape[0], down_sc.shape[1]
    half = gate_up_sc.shape[1] // 2
    tile = 256
    loads = [pltpu.make_async_copy(b, x_sc.at[pl.ds(i * rows, rows)], sems.at[i]) for i, b in enumerate(blocks)]
    loads.append(pltpu.make_async_copy(gate_up_hbm, gate_up_sc, sems.at[count]))
    down_load = pltpu.make_async_copy(down_hbm, down_sc, sems.at[count + 1])
    for load in (*loads, down_load):
        load.start()
    for load in loads:
        load.wait()

    @pl.loop(0, 2 * half // tile)
    def _(j):
        lanes = pl.ds(pl.multiple_of(j * tile, tile), tile)
        both_sc[:, lanes] = jnp.dot(x_sc[...], gate_up_sc[:, lanes], preferred_element_type=F32)

    gate, up = both_sc[:, :units], both_sc[:, half : half + units]
    act = (gate / (1.0 + jnp.exp(-gate)) * up).astype(BF16)
    down_load.wait()

    @pl.loop(0, down_sc.shape[0] // tile)
    def _(j):
        lanes = pl.ds(pl.multiple_of(j * tile, tile), tile)
        y_sc[:, lanes] = nt_dot(act, down_sc[lanes, :]).astype(BF16)
        for i, out in enumerate(outs):
            at = pl.ds(i * out_rows, out_rows)
            pltpu.make_async_copy(y_sc.at[at, lanes], out.at[:, lanes], sems.at[count + 2 + i]).start()

    for i, out in enumerate(outs):
        pltpu.make_async_copy(y_sc.at[pl.ds(i * out_rows, out_rows)], out, sems.at[count + 2 + i]).wait()


def expert(blocks, gate_up, down, out_rows):
    rows, width = blocks[0].shape
    units = down.shape[1]
    count = len(blocks)
    total = count * rows
    anywhere = pl.BlockSpec(memory_space=pltpu.HBM)
    return pl.pallas_call(
        functools.partial(expert_kernel, count=count),
        in_specs=[anywhere] * (count + 2),
        out_specs=[anywhere] * (total // out_rows),
        out_shape=[jax.ShapeDtypeStruct((out_rows, width), BF16)] * (total // out_rows),
        scratch_shapes=[
            pltpu.VMEM((total, width), BF16),
            pltpu.VMEM(gate_up.shape, BF16),
            pltpu.VMEM(down.shape, BF16),
            pltpu.VMEM((total, gate_up.shape[1]), F32),
            pltpu.VMEM((total, width), BF16),
            pltpu.SemaphoreType.DMA((count + 2 + total // out_rows,)),
        ],
        cost_estimate=pl.CostEstimate(
            flops=6 * total * width * units,
            bytes_accessed=4 * total * width + 6 * width * units,
            transcendentals=total * units,
        ),
        compiler_params=pltpu.CompilerParams(vmem_limit_bytes=60 << 20),
        name="expert",
    )(*blocks, gate_up, down)


def total_of(refs):
    return functools.reduce(jnp.add, [ref[...].astype(F32) for ref in refs])


def add_kernel(*refs):
    outs = refs[6:]
    rows = outs[0].shape[0]
    for i, out in enumerate(outs):
        at = slice(i % 2 * rows, i % 2 * rows + rows)
        lower = slice((i % 2 + 2) * rows, (i % 2 + 3) * rows)
        first, second, third = refs[:3] if i < 2 else refs[3:6]
        total = first[at, :].astype(F32) + second[at, :].astype(F32) + third[lower, :].astype(F32)
        out[...] = total.astype(BF16)


def add_blocks(low, high):
    rows, width = low[0].shape
    return pl.pallas_call(
        add_kernel,
        out_shape=[jax.ShapeDtypeStruct((rows // 2, width), BF16)] * 4,
        cost_estimate=pl.CostEstimate(flops=0, bytes_accessed=16 * rows * width, transcendentals=0),
        compiler_params=pltpu.CompilerParams(vmem_limit_bytes=8 << 20),
        name="add_blocks",
    )(*low, *high)


def finish_kernel(*refs):
    out_ref = refs[-1]
    groups, _, share = out_ref.shape
    both = jnp.concatenate([total_of(refs[:4]), total_of(refs[4:8])], axis=0).astype(BF16)
    for g in range(groups):
        out_ref[g] = both[:, g * share : (g + 1) * share]


def finish(blocks, groups):
    rows, width = blocks[0].shape
    return pl.pallas_call(
        finish_kernel,
        out_shape=jax.ShapeDtypeStruct((groups, 2 * rows, width // groups), BF16),
        cost_estimate=pl.CostEstimate(flops=0, bytes_accessed=20 * rows * width, transcendentals=0),
        compiler_params=pltpu.CompilerParams(vmem_limit_bytes=8 << 20),
        name="finish",
    )(*blocks)


def mix_kernel(rows_ref, slot_ref, weight_ref, hidden_ref, out_ref):
    tokens = out_ref.shape[1]
    slots = rows_ref.shape[0]
    at = lax.broadcasted_iota(jnp.int32, (slots, tokens), 0)
    table = jnp.where(at == slot_ref[0:1, :], weight_ref[0:1, :], 0.0)
    table = table + jnp.where(at == slot_ref[1:2, :], weight_ref[1:2, :], 0.0)
    high = table.astype(BF16)
    low = (table - high.astype(F32)).astype(BF16)
    rows = rows_ref[...]
    out_ref[...] = (hidden_ref[...] + (tn_dot(rows, high) + tn_dot(rows, low))).astype(BF16)


def mix(rows, slots, weights, hidden):
    return pl.pallas_call(
        mix_kernel,
        out_shape=jax.ShapeDtypeStruct(hidden.shape, BF16),
        cost_estimate=pl.CostEstimate(flops=4 * hidden.size * rows.shape[0], bytes_accessed=rows.size * 2 + hidden.size * 6, transcendentals=0),
        compiler_params=pltpu.CompilerParams(vmem_limit_bytes=6 << 20),
        name="mix",
    )(rows, slots, weights, hidden)


def ring_pairs(axis, step):
    pairs = []
    for index in range(RING * RING):
        y, z = divmod(index, RING)
        if axis == "y":
            y = (y + step) % RING
        else:
            z = (z + step) % RING
        pairs.append((index, y * RING + z))
    return pairs


def shift(x, axis, step):
    return lax.ppermute(x, "wide", ring_pairs(axis, step))


def local(
    queries,
    new_kv,
    cache_pool,
    page_table,
    cached_len,
    residual,
    norm_gain,
    expert_ids,
    route_weight,
    w_gate_up,
    w_down,
):
    narrow_count = lax.axis_size("narrow")
    narrow_pos = lax.axis_index("narrow").astype(jnp.int32)
    _, _, width = queries.shape
    token_rows = expert_ids.shape[0]
    expert_count = w_gate_up.shape[0]
    units = w_down.shape[1]
    share = width // narrow_count

    def exchange(x):
        return lax.all_to_all(x, "narrow", 0, 0, tiled=True)

    down_all = exchange(jnp.transpose(w_down, (0, 2, 1)))
    place = narrow_pos.reshape(1)
    own, other = attend(page_table, cached_len, place, queries, cache_pool, new_kv, narrow_count)
    own, w_gate_up = lax.optimization_barrier((own, w_gate_up))
    padding = ((0, 0), (0, 0), (0, -units % 128))
    later = jnp.concatenate([jnp.pad(w_gate_up[:, :, 0], padding), jnp.pad(w_gate_up[:, :, 1], padding)], axis=2)
    other = lax.ppermute(other, "narrow", [(i, i ^ 1) for i in range(narrow_count)])
    sums = merge(place, own, other)
    sums, down_all = lax.optimization_barrier((sums, down_all))
    chips = [[2 * x + core for x in range(narrow_count // 2)] for core in range(2)]
    sums = lax.all_to_all(sums, "narrow", 0, 0, axis_index_groups=chips, tiled=True)

    flat_ids = expert_ids.reshape(token_rows * 2)
    onehot = (flat_ids[:, None] == jnp.arange(expert_count, dtype=jnp.int32)[None, :]).astype(BF16)
    order = jnp.arange(token_rows * 2, dtype=jnp.int32)
    earlier = jnp.dot((order[:, None] > order[None, :]).astype(BF16), onehot, preferred_element_type=F32)
    position = jnp.sum(earlier * onehot.astype(F32), axis=1).astype(jnp.int32)
    slots = (flat_ids * CAP + position).reshape(token_rows, 2)

    res_share = lax.dynamic_slice_in_dim(residual, narrow_pos * share, share, 1).astype(F32).T
    gain_share = lax.dynamic_slice_in_dim(norm_gain, narrow_pos * share, share, 0)[:, None]
    placed, hidden = join(place, sums, res_share, gain_share, slots.T, expert_count)
    placed = exchange(placed)
    later, placed = lax.optimization_barrier((later, placed))
    later = exchange(later)
    later, down_all = later.reshape(width, -1), down_all.reshape(width, units)
    rows = norm_rows(placed, share)

    half = CAP // 2

    def around(block, axis):
        return [block, *(shift(block, axis, step) for step in STEPS)]

    early, late = [], []
    for first, second, block in (("z", "y", rows[:half]), ("y", "z", rows[half:])):
        low, high = stack(around(block, first))
        before_low, after_high = shift(low, second, 1), shift(high, second, -1)
        before_high, after_low = shift(high, second, 1), shift(low, second, -1)
        far_low, far_high = shift(before_low, second, 1), shift(after_high, second, -1)
        early += [far_low, after_high, far_high, before_low]
        late += [low, high, after_low, before_high]
    early = list(expert(early, later, down_all, 2 * CAP))
    early[0], *late = lax.optimization_barrier((early[0], *late))
    late = expert(late, later, down_all, CAP)

    def back(blocks, axis):
        return [blocks[0], *(shift(block, axis, -step) for block, step in zip(blocks[1:], STEPS))]

    def joined(a, b):
        return (a.astype(F32) + b.astype(F32)).astype(BF16)

    four = []
    for color, second in enumerate(("y", "z")):
        low, high, after_low, before_high = late[4 * color : 4 * color + 4]
        got = []
        for block, step in zip(early[2 * color : 2 * color + 2], (1, -1)):
            got.append(shift(block, second, step))
        more_low, more_high = (
            shift(joined(after_low, got[0][:CAP]), second, 1),
            shift(joined(before_high, got[1][:CAP]), second, -1),
        )
        four.append(add_blocks([low, more_low, got[1]], [high, more_high, got[0]]))
    out_rows = finish([*back(four[0], "z"), *back(four[1], "y")], narrow_count)
    out_rows = exchange(out_rows)
    return mix(out_rows.reshape(expert_count * CAP, share), slots.T, route_weight.T, hidden).T


def solution(mesh):
    return jax.shard_map(
        local,
        mesh=mesh,
        in_specs=(
            P("wide", None, None),
            P("wide", None, "narrow", None),
            P("wide", "narrow", None, None, None),
            P("wide", None),
            P("wide"),
            P("wide", None),
            P(),
            P("wide", None),
            P("wide", None),
            P(None, "narrow", None, "wide"),
            P(None, "wide", "narrow"),
        ),
        out_specs=P("wide", "narrow"),
        check_vma=False,
    )
```

```python
import functools

import jax
import jax.numpy as jnp
from jax import lax
from jax.experimental import pallas as pl
from jax.experimental.pallas import tpu as pltpu
from jax.sharding import PartitionSpec as P


HD = 64
CAP = 80
NEG_FILL = -(2.0**100)
SCORE_SCALE = 0.125
EPSILON = 1e-05
STAT_ROWS = 16
RING = 4
STEPS = (2, 1, -1)


F32 = jnp.float32
BF16 = jnp.bfloat16


def nt_dot(a, b):
    return lax.dot_general(a, b, (((1,), (1,)), ((), ())), preferred_element_type=F32)


def tn_dot(a, b):
    return lax.dot_general(a, b, (((0,), (0,)), ((), ())), preferred_element_type=F32)


def attend_kernel(table, length, place, q_ref, k_ref, v_ref, nk_ref, nv_ref, keep_ref, send_ref, sum_sc, top_sc, den_sc, *, share):
    groups = 2 * keep_ref.shape[0]
    req, group = pl.program_id(0), pl.program_id(1)
    new_len = q_ref.shape[1]
    pages, page_len = k_ref.shape[1], k_ref.shape[3]
    local_new = nk_ref.shape[2]
    pairs = q_ref.shape[2] // 128
    lane_at = pl.multiple_of(req * new_len, new_len)
    col = lax.broadcasted_iota(jnp.int32, (new_len, 128), 1)
    row = lax.broadcasted_iota(jnp.int32, (128, new_len), 0)
    page_row = lax.broadcasted_iota(jnp.int32, (page_len, 2 * new_len), 0)
    new_row = lax.broadcasted_iota(jnp.int32, (local_new, 2 * new_len), 0) + place[0] * local_new
    new_col = lax.broadcasted_iota(jnp.int32, (local_new, 2 * new_len), 1) % new_len
    new_valid = new_row <= new_col
    logical = [place[0] + i * groups for i in range(pages)]
    places = [table[req, j] - place[0] * pages for j in logical]
    limits = [length[req] - j * page_len for j in logical]

    @pl.when((req == 0) & (group == 0))
    def _():
        top_sc[...] = jnp.zeros_like(top_sc)
        den_sc[...] = jnp.zeros_like(den_sc)

    for pair in range(pairs):
        at = slice(pair * 128, pair * 128 + 128)
        q = q_ref[0, :, at].astype(F32) * SCORE_SCALE
        both = jnp.concatenate([jnp.where(col < HD, q, 0.0), jnp.where(col < HD, 0.0, q)], axis=0).astype(BF16)
        parts = [
            jnp.where(page_row < limits[i], nt_dot(k_ref[0, places[i], 0, :, at], both), NEG_FILL) for i in range(pages)
        ]
        parts.append(jnp.where(new_valid, nt_dot(nk_ref[0, 0, :, at], both), NEG_FILL))
        top = functools.reduce(jnp.maximum, [jnp.max(s, axis=0, keepdims=True) for s in parts])
        top = top.astype(BF16).astype(F32)
        weights = [jnp.exp(s - top) for s in parts]
        den = functools.reduce(jnp.add, [jnp.sum(w, axis=0, keepdims=True) for w in weights])
        low = jnp.concatenate([w.astype(BF16) for w in weights[:-1]], axis=0)
        values = jnp.concatenate([v_ref[0, places[i], 0, :, at] for i in range(pages)], axis=0)
        num = tn_dot(values, low) + tn_dot(nv_ref[0, 0, :, at], weights[-1].astype(BF16))
        num = jnp.where(row < HD, num[:, :new_len], num[:, new_len:]).astype(BF16)
        for piece in range(4):
            index = (group * pairs + pair) * 4 + piece
            dest = index // (share // 32)
            offset = pl.multiple_of((index - dest * (share // 32)) * 32, 32)
            side = (dest + place[0]) % 2
            sum_sc[side, dest // 2, pl.ds(offset, 32), pl.ds(lane_at, new_len)] = num[piece * 32 : piece * 32 + 32]
        head = (group * pairs + pair) * 2
        for half in range(2):
            lanes = slice(half * new_len, half * new_len + new_len)
            top_sc[head + half, :, pl.ds(lane_at, new_len)] = top[:, lanes]
            den_sc[head + half, :, pl.ds(lane_at, new_len)] = den[:, lanes]

    @pl.when((req == pl.num_programs(0) - 1) & (group == pl.num_programs(1) - 1))
    def _():
        for dest in range(groups):
            first = dest * share // HD
            stats = jnp.concatenate([top_sc[first : first + 8, 0, :], den_sc[first : first + 8, 0, :]], axis=0)
            sum_sc[(dest + place[0]) % 2, dest // 2, share : share + STAT_ROWS, :] = stats.astype(BF16)
        keep_ref[...] = sum_sc[0]
        send_ref[...] = sum_sc[1]


def attend(table, length, place, queries, cache_pool, new_kv, dests):
    req_here, new_len, width = queries.shape
    pages, page_len = cache_pool.shape[1], cache_pool.shape[3]
    local_new = new_kv.shape[2]
    share = width // dests
    groups = 3
    block = width // groups
    heads = width // HD
    keys = pages * page_len + local_new
    return pl.pallas_call(
        functools.partial(attend_kernel, share=share),
        grid_spec=pltpu.PrefetchScalarGridSpec(
            num_scalar_prefetch=3,
            grid=(req_here, groups),
            in_specs=[
                pl.BlockSpec((1, new_len, block), lambda r, g, *_: (r, 0, g)),
                pl.BlockSpec((1, pages, 1, page_len, block), lambda r, g, *_: (r, 0, 0, 0, g)),
                pl.BlockSpec((1, pages, 1, page_len, block), lambda r, g, *_: (r, 0, 1, 0, g)),
                pl.BlockSpec((1, 1, local_new, block), lambda r, g, *_: (r, 0, 0, g)),
                pl.BlockSpec((1, 1, local_new, block), lambda r, g, *_: (r, 1, 0, g)),
            ],
            out_specs=[pl.BlockSpec((dests // 2, share + STAT_ROWS, req_here * new_len), lambda r, g, *_: (0, 0, 0))] * 2,
            scratch_shapes=[pltpu.VMEM((2, dests // 2, share + STAT_ROWS, req_here * new_len), BF16)]
            + [pltpu.VMEM((heads + 12, 1, req_here * new_len), F32)] * 2,
        ),
        out_shape=[jax.ShapeDtypeStruct((dests // 2, share + STAT_ROWS, req_here * new_len), BF16)] * 2,
        cost_estimate=pl.CostEstimate(
            flops=4 * req_here * new_len * width * keys,
            bytes_accessed=cache_pool.size * 2 + queries.size * 2,
            transcendentals=req_here * heads * new_len * keys,
        ),
        compiler_params=pltpu.CompilerParams(vmem_limit_bytes=60 << 20),
        name="attend",
    )(table, length, place, queries, cache_pool, cache_pool, new_kv, new_kv)


def merge_kernel(place, own_ref, other_ref, *refs, share):
    outs, spread_sc = refs[:-1], refs[-1]
    tokens = own_ref.shape[2]
    offset = pl.multiple_of(place[0] % 2 * (HD // 2), HD // 2)
    both = (own_ref, other_ref)
    for step, out_ref in enumerate(outs):
        dest = (place[0] // 2 + step) % len(outs)
        tops = [ref[dest, share : share + 8, :].astype(F32) for ref in both]
        top = jnp.maximum(*tops)
        scales = [jnp.exp(t - top) for t in tops]
        den = functools.reduce(jnp.add, [s * ref[dest, share + 8 : share + 16, :].astype(F32) for s, ref in zip(scales, both)])
        total = None
        for side, ref in enumerate(both):
            for head in range(5):
                spread_sc[side, head * HD : head * HD + HD, :] = jnp.broadcast_to(scales[side][head : head + 1, :], (HD, tokens))
            term = ref[dest, :share, :].astype(F32) * spread_sc[side, pl.ds(offset, share), :]
            total = term if total is None else total + term
        out_ref[:share, :] = total.astype(BF16)
        out_ref[share:, :] = jnp.concatenate([top, den], axis=0).astype(BF16)


def merge(place, own, other):
    dests, rows, tokens = own.shape
    whole = pl.BlockSpec((dests, rows, tokens), lambda i, *_: (0, 0, 0))
    return pl.pallas_call(
        functools.partial(merge_kernel, share=rows - STAT_ROWS),
        grid_spec=pltpu.PrefetchScalarGridSpec(
            num_scalar_prefetch=1,
            grid=(1,),
            in_specs=[whole, whole],
            out_specs=[pl.BlockSpec((rows, tokens), lambda i, *_: (0, 0))] * dests,
            scratch_shapes=[pltpu.VMEM((2, 5 * HD, tokens), F32)],
        ),
        out_shape=[jax.ShapeDtypeStruct((rows, tokens), BF16)] * dests,
        cost_estimate=pl.CostEstimate(flops=4 * own.size, bytes_accessed=6 * own.size, transcendentals=0),
        compiler_params=pltpu.CompilerParams(vmem_limit_bytes=10 << 20),
        name="merge",
    )(place, own, other)


def join_kernel(place, *refs, share, groups):
    recv_refs, (res_ref, gain_ref, slot_ref) = refs[:groups], refs[groups : groups + 3]
    outs, (hidden_ref, spread_sc) = refs[groups + 3 : -2], refs[-2:]
    tokens = hidden_ref.shape[1]
    rows, padded = outs[0].shape
    slots = len(outs) * rows
    tops = [ref[share : share + 8, :].astype(F32) for ref in recv_refs]
    top = functools.reduce(jnp.maximum, tops)
    scales = [jnp.exp(t - top) for t in tops]
    den = functools.reduce(jnp.add, [s * ref[share + 8 : share + 16, :].astype(F32) for s, ref in zip(scales, recv_refs)])
    offset = pl.multiple_of(place[0] % 2 * (HD // 2), HD // 2)
    total = res_ref[...]
    for g, ref in enumerate(recv_refs):
        factor = scales[g] / den
        for head in range(5):
            spread_sc[g, head * HD : head * HD + HD, :] = jnp.broadcast_to(factor[head : head + 1, :], (HD, tokens))
        total = total + ref[:share, :].astype(F32) * spread_sc[g, pl.ds(offset, share), :]
    hidden_ref[...] = total
    square = jnp.sum(total * total, axis=0, keepdims=True)
    high = square.astype(BF16).astype(F32)
    row = lax.broadcasted_iota(jnp.int32, (padded - share, tokens), 0)
    tail = jnp.where(row == 0, high, jnp.where(row == 1, square - high, 0.0)).astype(BF16)
    filled = jnp.concatenate([(total * gain_ref[...]).astype(BF16), tail], axis=0)
    at = lax.broadcasted_iota(jnp.int32, (slots, tokens), 0) + place[0] * rows
    at = jnp.where(at < slots, at, at - slots)
    picks = (at == slot_ref[0:1, :]) | (at == slot_ref[1:2, :])
    placed = nt_dot(jnp.where(picks, 1.0, 0.0).astype(BF16), filled).astype(BF16)
    for i, out in enumerate(outs):
        out[...] = placed[i * rows : i * rows + rows]


def join(place, recv, residual, gain, slots, experts):
    rows, tokens = recv[0].shape
    share = rows - STAT_ROWS
    padded = -(-(share + 2) // 128) * 128
    whole = lambda *shape: pl.BlockSpec(shape, lambda i, *_: (0,) * len(shape))
    return pl.pallas_call(
        functools.partial(join_kernel, share=share, groups=len(recv)),
        grid_spec=pltpu.PrefetchScalarGridSpec(
            num_scalar_prefetch=1,
            grid=(1,),
            in_specs=[whole(rows, tokens)] * len(recv) + [whole(share, tokens), whole(share, 1), whole(2, tokens)],
            out_specs=[whole(CAP, padded)] * experts + [whole(share, tokens)],
            scratch_shapes=[pltpu.VMEM((len(recv), 5 * HD, tokens), F32)],
        ),
        out_shape=[jax.ShapeDtypeStruct((CAP, padded), BF16)] * experts + [jax.ShapeDtypeStruct((share, tokens), F32)],
        cost_estimate=pl.CostEstimate(
            flops=2 * experts * CAP * padded * tokens, bytes_accessed=8 * rows * tokens + experts * CAP * padded * 2, transcendentals=0
        ),
        compiler_params=pltpu.CompilerParams(vmem_limit_bytes=10 << 20),
        name="join",
    )(place, *recv, residual, gain, slots)


def norm_kernel(*refs, share):
    recv_refs, out_ref = refs[:-1], refs[-1]
    blocks = [ref[...].astype(F32) for ref in recv_refs]
    square = functools.reduce(jnp.add, [b[:, share : share + 1] + b[:, share + 1 : share + 2] for b in blocks])
    scale = lax.rsqrt(square / (len(blocks) * share) + EPSILON)
    out_ref[...] = jnp.concatenate([b[:, :share] * scale for b in blocks], axis=1).astype(BF16)


def norm_rows(recv, share):
    rows, padded = recv[0].shape
    return pl.pallas_call(
        functools.partial(norm_kernel, share=share),
        out_shape=jax.ShapeDtypeStruct((rows, len(recv) * share), BF16),
        cost_estimate=pl.CostEstimate(flops=0, bytes_accessed=len(recv) * rows * padded * 4, transcendentals=0),
        compiler_params=pltpu.CompilerParams(vmem_limit_bytes=4 << 20),
        name="norm_rows",
    )(*recv)


def stack_kernel(*refs):
    blocks, outs = refs[:4], refs[4:]
    for i, ref in enumerate(blocks):
        outs[i // 2][i % 2] = ref[...]


def stack(blocks):
    rows, width = blocks[0].shape
    pairs = pl.pallas_call(
        stack_kernel,
        out_shape=[jax.ShapeDtypeStruct((2, rows, width), BF16)] * 2,
        cost_estimate=pl.CostEstimate(flops=0, bytes_accessed=16 * rows * width, transcendentals=0),
        compiler_params=pltpu.CompilerParams(vmem_limit_bytes=4 << 20),
        name="stack",
    )(*blocks)
    return [pair.reshape(2 * rows, width) for pair in pairs]


def expert_kernel(place, *refs, count):
    blocks, gate_up_hbm, down_hbm = refs[:count], refs[count], refs[count + 1]
    outs, (x_sc, gate_up_sc, down_sc, both_sc, y_sc, sems) = refs[count + 2 : -6], refs[-6:]
    rows, out_rows, units = blocks[0].shape[0], outs[0].shape[0], down_sc.shape[1]
    half = gate_up_sc.shape[1] // 2
    tile = 256
    loads = [pltpu.make_async_copy(b, x_sc.at[pl.ds(i * rows, rows)], sems.at[i]) for i, b in enumerate(blocks)]
    groups, share = gate_up_hbm.shape[:2]
    for g in range(groups):
        source = (place[0] + groups - g) % groups
        loads.append(pltpu.make_async_copy(gate_up_hbm.at[source], gate_up_sc.at[pl.ds(g * share, share)], sems.at[count + 2 + len(outs) + g]))
    down_load = pltpu.make_async_copy(down_hbm, down_sc, sems.at[count + 1])
    for load in (*loads, down_load):
        load.start()
    for load in loads:
        load.wait()

    @pl.loop(0, 2 * half // tile)
    def _(j):
        lanes = pl.ds(pl.multiple_of(j * tile, tile), tile)
        both_sc[:, lanes] = jnp.dot(x_sc[...], gate_up_sc[:, lanes], preferred_element_type=F32)

    gate, up = both_sc[:, :units], both_sc[:, half : half + units]
    act = (gate / (1.0 + jnp.exp(-gate)) * up).astype(BF16)
    down_load.wait()

    @pl.loop(0, down_sc.shape[0] // tile)
    def _(j):
        lanes = pl.ds(pl.multiple_of(j * tile, tile), tile)
        y_sc[:, lanes] = nt_dot(act, down_sc[lanes, :]).astype(BF16)
        for i, out in enumerate(outs):
            at = pl.ds(i * out_rows, out_rows)
            pltpu.make_async_copy(y_sc.at[at, lanes], out.at[:, lanes], sems.at[count + 2 + i]).start()

    for i, out in enumerate(outs):
        pltpu.make_async_copy(y_sc.at[pl.ds(i * out_rows, out_rows)], out, sems.at[count + 2 + i]).wait()


def expert(place, blocks, gate_up, down, out_rows):
    rows, width = blocks[0].shape
    units = down.shape[1]
    count = len(blocks)
    total = count * rows
    anywhere = pl.BlockSpec(memory_space=pltpu.HBM)
    return pl.pallas_call(
        functools.partial(expert_kernel, count=count),
        in_specs=[pl.BlockSpec(memory_space=pltpu.SMEM)] + [anywhere] * (count + 2),
        out_specs=[anywhere] * (total // out_rows),
        out_shape=[jax.ShapeDtypeStruct((out_rows, width), BF16)] * (total // out_rows),
        scratch_shapes=[
            pltpu.VMEM((total, width), BF16),
            pltpu.VMEM((width, gate_up.shape[2]), BF16),
            pltpu.VMEM(down.shape, BF16),
            pltpu.VMEM((total, gate_up.shape[2]), F32),
            pltpu.VMEM((total, width), BF16),
            pltpu.SemaphoreType.DMA((count + 2 + total // out_rows + gate_up.shape[0],)),
        ],
        cost_estimate=pl.CostEstimate(
            flops=6 * total * width * units,
            bytes_accessed=4 * total * width + 6 * width * units,
            transcendentals=total * units,
        ),
        compiler_params=pltpu.CompilerParams(vmem_limit_bytes=60 << 20),
        name="expert",
    )(place, *blocks, gate_up, down)


def total_of(refs):
    return functools.reduce(jnp.add, [ref[...].astype(F32) for ref in refs])


def add_kernel(*refs):
    outs = refs[6:]
    rows = outs[0].shape[0]
    for i, out in enumerate(outs):
        at = slice(i % 2 * rows, i % 2 * rows + rows)
        lower = slice((i % 2 + 2) * rows, (i % 2 + 3) * rows)
        first, second, third = refs[:3] if i < 2 else refs[3:6]
        total = first[at, :].astype(F32) + second[at, :].astype(F32) + third[lower, :].astype(F32)
        out[...] = total.astype(BF16)


def add_blocks(low, high):
    rows, width = low[0].shape
    return pl.pallas_call(
        add_kernel,
        out_shape=[jax.ShapeDtypeStruct((rows // 2, width), BF16)] * 4,
        cost_estimate=pl.CostEstimate(flops=0, bytes_accessed=16 * rows * width, transcendentals=0),
        compiler_params=pltpu.CompilerParams(vmem_limit_bytes=8 << 20),
        name="add_blocks",
    )(*low, *high)


def finish_kernel(*refs):
    out_ref = refs[-1]
    groups, _, share = out_ref.shape
    both = jnp.concatenate([total_of(refs[:4]), total_of(refs[4:8])], axis=0).astype(BF16)
    for g in range(groups):
        out_ref[g] = both[:, g * share : (g + 1) * share]


def finish(blocks, groups):
    rows, width = blocks[0].shape
    return pl.pallas_call(
        finish_kernel,
        out_shape=jax.ShapeDtypeStruct((groups, 2 * rows, width // groups), BF16),
        cost_estimate=pl.CostEstimate(flops=0, bytes_accessed=20 * rows * width, transcendentals=0),
        compiler_params=pltpu.CompilerParams(vmem_limit_bytes=8 << 20),
        name="finish",
    )(*blocks)


def mix_kernel(rows_ref, slot_ref, weight_ref, hidden_ref, out_ref):
    tokens = out_ref.shape[1]
    slots = rows_ref.shape[0]
    at = lax.broadcasted_iota(jnp.int32, (slots, tokens), 0)
    table = jnp.where(at == slot_ref[0:1, :], weight_ref[0:1, :], 0.0)
    table = table + jnp.where(at == slot_ref[1:2, :], weight_ref[1:2, :], 0.0)
    high = table.astype(BF16)
    low = (table - high.astype(F32)).astype(BF16)
    rows = rows_ref[...]
    out_ref[...] = (hidden_ref[...] + (tn_dot(rows, high) + tn_dot(rows, low))).astype(BF16)


def mix(rows, slots, weights, hidden):
    return pl.pallas_call(
        mix_kernel,
        out_shape=jax.ShapeDtypeStruct(hidden.shape, BF16),
        cost_estimate=pl.CostEstimate(flops=4 * hidden.size * rows.shape[0], bytes_accessed=rows.size * 2 + hidden.size * 6, transcendentals=0),
        compiler_params=pltpu.CompilerParams(vmem_limit_bytes=6 << 20),
        name="mix",
    )(rows, slots, weights, hidden)


def ring_pairs(axis, step):
    pairs = []
    for index in range(RING * RING):
        y, z = divmod(index, RING)
        if axis == "y":
            y = (y + step) % RING
        else:
            z = (z + step) % RING
        pairs.append((index, y * RING + z))
    return pairs


def shift(x, axis, step):
    return lax.ppermute(x, "wide", ring_pairs(axis, step))


def local(
    queries,
    new_kv,
    cache_pool,
    page_table,
    cached_len,
    residual,
    norm_gain,
    expert_ids,
    route_weight,
    w_gate_up,
    w_down,
):
    narrow_count = lax.axis_size("narrow")
    narrow_pos = lax.axis_index("narrow").astype(jnp.int32)
    _, _, width = queries.shape
    token_rows = expert_ids.shape[0]
    expert_count = w_gate_up.shape[0]
    units = w_down.shape[1]
    share = width // narrow_count

    def exchange(x):
        return lax.all_to_all(x, "narrow", 0, 0, tiled=True)

    down_all = exchange(jnp.transpose(w_down, (0, 2, 1)))
    place = narrow_pos.reshape(1)
    own, other = attend(page_table, cached_len, place, queries, cache_pool, new_kv, narrow_count)
    other = lax.ppermute(other, "narrow", [(i, i ^ 1) for i in range(narrow_count)])

    def along(x, step):
        return lax.ppermute(x, "narrow", [(i, (i + step) % narrow_count) for i in range(narrow_count)])

    merged = list(merge(place, own, other))
    w_gate_up, down_all, merged[0] = lax.optimization_barrier((w_gate_up, down_all, merged[0]))
    sums = merged[:1]
    for step in range(1, len(merged)):
        sums.append(along(merged[step], 2 * step))
    gate_up_all = exchange(w_gate_up)

    flat_ids = expert_ids.reshape(token_rows * 2)
    onehot = (flat_ids[:, None] == jnp.arange(expert_count, dtype=jnp.int32)[None, :]).astype(BF16)
    order = jnp.arange(token_rows * 2, dtype=jnp.int32)
    earlier = jnp.dot((order[:, None] > order[None, :]).astype(BF16), onehot, preferred_element_type=F32)
    position = jnp.sum(earlier * onehot.astype(F32), axis=1).astype(jnp.int32)
    slots = (flat_ids * CAP + position).reshape(token_rows, 2)

    res_share = lax.dynamic_slice_in_dim(residual, narrow_pos * share, share, 1).astype(F32).T
    gain_share = lax.dynamic_slice_in_dim(norm_gain, narrow_pos * share, share, 0)[:, None]
    *placed, hidden = join(place, sums, res_share, gain_share, slots.T, expert_count)
    rows = norm_rows([along(x, i) if i else x for i, x in enumerate(placed)], share)
    gate_up_all = jnp.pad(gate_up_all.reshape(width, 2, units), ((0, 0), (0, 0), (0, -units % 128)))
    gate_up_all = gate_up_all.reshape(width, -1).reshape(narrow_count, share, -1)
    down_all = down_all.reshape(width, units)

    half = CAP // 2

    def around(block, axis):
        return [block, *(shift(block, axis, step) for step in STEPS)]

    early, late = [], []
    for first, second, block in (("z", "y", rows[:half]), ("y", "z", rows[half:])):
        low, high = stack(around(block, first))
        before_low, after_high = shift(low, second, 1), shift(high, second, -1)
        before_high, after_low = shift(high, second, 1), shift(low, second, -1)
        far_low, far_high = shift(before_low, second, 1), shift(after_high, second, -1)
        early += [far_low, after_high, far_high, before_low]
        late += [low, high, after_low, before_high]
    early = list(expert(place, early, gate_up_all, down_all, 2 * CAP))
    early[0], *late = lax.optimization_barrier((early[0], *late))
    late = expert(place, late, gate_up_all, down_all, CAP)

    def back(blocks, axis):
        return [blocks[0], *(shift(block, axis, -step) for block, step in zip(blocks[1:], STEPS))]

    def joined(a, b):
        return (a.astype(F32) + b.astype(F32)).astype(BF16)

    four = []
    for color, second in enumerate(("y", "z")):
        low, high, after_low, before_high = late[4 * color : 4 * color + 4]
        got = []
        for block, step in zip(early[2 * color : 2 * color + 2], (1, -1)):
            got.append(shift(block, second, step))
        more_low, more_high = (
            shift(joined(after_low, got[0][:CAP]), second, 1),
            shift(joined(before_high, got[1][:CAP]), second, -1),
        )
        four.append(add_blocks([low, more_low, got[1]], [high, more_high, got[0]]))
    out_rows = finish([*back(four[0], "z"), *back(four[1], "y")], narrow_count)
    out_rows = exchange(out_rows)
    return mix(out_rows.reshape(expert_count * CAP, share), slots.T, route_weight.T, hidden).T


def solution(mesh):
    return jax.shard_map(
        local,
        mesh=mesh,
        in_specs=(
            P("wide", None, None),
            P("wide", None, "narrow", None),
            P("wide", "narrow", None, None, None),
            P("wide", None),
            P("wide"),
            P("wide", None),
            P(),
            P("wide", None),
            P("wide", None),
            P(None, "narrow", None, "wide"),
            P(None, "wide", "narrow"),
        ),
        out_specs=P("wide", "narrow"),
        check_vma=False,
    )
```

```python
import functools

import jax
import jax.numpy as jnp
from jax import lax
from jax.experimental import pallas as pl
from jax.experimental.pallas import tpu as pltpu
from jax.sharding import PartitionSpec as P


HD = 64
CAP = 80
NEG_FILL = -(2.0**100)
SCORE_SCALE = 0.125
EPSILON = 1e-05
STAT_ROWS = 16
RING = 4
STEPS = (2, 1, -1)


F32 = jnp.float32
BF16 = jnp.bfloat16


def nt_dot(a, b):
    return lax.dot_general(a, b, (((1,), (1,)), ((), ())), preferred_element_type=F32)


def tn_dot(a, b):
    return lax.dot_general(a, b, (((0,), (0,)), ((), ())), preferred_element_type=F32)


def attend_kernel(table, length, place, q_ref, k_ref, v_ref, nk_ref, nv_ref, keep_ref, send_ref, sum_sc, top_sc, den_sc, *, share):
    groups = 2 * keep_ref.shape[0]
    req, group = pl.program_id(0), pl.program_id(1)
    new_len = q_ref.shape[1]
    pages, page_len = k_ref.shape[1], k_ref.shape[3]
    local_new = nk_ref.shape[2]
    pairs = q_ref.shape[2] // 128
    lane_at = pl.multiple_of(req * new_len, new_len)
    col = lax.broadcasted_iota(jnp.int32, (new_len, 128), 1)
    row = lax.broadcasted_iota(jnp.int32, (128, new_len), 0)
    page_row = lax.broadcasted_iota(jnp.int32, (page_len, 2 * new_len), 0)
    new_row = lax.broadcasted_iota(jnp.int32, (local_new, 2 * new_len), 0) + place[0] * local_new
    new_col = lax.broadcasted_iota(jnp.int32, (local_new, 2 * new_len), 1) % new_len
    new_valid = new_row <= new_col
    logical = [place[0] + i * groups for i in range(pages)]
    places = [table[req, j] - place[0] * pages for j in logical]
    limits = [length[req] - j * page_len for j in logical]

    @pl.when((req == 0) & (group == 0))
    def _():
        top_sc[...] = jnp.zeros_like(top_sc)
        den_sc[...] = jnp.zeros_like(den_sc)

    for pair in range(pairs):
        at = slice(pair * 128, pair * 128 + 128)
        q = q_ref[0, :, at].astype(F32) * SCORE_SCALE
        both = jnp.concatenate([jnp.where(col < HD, q, 0.0), jnp.where(col < HD, 0.0, q)], axis=0).astype(BF16)
        parts = [
            jnp.where(page_row < limits[i], nt_dot(k_ref[0, places[i], 0, :, at], both), NEG_FILL) for i in range(pages)
        ]
        parts.append(jnp.where(new_valid, nt_dot(nk_ref[0, 0, :, at], both), NEG_FILL))
        top = functools.reduce(jnp.maximum, [jnp.max(s, axis=0, keepdims=True) for s in parts])
        top = top.astype(BF16).astype(F32)
        weights = [jnp.exp(s - top) for s in parts]
        den = functools.reduce(jnp.add, [jnp.sum(w, axis=0, keepdims=True) for w in weights])
        low = jnp.concatenate([w.astype(BF16) for w in weights[:-1]], axis=0)
        values = jnp.concatenate([v_ref[0, places[i], 0, :, at] for i in range(pages)], axis=0)
        num = tn_dot(values, low) + tn_dot(nv_ref[0, 0, :, at], weights[-1].astype(BF16))
        num = jnp.where(row < HD, num[:, :new_len], num[:, new_len:]).astype(BF16)
        for piece in range(4):
            index = (group * pairs + pair) * 4 + piece
            dest = index // (share // 32)
            offset = pl.multiple_of((index - dest * (share // 32)) * 32, 32)
            side = (dest + place[0]) % 2
            sum_sc[side, dest // 2, pl.ds(offset, 32), pl.ds(lane_at, new_len)] = num[piece * 32 : piece * 32 + 32]
        head = (group * pairs + pair) * 2
        for half in range(2):
            lanes = slice(half * new_len, half * new_len + new_len)
            top_sc[head + half, :, pl.ds(lane_at, new_len)] = top[:, lanes]
            den_sc[head + half, :, pl.ds(lane_at, new_len)] = den[:, lanes]

    @pl.when((req == pl.num_programs(0) - 1) & (group == pl.num_programs(1) - 1))
    def _():
        for dest in range(groups):
            first = dest * share // HD
            stats = jnp.concatenate([top_sc[first : first + 8, 0, :], den_sc[first : first + 8, 0, :]], axis=0)
            sum_sc[(dest + place[0]) % 2, dest // 2, share : share + STAT_ROWS, :] = stats.astype(BF16)
        keep_ref[...] = sum_sc[0]
        send_ref[...] = sum_sc[1]


def attend(table, length, place, queries, cache_pool, new_kv, dests):
    req_here, new_len, width = queries.shape
    pages, page_len = cache_pool.shape[1], cache_pool.shape[3]
    local_new = new_kv.shape[2]
    share = width // dests
    groups = 3
    block = width // groups
    heads = width // HD
    keys = pages * page_len + local_new
    return pl.pallas_call(
        functools.partial(attend_kernel, share=share),
        grid_spec=pltpu.PrefetchScalarGridSpec(
            num_scalar_prefetch=3,
            grid=(req_here, groups),
            in_specs=[
                pl.BlockSpec((1, new_len, block), lambda r, g, *_: (r, 0, g)),
                pl.BlockSpec((1, pages, 1, page_len, block), lambda r, g, *_: (r, 0, 0, 0, g)),
                pl.BlockSpec((1, pages, 1, page_len, block), lambda r, g, *_: (r, 0, 1, 0, g)),
                pl.BlockSpec((1, 1, local_new, block), lambda r, g, *_: (r, 0, 0, g)),
                pl.BlockSpec((1, 1, local_new, block), lambda r, g, *_: (r, 1, 0, g)),
            ],
            out_specs=[pl.BlockSpec((dests // 2, share + STAT_ROWS, req_here * new_len), lambda r, g, *_: (0, 0, 0))] * 2,
            scratch_shapes=[pltpu.VMEM((2, dests // 2, share + STAT_ROWS, req_here * new_len), BF16)]
            + [pltpu.VMEM((heads + 12, 1, req_here * new_len), F32)] * 2,
        ),
        out_shape=[jax.ShapeDtypeStruct((dests // 2, share + STAT_ROWS, req_here * new_len), BF16)] * 2,
        cost_estimate=pl.CostEstimate(
            flops=4 * req_here * new_len * width * keys,
            bytes_accessed=cache_pool.size * 2 + queries.size * 2,
            transcendentals=req_here * heads * new_len * keys,
        ),
        compiler_params=pltpu.CompilerParams(vmem_limit_bytes=60 << 20),
        name="attend",
    )(table, length, place, queries, cache_pool, cache_pool, new_kv, new_kv)


def merge_kernel(place, own_ref, other_ref, *refs, share):
    outs, spread_sc = refs[:-1], refs[-1]
    tokens = own_ref.shape[2]
    offset = pl.multiple_of(place[0] % 2 * (HD // 2), HD // 2)
    both = (own_ref, other_ref)
    for step, out_ref in enumerate(outs):
        dest = (place[0] // 2 + step) % len(outs)
        tops = [ref[dest, share : share + 8, :].astype(F32) for ref in both]
        top = jnp.maximum(*tops)
        scales = [jnp.exp(t - top) for t in tops]
        den = functools.reduce(jnp.add, [s * ref[dest, share + 8 : share + 16, :].astype(F32) for s, ref in zip(scales, both)])
        total = None
        for side, ref in enumerate(both):
            for head in range(5):
                spread_sc[side, head * HD : head * HD + HD, :] = jnp.broadcast_to(scales[side][head : head + 1, :], (HD, tokens))
            term = ref[dest, :share, :].astype(F32) * spread_sc[side, pl.ds(offset, share), :]
            total = term if total is None else total + term
        out_ref[:share, :] = total.astype(BF16)
        out_ref[share:, :] = jnp.concatenate([top, den], axis=0).astype(BF16)


def merge(place, own, other):
    dests, rows, tokens = own.shape
    whole = pl.BlockSpec((dests, rows, tokens), lambda i, *_: (0, 0, 0))
    return pl.pallas_call(
        functools.partial(merge_kernel, share=rows - STAT_ROWS),
        grid_spec=pltpu.PrefetchScalarGridSpec(
            num_scalar_prefetch=1,
            grid=(1,),
            in_specs=[whole, whole],
            out_specs=[pl.BlockSpec((rows, tokens), lambda i, *_: (0, 0))] * dests,
            scratch_shapes=[pltpu.VMEM((2, 5 * HD, tokens), F32)],
        ),
        out_shape=[jax.ShapeDtypeStruct((rows, tokens), BF16)] * dests,
        cost_estimate=pl.CostEstimate(flops=4 * own.size, bytes_accessed=6 * own.size, transcendentals=0),
        compiler_params=pltpu.CompilerParams(vmem_limit_bytes=10 << 20),
        name="merge",
    )(place, own, other)


def join_kernel(place, *refs, share, groups):
    recv_refs, (res_ref, gain_ref, slot_ref) = refs[:groups], refs[groups : groups + 3]
    outs, (hidden_ref, spread_sc) = refs[groups + 3 : -2], refs[-2:]
    tokens = hidden_ref.shape[1]
    rows, padded = outs[0].shape
    slots = len(outs) * rows
    tops = [ref[share : share + 8, :].astype(F32) for ref in recv_refs]
    top = functools.reduce(jnp.maximum, tops)
    scales = [jnp.exp(t - top) for t in tops]
    den = functools.reduce(jnp.add, [s * ref[share + 8 : share + 16, :].astype(F32) for s, ref in zip(scales, recv_refs)])
    offset = pl.multiple_of(place[0] % 2 * (HD // 2), HD // 2)
    total = res_ref[...]
    for g, ref in enumerate(recv_refs):
        factor = scales[g] / den
        for head in range(5):
            spread_sc[g, head * HD : head * HD + HD, :] = jnp.broadcast_to(factor[head : head + 1, :], (HD, tokens))
        total = total + ref[:share, :].astype(F32) * spread_sc[g, pl.ds(offset, share), :]
    hidden_ref[...] = total
    square = jnp.sum(total * total, axis=0, keepdims=True)
    high = square.astype(BF16).astype(F32)
    row = lax.broadcasted_iota(jnp.int32, (padded - share, tokens), 0)
    tail = jnp.where(row == 0, high, jnp.where(row == 1, square - high, 0.0)).astype(BF16)
    filled = jnp.concatenate([(total * gain_ref[...]).astype(BF16), tail], axis=0)
    at = lax.broadcasted_iota(jnp.int32, (slots, tokens), 0) + place[0] * rows
    at = jnp.where(at < slots, at, at - slots)
    picks = (at == slot_ref[0:1, :]) | (at == slot_ref[1:2, :])
    placed = nt_dot(jnp.where(picks, 1.0, 0.0).astype(BF16), filled).astype(BF16)
    for i, out in enumerate(outs):
        out[...] = placed[i * rows : i * rows + rows]


def join(place, recv, residual, gain, slots, experts):
    rows, tokens = recv[0].shape
    share = rows - STAT_ROWS
    padded = -(-(share + 2) // 128) * 128
    whole = lambda *shape: pl.BlockSpec(shape, lambda i, *_: (0,) * len(shape))
    return pl.pallas_call(
        functools.partial(join_kernel, share=share, groups=len(recv)),
        grid_spec=pltpu.PrefetchScalarGridSpec(
            num_scalar_prefetch=1,
            grid=(1,),
            in_specs=[whole(rows, tokens)] * len(recv) + [whole(share, tokens), whole(share, 1), whole(2, tokens)],
            out_specs=[whole(CAP, padded)] * experts + [whole(share, tokens)],
            scratch_shapes=[pltpu.VMEM((len(recv), 5 * HD, tokens), F32)],
        ),
        out_shape=[jax.ShapeDtypeStruct((CAP, padded), BF16)] * experts + [jax.ShapeDtypeStruct((share, tokens), F32)],
        cost_estimate=pl.CostEstimate(
            flops=2 * experts * CAP * padded * tokens, bytes_accessed=8 * rows * tokens + experts * CAP * padded * 2, transcendentals=0
        ),
        compiler_params=pltpu.CompilerParams(vmem_limit_bytes=10 << 20),
        name="join",
    )(place, *recv, residual, gain, slots)


def norm_kernel(*refs, share):
    recv_refs, out_ref = refs[:-1], refs[-1]
    blocks = [ref[...].astype(F32) for ref in recv_refs]
    square = functools.reduce(jnp.add, [b[:, share : share + 1] + b[:, share + 1 : share + 2] for b in blocks])
    scale = lax.rsqrt(square / (len(blocks) * share) + EPSILON)
    out_ref[...] = jnp.concatenate([b[:, :share] * scale for b in blocks], axis=1).astype(BF16)


def norm_rows(recv, share):
    rows, padded = recv[0].shape
    return pl.pallas_call(
        functools.partial(norm_kernel, share=share),
        out_shape=jax.ShapeDtypeStruct((rows, len(recv) * share), BF16),
        cost_estimate=pl.CostEstimate(flops=0, bytes_accessed=len(recv) * rows * padded * 4, transcendentals=0),
        compiler_params=pltpu.CompilerParams(vmem_limit_bytes=4 << 20),
        name="norm_rows",
    )(*recv)


def stack_kernel(*refs):
    blocks, outs = refs[:4], refs[4:]
    for i, ref in enumerate(blocks):
        outs[i // 2][i % 2] = ref[...]


def stack(blocks):
    rows, width = blocks[0].shape
    pairs = pl.pallas_call(
        stack_kernel,
        out_shape=[jax.ShapeDtypeStruct((2, rows, width), BF16)] * 2,
        cost_estimate=pl.CostEstimate(flops=0, bytes_accessed=16 * rows * width, transcendentals=0),
        compiler_params=pltpu.CompilerParams(vmem_limit_bytes=4 << 20),
        name="stack",
    )(*blocks)
    return [pair.reshape(2 * rows, width) for pair in pairs]


def expert_kernel(place, *refs, count):
    blocks, gate_up_hbm, down_hbm = refs[:count], refs[count], refs[count + 1]
    outs, (x_sc, part_sc, gate_up_sc, down_sc, both_sc, y_sc, sems) = refs[count + 2 : -7], refs[-7:]
    rows, out_rows, units = blocks[0].shape[0], outs[0].shape[0], down_sc.shape[1]
    half = gate_up_sc.shape[1] // 2
    tile = 256
    loads = [pltpu.make_async_copy(b, x_sc.at[pl.ds(i * rows, rows)], sems.at[i]) for i, b in enumerate(blocks)]
    groups, _, share, _ = gate_up_hbm.shape
    parts = []
    for g in range(groups):
        source = (place[0] + groups - g) % groups
        parts.append(pltpu.make_async_copy(gate_up_hbm.at[source], part_sc.at[g], sems.at[count + 2 + len(outs) + g]))
    down_load = pltpu.make_async_copy(down_hbm, down_sc, sems.at[count + 1])
    for load in (*parts, *loads, down_load):
        load.start()
    for g in range(groups):
        parts[g].wait()
        at = slice(g * share, g * share + share)
        gate_up_sc[at, :units] = part_sc[g, 0]
        gate_up_sc[at, half : half + units] = part_sc[g, 1]
    for load in loads:
        load.wait()

    @pl.loop(0, 2 * half // tile)
    def _(j):
        lanes = pl.ds(pl.multiple_of(j * tile, tile), tile)
        both_sc[:, lanes] = jnp.dot(x_sc[...], gate_up_sc[:, lanes], preferred_element_type=F32)

    gate, up = both_sc[:, :units], both_sc[:, half : half + units]
    act = (gate / (1.0 + jnp.exp(-gate)) * up).astype(BF16)
    down_load.wait()

    @pl.loop(0, down_sc.shape[0] // tile)
    def _(j):
        lanes = pl.ds(pl.multiple_of(j * tile, tile), tile)
        y_sc[:, lanes] = nt_dot(act, down_sc[lanes, :]).astype(BF16)
        for i, out in enumerate(outs):
            at = pl.ds(i * out_rows, out_rows)
            pltpu.make_async_copy(y_sc.at[at, lanes], out.at[:, lanes], sems.at[count + 2 + i]).start()

    for i, out in enumerate(outs):
        pltpu.make_async_copy(y_sc.at[pl.ds(i * out_rows, out_rows)], out, sems.at[count + 2 + i]).wait()


def expert(place, blocks, gate_up, down, out_rows):
    rows, width = blocks[0].shape
    units = down.shape[1]
    count = len(blocks)
    total = count * rows
    packed = 2 * (-(-units // 128) * 128)
    anywhere = pl.BlockSpec(memory_space=pltpu.HBM)
    return pl.pallas_call(
        functools.partial(expert_kernel, count=count),
        in_specs=[pl.BlockSpec(memory_space=pltpu.SMEM)] + [anywhere] * (count + 2),
        out_specs=[anywhere] * (total // out_rows),
        out_shape=[jax.ShapeDtypeStruct((out_rows, width), BF16)] * (total // out_rows),
        scratch_shapes=[
            pltpu.VMEM((total, width), BF16),
            pltpu.VMEM(gate_up.shape, BF16),
            pltpu.VMEM((width, packed), BF16),
            pltpu.VMEM(down.shape, BF16),
            pltpu.VMEM((total, packed), F32),
            pltpu.VMEM((total, width), BF16),
            pltpu.SemaphoreType.DMA((count + 2 + total // out_rows + gate_up.shape[0],)),
        ],
        cost_estimate=pl.CostEstimate(
            flops=6 * total * width * units,
            bytes_accessed=4 * total * width + 6 * width * units,
            transcendentals=total * units,
        ),
        compiler_params=pltpu.CompilerParams(vmem_limit_bytes=60 << 20),
        name="expert",
    )(place, *blocks, gate_up, down)


def total_of(refs):
    return functools.reduce(jnp.add, [ref[...].astype(F32) for ref in refs])


def add_kernel(*refs):
    outs = refs[6:]
    rows = outs[0].shape[0]
    for i, out in enumerate(outs):
        at = slice(i % 2 * rows, i % 2 * rows + rows)
        lower = slice((i % 2 + 2) * rows, (i % 2 + 3) * rows)
        first, second, third = refs[:3] if i < 2 else refs[3:6]
        total = first[at, :].astype(F32) + second[at, :].astype(F32) + third[lower, :].astype(F32)
        out[...] = total.astype(BF16)


def add_blocks(low, high):
    rows, width = low[0].shape
    return pl.pallas_call(
        add_kernel,
        out_shape=[jax.ShapeDtypeStruct((rows // 2, width), BF16)] * 4,
        cost_estimate=pl.CostEstimate(flops=0, bytes_accessed=16 * rows * width, transcendentals=0),
        compiler_params=pltpu.CompilerParams(vmem_limit_bytes=8 << 20),
        name="add_blocks",
    )(*low, *high)


def finish_kernel(*refs):
    out_ref = refs[-1]
    groups, _, share = out_ref.shape
    both = jnp.concatenate([total_of(refs[:4]), total_of(refs[4:8])], axis=0).astype(BF16)
    for g in range(groups):
        out_ref[g] = both[:, g * share : (g + 1) * share]


def finish(blocks, groups):
    rows, width = blocks[0].shape
    return pl.pallas_call(
        finish_kernel,
        out_shape=jax.ShapeDtypeStruct((groups, 2 * rows, width // groups), BF16),
        cost_estimate=pl.CostEstimate(flops=0, bytes_accessed=20 * rows * width, transcendentals=0),
        compiler_params=pltpu.CompilerParams(vmem_limit_bytes=8 << 20),
        name="finish",
    )(*blocks)


def mix_kernel(rows_ref, slot_ref, weight_ref, hidden_ref, out_ref):
    tokens = out_ref.shape[1]
    slots = rows_ref.shape[0]
    at = lax.broadcasted_iota(jnp.int32, (slots, tokens), 0)
    table = jnp.where(at == slot_ref[0:1, :], weight_ref[0:1, :], 0.0)
    table = table + jnp.where(at == slot_ref[1:2, :], weight_ref[1:2, :], 0.0)
    high = table.astype(BF16)
    low = (table - high.astype(F32)).astype(BF16)
    rows = rows_ref[...]
    out_ref[...] = (hidden_ref[...] + (tn_dot(rows, high) + tn_dot(rows, low))).astype(BF16)


def mix(rows, slots, weights, hidden):
    return pl.pallas_call(
        mix_kernel,
        out_shape=jax.ShapeDtypeStruct(hidden.shape, BF16),
        cost_estimate=pl.CostEstimate(flops=4 * hidden.size * rows.shape[0], bytes_accessed=rows.size * 2 + hidden.size * 6, transcendentals=0),
        compiler_params=pltpu.CompilerParams(vmem_limit_bytes=6 << 20),
        name="mix",
    )(rows, slots, weights, hidden)


def ring_pairs(axis, step):
    pairs = []
    for index in range(RING * RING):
        y, z = divmod(index, RING)
        if axis == "y":
            y = (y + step) % RING
        else:
            z = (z + step) % RING
        pairs.append((index, y * RING + z))
    return pairs


def shift(x, axis, step):
    return lax.ppermute(x, "wide", ring_pairs(axis, step))


def local(
    queries,
    new_kv,
    cache_pool,
    page_table,
    cached_len,
    residual,
    norm_gain,
    expert_ids,
    route_weight,
    w_gate_up,
    w_down,
):
    narrow_count = lax.axis_size("narrow")
    narrow_pos = lax.axis_index("narrow").astype(jnp.int32)
    _, _, width = queries.shape
    token_rows = expert_ids.shape[0]
    expert_count = w_gate_up.shape[0]
    units = w_down.shape[1]
    share = width // narrow_count

    def exchange(x):
        return lax.all_to_all(x, "narrow", 0, 0, tiled=True)

    down_all = exchange(jnp.transpose(w_down, (0, 2, 1)))
    place = narrow_pos.reshape(1)
    own, other = attend(page_table, cached_len, place, queries, cache_pool, new_kv, narrow_count)
    other = lax.ppermute(other, "narrow", [(i, i ^ 1) for i in range(narrow_count)])

    def along(x, step):
        return lax.ppermute(x, "narrow", [(i, (i + step) % narrow_count) for i in range(narrow_count)])

    merged = list(merge(place, own, other))
    w_gate_up, down_all, merged[0] = lax.optimization_barrier((w_gate_up, down_all, merged[0]))
    sums = merged[:1]
    for step in range(1, len(merged)):
        sums.append(along(merged[step], 2 * step))
    w_gate_up, sums[1] = lax.optimization_barrier((jnp.transpose(w_gate_up, (0, 2, 1, 3)), sums[1]))
    gate_up_all = exchange(w_gate_up)

    flat_ids = expert_ids.reshape(token_rows * 2)
    onehot = (flat_ids[:, None] == jnp.arange(expert_count, dtype=jnp.int32)[None, :]).astype(BF16)
    order = jnp.arange(token_rows * 2, dtype=jnp.int32)
    earlier = jnp.dot((order[:, None] > order[None, :]).astype(BF16), onehot, preferred_element_type=F32)
    position = jnp.sum(earlier * onehot.astype(F32), axis=1).astype(jnp.int32)
    slots = (flat_ids * CAP + position).reshape(token_rows, 2)

    res_share = lax.dynamic_slice_in_dim(residual, narrow_pos * share, share, 1).astype(F32).T
    gain_share = lax.dynamic_slice_in_dim(norm_gain, narrow_pos * share, share, 0)[:, None]
    *placed, hidden = join(place, sums, res_share, gain_share, slots.T, expert_count)
    for step in range(1, narrow_count):
        placed[step] = along(placed[step], step)
    rows = norm_rows(placed, share)
    down_all = down_all.reshape(width, units)

    half = CAP // 2

    def around(block, axis):
        return [block, *(shift(block, axis, step) for step in STEPS)]

    early, late = [], []
    for first, second, block in (("z", "y", rows[:half]), ("y", "z", rows[half:])):
        low, high = stack(around(block, first))
        before_low, after_high = shift(low, second, 1), shift(high, second, -1)
        before_high, after_low = shift(high, second, 1), shift(low, second, -1)
        far_low, far_high = shift(before_low, second, 1), shift(after_high, second, -1)
        early += [far_low, after_high, far_high, before_low]
        late += [low, high, after_low, before_high]
    early = list(expert(place, early, gate_up_all, down_all, 2 * CAP))
    early[0], *late = lax.optimization_barrier((early[0], *late))
    late = expert(place, late, gate_up_all, down_all, CAP)

    def back(blocks, axis):
        return [blocks[0], *(shift(block, axis, -step) for block, step in zip(blocks[1:], STEPS))]

    def joined(a, b):
        return (a.astype(F32) + b.astype(F32)).astype(BF16)

    four = []
    for color, second in enumerate(("y", "z")):
        low, high, after_low, before_high = late[4 * color : 4 * color + 4]
        got = []
        for block, step in zip(early[2 * color : 2 * color + 2], (1, -1)):
            got.append(shift(block, second, step))
        more_low, more_high = (
            shift(joined(after_low, got[0][:CAP]), second, 1),
            shift(joined(before_high, got[1][:CAP]), second, -1),
        )
        four.append(add_blocks([low, more_low, got[1]], [high, more_high, got[0]]))
    out_rows = finish([*back(four[0], "z"), *back(four[1], "y")], narrow_count)
    out_rows = exchange(out_rows)
    return mix(out_rows.reshape(expert_count * CAP, share), slots.T, route_weight.T, hidden).T


def solution(mesh):
    return jax.shard_map(
        local,
        mesh=mesh,
        in_specs=(
            P("wide", None, None),
            P("wide", None, "narrow", None),
            P("wide", "narrow", None, None, None),
            P("wide", None),
            P("wide"),
            P("wide", None),
            P(),
            P("wide", None),
            P("wide", None),
            P(None, "narrow", None, "wide"),
            P(None, "wide", "narrow"),
        ),
        out_specs=P("wide", "narrow"),
        check_vma=False,
    )
```

```python
import functools

import jax
import jax.numpy as jnp
from jax import lax
from jax.experimental import pallas as pl
from jax.experimental.pallas import tpu as pltpu
from jax.sharding import PartitionSpec as P


HD = 64
CAP = 80
NEG_FILL = -(2.0**100)
SCORE_SCALE = 0.125
EPSILON = 1e-05
STAT_ROWS = 16
RING = 4
STEPS = (2, 1, -1)


F32 = jnp.float32
BF16 = jnp.bfloat16


def nt_dot(a, b):
    return lax.dot_general(a, b, (((1,), (1,)), ((), ())), preferred_element_type=F32)


def tn_dot(a, b):
    return lax.dot_general(a, b, (((0,), (0,)), ((), ())), preferred_element_type=F32)


def attend_kernel(table, length, place, q_ref, k_ref, v_ref, nk_ref, nv_ref, keep_ref, send_ref, score_sc, sum_sc, top_sc, den_sc, *, share):
    groups = 2 * keep_ref.shape[0]
    req, group = pl.program_id(0), pl.program_id(1)
    new_len = q_ref.shape[1]
    pages, page_len = k_ref.shape[1], k_ref.shape[3]
    local_new = nk_ref.shape[2]
    pairs = q_ref.shape[2] // 128
    lane_at = pl.multiple_of(req * new_len, new_len)
    col = lax.broadcasted_iota(jnp.int32, (new_len, 128), 1)
    row = lax.broadcasted_iota(jnp.int32, (128, new_len), 0)
    new_row = lax.broadcasted_iota(jnp.int32, (local_new, 2 * new_len), 0) + place[0] * local_new
    new_col = lax.broadcasted_iota(jnp.int32, (local_new, 2 * new_len), 1) % new_len
    new_valid = new_row <= new_col
    logical = [place[0] + i * groups for i in range(pages)]
    places = [table[req, j] - place[0] * pages for j in logical]
    limits = [length[req] - j * page_len for j in logical]

    @pl.when((req == 0) & (group == 0))
    def _():
        top_sc[...] = jnp.zeros_like(top_sc)
        den_sc[...] = jnp.zeros_like(den_sc)

    lane = lax.broadcasted_iota(jnp.int32, (page_len, 128), 1)
    key = lax.broadcasted_iota(jnp.int32, (page_len, 128), 0)
    biases = [jnp.where((lane == 0) & (key >= limits[i]), NEG_FILL, 0.0).astype(BF16) for i in range(pages)]
    one = jnp.where(lax.broadcasted_iota(jnp.int32, (2 * new_len, 128), 1) == 0, 1.0, 0.0).astype(BF16)

    def score(pair):
        at = slice(pair * 128, pair * 128 + 128)
        q = q_ref[0, :, at].astype(F32) * SCORE_SCALE
        both = jnp.concatenate([jnp.where(col < HD, q, 0.0), jnp.where(col < HD, 0.0, q)], axis=0).astype(BF16)
        wide = jnp.concatenate([both, one], axis=1)
        for i in range(pages):
            keys = jnp.concatenate([k_ref[0, places[i], 0, :, at], biases[i]], axis=1)
            score_sc[pair % 2, i * page_len : (i + 1) * page_len, :] = nt_dot(keys, wide)
        score_sc[pair % 2, pages * page_len :, :] = jnp.where(new_valid, nt_dot(nk_ref[0, 0, :, at], both), NEG_FILL)

    score(0)
    for pair in range(pairs):
        at = slice(pair * 128, pair * 128 + 128)
        if pair + 1 < pairs:
            score(pair + 1)
        cuts = [slice(i * page_len, (i + 1) * page_len) for i in range(pages)] + [slice(pages * page_len, None)]
        tops = [jnp.max(score_sc[pair % 2, cut, :], axis=0, keepdims=True) for cut in cuts]
        top = functools.reduce(jnp.maximum, tops).astype(BF16).astype(F32)
        weights = [jnp.exp(score_sc[pair % 2, cut, :] - top) for cut in cuts]
        den = functools.reduce(jnp.add, [jnp.sum(w, axis=0, keepdims=True) for w in weights])
        low = jnp.concatenate([w.astype(BF16) for w in weights[:-1]], axis=0)
        values = jnp.concatenate([v_ref[0, places[i], 0, :, at] for i in range(pages)], axis=0)
        num = tn_dot(values, low) + tn_dot(nv_ref[0, 0, :, at], weights[-1].astype(BF16))
        num = jnp.where(row < HD, num[:, :new_len], num[:, new_len:]).astype(BF16)
        for piece in range(4):
            index = (group * pairs + pair) * 4 + piece
            dest = index // (share // 32)
            offset = pl.multiple_of((index - dest * (share // 32)) * 32, 32)
            side = (dest + place[0]) % 2
            sum_sc[side, dest // 2, pl.ds(offset, 32), pl.ds(lane_at, new_len)] = num[piece * 32 : piece * 32 + 32]
        head = (group * pairs + pair) * 2
        for half in range(2):
            lanes = slice(half * new_len, half * new_len + new_len)
            top_sc[head + half, :, pl.ds(lane_at, new_len)] = top[:, lanes]
            den_sc[head + half, :, pl.ds(lane_at, new_len)] = den[:, lanes]

    @pl.when((req == pl.num_programs(0) - 1) & (group == pl.num_programs(1) - 1))
    def _():
        for dest in range(groups):
            first = dest * share // HD
            stats = jnp.concatenate([top_sc[first : first + 8, 0, :], den_sc[first : first + 8, 0, :]], axis=0)
            sum_sc[(dest + place[0]) % 2, dest // 2, share : share + STAT_ROWS, :] = stats.astype(BF16)
        keep_ref[...] = sum_sc[0]
        send_ref[...] = sum_sc[1]


def attend(table, length, place, queries, cache_pool, new_kv, dests):
    req_here, new_len, width = queries.shape
    pages, page_len = cache_pool.shape[1], cache_pool.shape[3]
    local_new = new_kv.shape[2]
    share = width // dests
    groups = 3
    block = width // groups
    heads = width // HD
    keys = pages * page_len + local_new
    return pl.pallas_call(
        functools.partial(attend_kernel, share=share),
        grid_spec=pltpu.PrefetchScalarGridSpec(
            num_scalar_prefetch=3,
            grid=(req_here, groups),
            in_specs=[
                pl.BlockSpec((1, new_len, block), lambda r, g, *_: (r, 0, g)),
                pl.BlockSpec((1, pages, 1, page_len, block), lambda r, g, *_: (r, 0, 0, 0, g)),
                pl.BlockSpec((1, pages, 1, page_len, block), lambda r, g, *_: (r, 0, 1, 0, g)),
                pl.BlockSpec((1, 1, local_new, block), lambda r, g, *_: (r, 0, 0, g)),
                pl.BlockSpec((1, 1, local_new, block), lambda r, g, *_: (r, 1, 0, g)),
            ],
            out_specs=[pl.BlockSpec((dests // 2, share + STAT_ROWS, req_here * new_len), lambda r, g, *_: (0, 0, 0))] * 2,
            scratch_shapes=[pltpu.VMEM((2, keys, 2 * new_len), F32)]
            + [pltpu.VMEM((2, dests // 2, share + STAT_ROWS, req_here * new_len), BF16)]
            + [pltpu.VMEM((heads + 12, 1, req_here * new_len), F32)] * 2,
        ),
        out_shape=[jax.ShapeDtypeStruct((dests // 2, share + STAT_ROWS, req_here * new_len), BF16)] * 2,
        cost_estimate=pl.CostEstimate(
            flops=4 * req_here * new_len * width * keys,
            bytes_accessed=cache_pool.size * 2 + queries.size * 2,
            transcendentals=req_here * heads * new_len * keys,
        ),
        compiler_params=pltpu.CompilerParams(vmem_limit_bytes=60 << 20),
        name="attend",
    )(table, length, place, queries, cache_pool, cache_pool, new_kv, new_kv)


def merge_kernel(place, own_ref, other_ref, *refs, share):
    outs, spread_sc = refs[:-1], refs[-1]
    tokens = own_ref.shape[2]
    offset = pl.multiple_of(place[0] % 2 * (HD // 2), HD // 2)
    both = (own_ref, other_ref)
    for step, out_ref in enumerate(outs):
        dest = (place[0] // 2 + step) % len(outs)
        tops = [ref[dest, share : share + 8, :].astype(F32) for ref in both]
        top = jnp.maximum(*tops)
        scales = [jnp.exp(t - top) for t in tops]
        den = functools.reduce(jnp.add, [s * ref[dest, share + 8 : share + 16, :].astype(F32) for s, ref in zip(scales, both)])
        total = None
        for side, ref in enumerate(both):
            for head in range(5):
                spread_sc[side, head * HD : head * HD + HD, :] = jnp.broadcast_to(scales[side][head : head + 1, :], (HD, tokens))
            term = ref[dest, :share, :].astype(F32) * spread_sc[side, pl.ds(offset, share), :]
            total = term if total is None else total + term
        out_ref[:share, :] = total.astype(BF16)
        out_ref[share:, :] = jnp.concatenate([top, den], axis=0).astype(BF16)


def merge(place, own, other):
    dests, rows, tokens = own.shape
    whole = pl.BlockSpec((dests, rows, tokens), lambda i, *_: (0, 0, 0))
    return pl.pallas_call(
        functools.partial(merge_kernel, share=rows - STAT_ROWS),
        grid_spec=pltpu.PrefetchScalarGridSpec(
            num_scalar_prefetch=1,
            grid=(1,),
            in_specs=[whole, whole],
            out_specs=[pl.BlockSpec((rows, tokens), lambda i, *_: (0, 0))] * dests,
            scratch_shapes=[pltpu.VMEM((2, 5 * HD, tokens), F32)],
        ),
        out_shape=[jax.ShapeDtypeStruct((rows, tokens), BF16)] * dests,
        cost_estimate=pl.CostEstimate(flops=4 * own.size, bytes_accessed=6 * own.size, transcendentals=0),
        compiler_params=pltpu.CompilerParams(vmem_limit_bytes=10 << 20),
        name="merge",
    )(place, own, other)


def join_kernel(place, *refs, share, groups):
    recv_refs, (res_ref, gain_ref, slot_ref) = refs[:groups], refs[groups : groups + 3]
    outs, (hidden_ref, spread_sc) = refs[groups + 3 : -2], refs[-2:]
    tokens = hidden_ref.shape[1]
    rows, padded = outs[0].shape
    slots = len(outs) * rows
    tops = [ref[share : share + 8, :].astype(F32) for ref in recv_refs]
    top = functools.reduce(jnp.maximum, tops)
    scales = [jnp.exp(t - top) for t in tops]
    den = functools.reduce(jnp.add, [s * ref[share + 8 : share + 16, :].astype(F32) for s, ref in zip(scales, recv_refs)])
    offset = pl.multiple_of(place[0] % 2 * (HD // 2), HD // 2)
    total = res_ref[...]
    for g, ref in enumerate(recv_refs):
        factor = scales[g] / den
        for head in range(5):
            spread_sc[g, head * HD : head * HD + HD, :] = jnp.broadcast_to(factor[head : head + 1, :], (HD, tokens))
        total = total + ref[:share, :].astype(F32) * spread_sc[g, pl.ds(offset, share), :]
    hidden_ref[...] = total
    square = jnp.sum(total * total, axis=0, keepdims=True)
    high = square.astype(BF16).astype(F32)
    row = lax.broadcasted_iota(jnp.int32, (padded - share, tokens), 0)
    tail = jnp.where(row == 0, high, jnp.where(row == 1, square - high, 0.0)).astype(BF16)
    filled = jnp.concatenate([(total * gain_ref[...]).astype(BF16), tail], axis=0)
    at = lax.broadcasted_iota(jnp.int32, (slots, tokens), 0) + place[0] * rows
    at = jnp.where(at < slots, at, at - slots)
    picks = (at == slot_ref[0:1, :]) | (at == slot_ref[1:2, :])
    placed = nt_dot(jnp.where(picks, 1.0, 0.0).astype(BF16), filled).astype(BF16)
    for i, out in enumerate(outs):
        out[...] = placed[i * rows : i * rows + rows]


def join(place, recv, residual, gain, slots, experts):
    rows, tokens = recv[0].shape
    share = rows - STAT_ROWS
    padded = -(-(share + 2) // 128) * 128
    whole = lambda *shape: pl.BlockSpec(shape, lambda i, *_: (0,) * len(shape))
    return pl.pallas_call(
        functools.partial(join_kernel, share=share, groups=len(recv)),
        grid_spec=pltpu.PrefetchScalarGridSpec(
            num_scalar_prefetch=1,
            grid=(1,),
            in_specs=[whole(rows, tokens)] * len(recv) + [whole(share, tokens), whole(share, 1), whole(2, tokens)],
            out_specs=[whole(CAP, padded)] * experts + [whole(share, tokens)],
            scratch_shapes=[pltpu.VMEM((len(recv), 5 * HD, tokens), F32)],
        ),
        out_shape=[jax.ShapeDtypeStruct((CAP, padded), BF16)] * experts + [jax.ShapeDtypeStruct((share, tokens), F32)],
        cost_estimate=pl.CostEstimate(
            flops=2 * experts * CAP * padded * tokens, bytes_accessed=8 * rows * tokens + experts * CAP * padded * 2, transcendentals=0
        ),
        compiler_params=pltpu.CompilerParams(vmem_limit_bytes=10 << 20),
        name="join",
    )(place, *recv, residual, gain, slots)


def norm_kernel(*refs, share):
    recv_refs, out_ref = refs[:-1], refs[-1]
    blocks = [ref[...].astype(F32) for ref in recv_refs]
    square = functools.reduce(jnp.add, [b[:, share : share + 1] + b[:, share + 1 : share + 2] for b in blocks])
    scale = lax.rsqrt(square / (len(blocks) * share) + EPSILON)
    out_ref[...] = jnp.concatenate([b[:, :share] * scale for b in blocks], axis=1).astype(BF16)


def norm_rows(recv, share):
    rows, padded = recv[0].shape
    return pl.pallas_call(
        functools.partial(norm_kernel, share=share),
        out_shape=jax.ShapeDtypeStruct((rows, len(recv) * share), BF16),
        cost_estimate=pl.CostEstimate(flops=0, bytes_accessed=len(recv) * rows * padded * 4, transcendentals=0),
        compiler_params=pltpu.CompilerParams(vmem_limit_bytes=4 << 20),
        name="norm_rows",
    )(*recv)


def stack_kernel(*refs):
    blocks, outs = refs[:4], refs[4:]
    for i, ref in enumerate(blocks):
        outs[i // 2][i % 2] = ref[...]


def stack(blocks):
    rows, width = blocks[0].shape
    pairs = pl.pallas_call(
        stack_kernel,
        out_shape=[jax.ShapeDtypeStruct((2, rows, width), BF16)] * 2,
        cost_estimate=pl.CostEstimate(flops=0, bytes_accessed=16 * rows * width, transcendentals=0),
        compiler_params=pltpu.CompilerParams(vmem_limit_bytes=4 << 20),
        name="stack",
    )(*blocks)
    return [pair.reshape(2 * rows, width) for pair in pairs]


def expert_kernel(place, *refs, count):
    blocks, gate_up_hbm, down_hbm = refs[:count], refs[count], refs[count + 1]
    outs, (x_sc, part_sc, gate_up_sc, down_sc, both_sc, y_sc, sems) = refs[count + 2 : -7], refs[-7:]
    rows, out_rows, units = blocks[0].shape[0], outs[0].shape[0], down_sc.shape[1]
    half = gate_up_sc.shape[1] // 2
    tile = 256
    loads = [pltpu.make_async_copy(b, x_sc.at[pl.ds(i * rows, rows)], sems.at[i]) for i, b in enumerate(blocks)]
    groups, _, share, _ = gate_up_hbm.shape
    parts = []
    for g in range(groups):
        source = (place[0] + groups - g) % groups
        parts.append(pltpu.make_async_copy(gate_up_hbm.at[source], part_sc.at[g], sems.at[count + 2 + len(outs) + g]))
    down_load = pltpu.make_async_copy(down_hbm, down_sc, sems.at[count + 1])
    for load in (*parts, *loads, down_load):
        load.start()
    for g in range(groups):
        parts[g].wait()
        at = slice(g * share, g * share + share)
        gate_up_sc[at, :units] = part_sc[g, 0]
        gate_up_sc[at, half : half + units] = part_sc[g, 1]
    for load in loads:
        load.wait()

    @pl.loop(0, 2 * half // tile)
    def _(j):
        lanes = pl.ds(pl.multiple_of(j * tile, tile), tile)
        both_sc[:, lanes] = jnp.dot(x_sc[...], gate_up_sc[:, lanes], preferred_element_type=F32)

    gate, up = both_sc[:, :units], both_sc[:, half : half + units]
    act = (gate / (1.0 + jnp.exp(-gate)) * up).astype(BF16)
    down_load.wait()

    @pl.loop(0, down_sc.shape[0] // tile)
    def _(j):
        lanes = pl.ds(pl.multiple_of(j * tile, tile), tile)
        y_sc[:, lanes] = nt_dot(act, down_sc[lanes, :]).astype(BF16)
        for i, out in enumerate(outs):
            at = pl.ds(i * out_rows, out_rows)
            pltpu.make_async_copy(y_sc.at[at, lanes], out.at[:, lanes], sems.at[count + 2 + i]).start()

    for i, out in enumerate(outs):
        pltpu.make_async_copy(y_sc.at[pl.ds(i * out_rows, out_rows)], out, sems.at[count + 2 + i]).wait()


def expert(place, blocks, gate_up, down, out_rows):
    rows, width = blocks[0].shape
    units = down.shape[1]
    count = len(blocks)
    total = count * rows
    packed = 2 * (-(-units // 128) * 128)
    anywhere = pl.BlockSpec(memory_space=pltpu.HBM)
    return pl.pallas_call(
        functools.partial(expert_kernel, count=count),
        in_specs=[pl.BlockSpec(memory_space=pltpu.SMEM)] + [anywhere] * (count + 2),
        out_specs=[anywhere] * (total // out_rows),
        out_shape=[jax.ShapeDtypeStruct((out_rows, width), BF16)] * (total // out_rows),
        scratch_shapes=[
            pltpu.VMEM((total, width), BF16),
            pltpu.VMEM(gate_up.shape, BF16),
            pltpu.VMEM((width, packed), BF16),
            pltpu.VMEM(down.shape, BF16),
            pltpu.VMEM((total, packed), F32),
            pltpu.VMEM((total, width), BF16),
            pltpu.SemaphoreType.DMA((count + 2 + total // out_rows + gate_up.shape[0],)),
        ],
        cost_estimate=pl.CostEstimate(
            flops=6 * total * width * units,
            bytes_accessed=4 * total * width + 6 * width * units,
            transcendentals=total * units,
        ),
        compiler_params=pltpu.CompilerParams(vmem_limit_bytes=60 << 20),
        name="expert",
    )(place, *blocks, gate_up, down)


def total_of(refs):
    return functools.reduce(jnp.add, [ref[...].astype(F32) for ref in refs])


def add_kernel(*refs):
    outs = refs[6:]
    rows = outs[0].shape[0]
    for i, out in enumerate(outs):
        at = slice(i % 2 * rows, i % 2 * rows + rows)
        lower = slice((i % 2 + 2) * rows, (i % 2 + 3) * rows)
        first, second, third = refs[:3] if i < 2 else refs[3:6]
        total = first[at, :].astype(F32) + second[at, :].astype(F32) + third[lower, :].astype(F32)
        out[...] = total.astype(BF16)


def add_blocks(low, high):
    rows, width = low[0].shape
    return pl.pallas_call(
        add_kernel,
        out_shape=[jax.ShapeDtypeStruct((rows // 2, width), BF16)] * 4,
        cost_estimate=pl.CostEstimate(flops=0, bytes_accessed=16 * rows * width, transcendentals=0),
        compiler_params=pltpu.CompilerParams(vmem_limit_bytes=8 << 20),
        name="add_blocks",
    )(*low, *high)


def finish_kernel(*refs):
    out_ref = refs[-1]
    groups, _, share = out_ref.shape
    both = jnp.concatenate([total_of(refs[:4]), total_of(refs[4:8])], axis=0).astype(BF16)
    for g in range(groups):
        out_ref[g] = both[:, g * share : (g + 1) * share]


def finish(blocks, groups):
    rows, width = blocks[0].shape
    return pl.pallas_call(
        finish_kernel,
        out_shape=jax.ShapeDtypeStruct((groups, 2 * rows, width // groups), BF16),
        cost_estimate=pl.CostEstimate(flops=0, bytes_accessed=20 * rows * width, transcendentals=0),
        compiler_params=pltpu.CompilerParams(vmem_limit_bytes=8 << 20),
        name="finish",
    )(*blocks)


def mix_kernel(rows_ref, slot_ref, weight_ref, hidden_ref, out_ref):
    tokens = out_ref.shape[1]
    slots = rows_ref.shape[0]
    at = lax.broadcasted_iota(jnp.int32, (slots, tokens), 0)
    table = jnp.where(at == slot_ref[0:1, :], weight_ref[0:1, :], 0.0)
    table = table + jnp.where(at == slot_ref[1:2, :], weight_ref[1:2, :], 0.0)
    high = table.astype(BF16)
    low = (table - high.astype(F32)).astype(BF16)
    rows = rows_ref[...]
    out_ref[...] = (hidden_ref[...] + (tn_dot(rows, high) + tn_dot(rows, low))).astype(BF16)


def mix(rows, slots, weights, hidden):
    return pl.pallas_call(
        mix_kernel,
        out_shape=jax.ShapeDtypeStruct(hidden.shape, BF16),
        cost_estimate=pl.CostEstimate(flops=4 * hidden.size * rows.shape[0], bytes_accessed=rows.size * 2 + hidden.size * 6, transcendentals=0),
        compiler_params=pltpu.CompilerParams(vmem_limit_bytes=6 << 20),
        name="mix",
    )(rows, slots, weights, hidden)


def ring_pairs(axis, step):
    pairs = []
    for index in range(RING * RING):
        y, z = divmod(index, RING)
        if axis == "y":
            y = (y + step) % RING
        else:
            z = (z + step) % RING
        pairs.append((index, y * RING + z))
    return pairs


def shift(x, axis, step):
    return lax.ppermute(x, "wide", ring_pairs(axis, step))


def local(
    queries,
    new_kv,
    cache_pool,
    page_table,
    cached_len,
    residual,
    norm_gain,
    expert_ids,
    route_weight,
    w_gate_up,
    w_down,
):
    narrow_count = lax.axis_size("narrow")
    narrow_pos = lax.axis_index("narrow").astype(jnp.int32)
    _, _, width = queries.shape
    token_rows = expert_ids.shape[0]
    expert_count = w_gate_up.shape[0]
    units = w_down.shape[1]
    share = width // narrow_count

    def exchange(x):
        return lax.all_to_all(x, "narrow", 0, 0, tiled=True)

    down_all = exchange(jnp.transpose(w_down, (0, 2, 1)))
    place = narrow_pos.reshape(1)
    own, other = attend(page_table, cached_len, place, queries, cache_pool, new_kv, narrow_count)
    other = lax.ppermute(other, "narrow", [(i, i ^ 1) for i in range(narrow_count)])

    def along(x, step):
        return lax.ppermute(x, "narrow", [(i, (i + step) % narrow_count) for i in range(narrow_count)])

    merged = list(merge(place, own, other))
    w_gate_up, down_all, merged[0] = lax.optimization_barrier((w_gate_up, down_all, merged[0]))
    sums = merged[:1]
    for step in range(1, len(merged)):
        sums.append(along(merged[step], 2 * step))
    w_gate_up, sums[1] = lax.optimization_barrier((jnp.transpose(w_gate_up, (0, 2, 1, 3)), sums[1]))
    gate_up_all = exchange(w_gate_up)

    flat_ids = expert_ids.reshape(token_rows * 2)
    onehot = (flat_ids[:, None] == jnp.arange(expert_count, dtype=jnp.int32)[None, :]).astype(BF16)
    order = jnp.arange(token_rows * 2, dtype=jnp.int32)
    earlier = jnp.dot((order[:, None] > order[None, :]).astype(BF16), onehot, preferred_element_type=F32)
    position = jnp.sum(earlier * onehot.astype(F32), axis=1).astype(jnp.int32)
    slots = (flat_ids * CAP + position).reshape(token_rows, 2)

    res_share = lax.dynamic_slice_in_dim(residual, narrow_pos * share, share, 1).astype(F32).T
    gain_share = lax.dynamic_slice_in_dim(norm_gain, narrow_pos * share, share, 0)[:, None]
    *placed, hidden = join(place, sums, res_share, gain_share, slots.T, expert_count)
    for step in range(1, narrow_count):
        placed[step] = along(placed[step], step)
    rows = norm_rows(placed, share)
    down_all = down_all.reshape(width, units)

    half = CAP // 2

    def around(block, axis):
        return [block, *(shift(block, axis, step) for step in STEPS)]

    early, late = [], []
    for first, second, block in (("z", "y", rows[:half]), ("y", "z", rows[half:])):
        low, high = stack(around(block, first))
        before_low, after_high = shift(low, second, 1), shift(high, second, -1)
        before_high, after_low = shift(high, second, 1), shift(low, second, -1)
        far_low, far_high = shift(before_low, second, 1), shift(after_high, second, -1)
        early += [far_low, after_high, far_high, before_low]
        late += [low, high, after_low, before_high]
    early = list(expert(place, early, gate_up_all, down_all, 2 * CAP))
    early[0], *late = lax.optimization_barrier((early[0], *late))
    late = expert(place, late, gate_up_all, down_all, CAP)

    def back(blocks, axis):
        return [blocks[0], *(shift(block, axis, -step) for block, step in zip(blocks[1:], STEPS))]

    def joined(a, b):
        return (a.astype(F32) + b.astype(F32)).astype(BF16)

    four = []
    for color, second in enumerate(("y", "z")):
        low, high, after_low, before_high = late[4 * color : 4 * color + 4]
        got = []
        for block, step in zip(early[2 * color : 2 * color + 2], (1, -1)):
            got.append(shift(block, second, step))
        more_low, more_high = (
            shift(joined(after_low, got[0][:CAP]), second, 1),
            shift(joined(before_high, got[1][:CAP]), second, -1),
        )
        four.append(add_blocks([low, more_low, got[1]], [high, more_high, got[0]]))
    out_rows = finish([*back(four[0], "z"), *back(four[1], "y")], narrow_count)
    out_rows = exchange(out_rows)
    return mix(out_rows.reshape(expert_count * CAP, share), slots.T, route_weight.T, hidden).T


def solution(mesh):
    return jax.shard_map(
        local,
        mesh=mesh,
        in_specs=(
            P("wide", None, None),
            P("wide", None, "narrow", None),
            P("wide", "narrow", None, None, None),
            P("wide", None),
            P("wide"),
            P("wide", None),
            P(),
            P("wide", None),
            P("wide", None),
            P(None, "narrow", None, "wide"),
            P(None, "wide", "narrow"),
        ),
        out_specs=P("wide", "narrow"),
        check_vma=False,
    )
```

```python
import functools

import jax
import jax.numpy as jnp
from jax import lax
from jax.experimental import pallas as pl
from jax.experimental.pallas import tpu as pltpu
from jax.sharding import PartitionSpec as P


HD = 64
CAP = 80
NEG_FILL = -(2.0**100)
SCORE_SCALE = 0.125
EPSILON = 1e-05
STAT_ROWS = 16
RING = 4
STEPS = (2, 1, -1)


F32 = jnp.float32
BF16 = jnp.bfloat16


def nt_dot(a, b):
    return lax.dot_general(a, b, (((1,), (1,)), ((), ())), preferred_element_type=F32)


def tn_dot(a, b):
    return lax.dot_general(a, b, (((0,), (0,)), ((), ())), preferred_element_type=F32)


def attend_kernel(table, length, place, q_ref, k_ref, v_ref, nk_ref, nv_ref, keep_ref, send_ref, score_sc, sum_sc, top_sc, den_sc, *, share):
    groups = 2 * keep_ref.shape[0]
    req, group = pl.program_id(0), pl.program_id(1)
    new_len = q_ref.shape[1]
    pages, page_len = k_ref.shape[1], k_ref.shape[3]
    local_new = nk_ref.shape[2]
    pairs = q_ref.shape[2] // 128
    lane_at = pl.multiple_of(req * new_len, new_len)
    col = lax.broadcasted_iota(jnp.int32, (new_len, 128), 1)
    row = lax.broadcasted_iota(jnp.int32, (128, new_len), 0)
    new_row = lax.broadcasted_iota(jnp.int32, (local_new, 2 * new_len), 0) + place[0] * local_new
    new_col = lax.broadcasted_iota(jnp.int32, (local_new, 2 * new_len), 1) % new_len
    new_valid = new_row <= new_col
    logical = [place[0] + i * groups for i in range(pages)]
    homes = [table[req, j] - place[0] * pages for j in logical]
    ends = [length[req] - j * page_len for j in logical]
    limits = [sum(jnp.where(home == slot, end, 0) for home, end in zip(homes, ends)) for slot in range(pages)]

    @pl.when((req == 0) & (group == 0))
    def _():
        top_sc[...] = jnp.zeros_like(top_sc)
        den_sc[...] = jnp.zeros_like(den_sc)

    lane = lax.broadcasted_iota(jnp.int32, (page_len, 128), 1)
    key = lax.broadcasted_iota(jnp.int32, (page_len, 128), 0)
    biases = [jnp.where((lane == 0) & (key >= limits[i]), NEG_FILL, 0.0).astype(BF16) for i in range(pages)]
    one = jnp.where(lax.broadcasted_iota(jnp.int32, (2 * new_len, 128), 1) == 0, 1.0, 0.0).astype(BF16)

    def score(pair):
        at = slice(pair * 128, pair * 128 + 128)
        q = q_ref[0, :, at].astype(F32) * SCORE_SCALE
        both = jnp.concatenate([jnp.where(col < HD, q, 0.0), jnp.where(col < HD, 0.0, q)], axis=0).astype(BF16)
        wide = jnp.concatenate([both, one], axis=1)
        for i in range(pages):
            keys = jnp.concatenate([k_ref[0, i, 0, :, at], biases[i]], axis=1)
            score_sc[pair % 2, i * page_len : (i + 1) * page_len, :] = nt_dot(keys, wide)
        score_sc[pair % 2, pages * page_len :, :] = jnp.where(new_valid, nt_dot(nk_ref[0, 0, :, at], both), NEG_FILL)

    score(0)
    for pair in range(pairs):
        at = slice(pair * 128, pair * 128 + 128)
        if pair + 1 < pairs:
            score(pair + 1)
        cuts = [slice(i * page_len, (i + 1) * page_len) for i in range(pages)] + [slice(pages * page_len, None)]
        tops = [jnp.max(score_sc[pair % 2, cut, :], axis=0, keepdims=True) for cut in cuts]
        top = functools.reduce(jnp.maximum, tops).astype(BF16).astype(F32)
        weights = [jnp.exp(score_sc[pair % 2, cut, :] - top) for cut in cuts]
        den = functools.reduce(jnp.add, [jnp.sum(w, axis=0, keepdims=True) for w in weights])
        low = jnp.concatenate([w.astype(BF16) for w in weights[:-1]], axis=0)
        values = jnp.concatenate([v_ref[0, i, 0, :, at] for i in range(pages)], axis=0)
        num = tn_dot(values, low) + tn_dot(nv_ref[0, 0, :, at], weights[-1].astype(BF16))
        num = jnp.where(row < HD, num[:, :new_len], num[:, new_len:]).astype(BF16)
        for piece in range(4):
            index = (group * pairs + pair) * 4 + piece
            dest = index // (share // 32)
            offset = pl.multiple_of((index - dest * (share // 32)) * 32, 32)
            side = (dest + place[0]) % 2
            sum_sc[side, dest // 2, pl.ds(offset, 32), pl.ds(lane_at, new_len)] = num[piece * 32 : piece * 32 + 32]
        head = (group * pairs + pair) * 2
        for half in range(2):
            lanes = slice(half * new_len, half * new_len + new_len)
            top_sc[head + half, :, pl.ds(lane_at, new_len)] = top[:, lanes]
            den_sc[head + half, :, pl.ds(lane_at, new_len)] = den[:, lanes]

    @pl.when((req == pl.num_programs(0) - 1) & (group == pl.num_programs(1) - 1))
    def _():
        for dest in range(groups):
            first = dest * share // HD
            stats = jnp.concatenate([top_sc[first : first + 8, 0, :], den_sc[first : first + 8, 0, :]], axis=0)
            sum_sc[(dest + place[0]) % 2, dest // 2, share : share + STAT_ROWS, :] = stats.astype(BF16)
        keep_ref[...] = sum_sc[0]
        send_ref[...] = sum_sc[1]


def attend(table, length, place, queries, cache_pool, new_kv, dests):
    req_here, new_len, width = queries.shape
    pages, page_len = cache_pool.shape[1], cache_pool.shape[3]
    local_new = new_kv.shape[2]
    share = width // dests
    groups = 3
    block = width // groups
    heads = width // HD
    keys = pages * page_len + local_new
    return pl.pallas_call(
        functools.partial(attend_kernel, share=share),
        grid_spec=pltpu.PrefetchScalarGridSpec(
            num_scalar_prefetch=3,
            grid=(req_here, groups),
            in_specs=[
                pl.BlockSpec((1, new_len, block), lambda r, g, *_: (r, 0, g)),
                pl.BlockSpec((1, pages, 1, page_len, block), lambda r, g, *_: (r, 0, 0, 0, g)),
                pl.BlockSpec((1, pages, 1, page_len, block), lambda r, g, *_: (r, 0, 1, 0, g)),
                pl.BlockSpec((1, 1, local_new, block), lambda r, g, *_: (r, 0, 0, g)),
                pl.BlockSpec((1, 1, local_new, block), lambda r, g, *_: (r, 1, 0, g)),
            ],
            out_specs=[pl.BlockSpec((dests // 2, share + STAT_ROWS, req_here * new_len), lambda r, g, *_: (0, 0, 0))] * 2,
            scratch_shapes=[pltpu.VMEM((2, keys, 2 * new_len), F32)]
            + [pltpu.VMEM((2, dests // 2, share + STAT_ROWS, req_here * new_len), BF16)]
            + [pltpu.VMEM((heads + 12, 1, req_here * new_len), F32)] * 2,
        ),
        out_shape=[jax.ShapeDtypeStruct((dests // 2, share + STAT_ROWS, req_here * new_len), BF16)] * 2,
        cost_estimate=pl.CostEstimate(
            flops=4 * req_here * new_len * width * keys,
            bytes_accessed=cache_pool.size * 2 + queries.size * 2,
            transcendentals=req_here * heads * new_len * keys,
        ),
        compiler_params=pltpu.CompilerParams(vmem_limit_bytes=60 << 20),
        name="attend",
    )(table, length, place, queries, cache_pool, cache_pool, new_kv, new_kv)


def merge_kernel(place, own_ref, other_ref, *refs, share):
    outs, spread_sc = refs[:-1], refs[-1]
    tokens = own_ref.shape[2]
    offset = pl.multiple_of(place[0] % 2 * (HD // 2), HD // 2)
    both = (own_ref, other_ref)
    for step, out_ref in enumerate(outs):
        dest = (place[0] // 2 + step) % len(outs)
        tops = [ref[dest, share : share + 8, :].astype(F32) for ref in both]
        top = jnp.maximum(*tops)
        scales = [jnp.exp(t - top) for t in tops]
        den = functools.reduce(jnp.add, [s * ref[dest, share + 8 : share + 16, :].astype(F32) for s, ref in zip(scales, both)])
        total = None
        for side, ref in enumerate(both):
            for head in range(5):
                spread_sc[side, head * HD : head * HD + HD, :] = jnp.broadcast_to(scales[side][head : head + 1, :], (HD, tokens))
            term = ref[dest, :share, :].astype(F32) * spread_sc[side, pl.ds(offset, share), :]
            total = term if total is None else total + term
        out_ref[:share, :] = total.astype(BF16)
        out_ref[share:, :] = jnp.concatenate([top, den], axis=0).astype(BF16)


def merge(place, own, other):
    dests, rows, tokens = own.shape
    whole = pl.BlockSpec((dests, rows, tokens), lambda i, *_: (0, 0, 0))
    return pl.pallas_call(
        functools.partial(merge_kernel, share=rows - STAT_ROWS),
        grid_spec=pltpu.PrefetchScalarGridSpec(
            num_scalar_prefetch=1,
            grid=(1,),
            in_specs=[whole, whole],
            out_specs=[pl.BlockSpec((rows, tokens), lambda i, *_: (0, 0))] * dests,
            scratch_shapes=[pltpu.VMEM((2, 5 * HD, tokens), F32)],
        ),
        out_shape=[jax.ShapeDtypeStruct((rows, tokens), BF16)] * dests,
        cost_estimate=pl.CostEstimate(flops=4 * own.size, bytes_accessed=6 * own.size, transcendentals=0),
        compiler_params=pltpu.CompilerParams(vmem_limit_bytes=10 << 20),
        name="merge",
    )(place, own, other)


def join_kernel(place, *refs, share, groups):
    recv_refs, (res_ref, gain_ref, slot_ref) = refs[:groups], refs[groups : groups + 3]
    outs, (hidden_ref, spread_sc) = refs[groups + 3 : -2], refs[-2:]
    tokens = hidden_ref.shape[1]
    rows, padded = outs[0].shape
    slots = len(outs) * rows
    tops = [ref[share : share + 8, :].astype(F32) for ref in recv_refs]
    top = functools.reduce(jnp.maximum, tops)
    scales = [jnp.exp(t - top) for t in tops]
    den = functools.reduce(jnp.add, [s * ref[share + 8 : share + 16, :].astype(F32) for s, ref in zip(scales, recv_refs)])
    offset = pl.multiple_of(place[0] % 2 * (HD // 2), HD // 2)
    total = res_ref[...]
    for g, ref in enumerate(recv_refs):
        factor = scales[g] / den
        for head in range(5):
            spread_sc[g, head * HD : head * HD + HD, :] = jnp.broadcast_to(factor[head : head + 1, :], (HD, tokens))
        total = total + ref[:share, :].astype(F32) * spread_sc[g, pl.ds(offset, share), :]
    hidden_ref[...] = total
    square = jnp.sum(total * total, axis=0, keepdims=True)
    high = square.astype(BF16).astype(F32)
    row = lax.broadcasted_iota(jnp.int32, (padded - share, tokens), 0)
    tail = jnp.where(row == 0, high, jnp.where(row == 1, square - high, 0.0)).astype(BF16)
    filled = jnp.concatenate([(total * gain_ref[...]).astype(BF16), tail], axis=0)
    at = lax.broadcasted_iota(jnp.int32, (slots, tokens), 0) + place[0] * rows
    at = jnp.where(at < slots, at, at - slots)
    picks = (at == slot_ref[0:1, :]) | (at == slot_ref[1:2, :])
    placed = nt_dot(jnp.where(picks, 1.0, 0.0).astype(BF16), filled).astype(BF16)
    for i, out in enumerate(outs):
        out[...] = placed[i * rows : i * rows + rows]


def join(place, recv, residual, gain, slots, experts):
    rows, tokens = recv[0].shape
    share = rows - STAT_ROWS
    padded = -(-(share + 2) // 128) * 128
    whole = lambda *shape: pl.BlockSpec(shape, lambda i, *_: (0,) * len(shape))
    return pl.pallas_call(
        functools.partial(join_kernel, share=share, groups=len(recv)),
        grid_spec=pltpu.PrefetchScalarGridSpec(
            num_scalar_prefetch=1,
            grid=(1,),
            in_specs=[whole(rows, tokens)] * len(recv) + [whole(share, tokens), whole(share, 1), whole(2, tokens)],
            out_specs=[whole(CAP, padded)] * experts + [whole(share, tokens)],
            scratch_shapes=[pltpu.VMEM((len(recv), 5 * HD, tokens), F32)],
        ),
        out_shape=[jax.ShapeDtypeStruct((CAP, padded), BF16)] * experts + [jax.ShapeDtypeStruct((share, tokens), F32)],
        cost_estimate=pl.CostEstimate(
            flops=2 * experts * CAP * padded * tokens, bytes_accessed=8 * rows * tokens + experts * CAP * padded * 2, transcendentals=0
        ),
        compiler_params=pltpu.CompilerParams(vmem_limit_bytes=10 << 20),
        name="join",
    )(place, *recv, residual, gain, slots)


def norm_kernel(*refs, share):
    recv_refs, out_ref = refs[:-1], refs[-1]
    blocks = [ref[...].astype(F32) for ref in recv_refs]
    square = functools.reduce(jnp.add, [b[:, share : share + 1] + b[:, share + 1 : share + 2] for b in blocks])
    scale = lax.rsqrt(square / (len(blocks) * share) + EPSILON)
    out_ref[...] = jnp.concatenate([b[:, :share] * scale for b in blocks], axis=1).astype(BF16)


def norm_rows(recv, share):
    rows, padded = recv[0].shape
    return pl.pallas_call(
        functools.partial(norm_kernel, share=share),
        out_shape=jax.ShapeDtypeStruct((rows, len(recv) * share), BF16),
        cost_estimate=pl.CostEstimate(flops=0, bytes_accessed=len(recv) * rows * padded * 4, transcendentals=0),
        compiler_params=pltpu.CompilerParams(vmem_limit_bytes=4 << 20),
        name="norm_rows",
    )(*recv)


def stack_kernel(*refs):
    blocks, outs = refs[:4], refs[4:]
    for i, ref in enumerate(blocks):
        outs[i // 2][i % 2] = ref[...]


def stack(blocks):
    rows, width = blocks[0].shape
    pairs = pl.pallas_call(
        stack_kernel,
        out_shape=[jax.ShapeDtypeStruct((2, rows, width), BF16)] * 2,
        cost_estimate=pl.CostEstimate(flops=0, bytes_accessed=16 * rows * width, transcendentals=0),
        compiler_params=pltpu.CompilerParams(vmem_limit_bytes=4 << 20),
        name="stack",
    )(*blocks)
    return [pair.reshape(2 * rows, width) for pair in pairs]


def expert_kernel(place, *refs, count):
    blocks, gate_up_hbm, down_hbm = refs[:count], refs[count], refs[count + 1]
    outs, (x_sc, part_sc, gate_up_sc, down_sc, both_sc, y_sc, sems) = refs[count + 2 : -7], refs[-7:]
    rows, out_rows, units = blocks[0].shape[0], outs[0].shape[0], down_sc.shape[1]
    half = gate_up_sc.shape[1] // 2
    tile = 256
    loads = [pltpu.make_async_copy(b, x_sc.at[pl.ds(i * rows, rows)], sems.at[i]) for i, b in enumerate(blocks)]
    groups, _, share, _ = gate_up_hbm.shape
    parts = []
    for g in range(groups):
        source = (place[0] + groups - g) % groups
        parts.append(pltpu.make_async_copy(gate_up_hbm.at[source], part_sc.at[g], sems.at[count + 2 + len(outs) + g]))
    down_load = pltpu.make_async_copy(down_hbm, down_sc, sems.at[count + 1])
    for load in (*parts, *loads, down_load):
        load.start()
    for g in range(groups):
        parts[g].wait()
        at = slice(g * share, g * share + share)
        gate_up_sc[at, :units] = part_sc[g, 0]
        gate_up_sc[at, half : half + units] = part_sc[g, 1]
    for load in loads:
        load.wait()

    @pl.loop(0, 2 * half // tile)
    def _(j):
        lanes = pl.ds(pl.multiple_of(j * tile, tile), tile)
        both_sc[:, lanes] = jnp.dot(x_sc[...], gate_up_sc[:, lanes], preferred_element_type=F32)

    gate, up = both_sc[:, :units], both_sc[:, half : half + units]
    act = (gate / (1.0 + jnp.exp(-gate)) * up).astype(BF16)
    down_load.wait()

    @pl.loop(0, down_sc.shape[0] // tile)
    def _(j):
        lanes = pl.ds(pl.multiple_of(j * tile, tile), tile)
        y_sc[:, lanes] = nt_dot(act, down_sc[lanes, :]).astype(BF16)
        for i, out in enumerate(outs):
            at = pl.ds(i * out_rows, out_rows)
            pltpu.make_async_copy(y_sc.at[at, lanes], out.at[:, lanes], sems.at[count + 2 + i]).start()

    for i, out in enumerate(outs):
        pltpu.make_async_copy(y_sc.at[pl.ds(i * out_rows, out_rows)], out, sems.at[count + 2 + i]).wait()


def expert(place, blocks, gate_up, down, out_rows):
    rows, width = blocks[0].shape
    units = down.shape[1]
    count = len(blocks)
    total = count * rows
    packed = 2 * (-(-units // 128) * 128)
    anywhere = pl.BlockSpec(memory_space=pltpu.HBM)
    return pl.pallas_call(
        functools.partial(expert_kernel, count=count),
        in_specs=[pl.BlockSpec(memory_space=pltpu.SMEM)] + [anywhere] * (count + 2),
        out_specs=[anywhere] * (total // out_rows),
        out_shape=[jax.ShapeDtypeStruct((out_rows, width), BF16)] * (total // out_rows),
        scratch_shapes=[
            pltpu.VMEM((total, width), BF16),
            pltpu.VMEM(gate_up.shape, BF16),
            pltpu.VMEM((width, packed), BF16),
            pltpu.VMEM(down.shape, BF16),
            pltpu.VMEM((total, packed), F32),
            pltpu.VMEM((total, width), BF16),
            pltpu.SemaphoreType.DMA((count + 2 + total // out_rows + gate_up.shape[0],)),
        ],
        cost_estimate=pl.CostEstimate(
            flops=6 * total * width * units,
            bytes_accessed=4 * total * width + 6 * width * units,
            transcendentals=total * units,
        ),
        compiler_params=pltpu.CompilerParams(vmem_limit_bytes=60 << 20),
        name="expert",
    )(place, *blocks, gate_up, down)


def total_of(refs):
    return functools.reduce(jnp.add, [ref[...].astype(F32) for ref in refs])


def add_kernel(*refs):
    outs = refs[6:]
    rows = outs[0].shape[0]
    for i, out in enumerate(outs):
        at = slice(i % 2 * rows, i % 2 * rows + rows)
        lower = slice((i % 2 + 2) * rows, (i % 2 + 3) * rows)
        first, second, third = refs[:3] if i < 2 else refs[3:6]
        total = first[at, :].astype(F32) + second[at, :].astype(F32) + third[lower, :].astype(F32)
        out[...] = total.astype(BF16)


def add_blocks(low, high):
    rows, width = low[0].shape
    return pl.pallas_call(
        add_kernel,
        out_shape=[jax.ShapeDtypeStruct((rows // 2, width), BF16)] * 4,
        cost_estimate=pl.CostEstimate(flops=0, bytes_accessed=16 * rows * width, transcendentals=0),
        compiler_params=pltpu.CompilerParams(vmem_limit_bytes=8 << 20),
        name="add_blocks",
    )(*low, *high)


def finish_kernel(*refs):
    out_ref = refs[-1]
    groups, _, share = out_ref.shape
    both = jnp.concatenate([total_of(refs[:4]), total_of(refs[4:8])], axis=0).astype(BF16)
    for g in range(groups):
        out_ref[g] = both[:, g * share : (g + 1) * share]


def finish(blocks, groups):
    rows, width = blocks[0].shape
    return pl.pallas_call(
        finish_kernel,
        out_shape=jax.ShapeDtypeStruct((groups, 2 * rows, width // groups), BF16),
        cost_estimate=pl.CostEstimate(flops=0, bytes_accessed=20 * rows * width, transcendentals=0),
        compiler_params=pltpu.CompilerParams(vmem_limit_bytes=8 << 20),
        name="finish",
    )(*blocks)


def mix_kernel(rows_ref, slot_ref, weight_ref, hidden_ref, out_ref):
    tokens = out_ref.shape[1]
    slots = rows_ref.shape[0]
    at = lax.broadcasted_iota(jnp.int32, (slots, tokens), 0)
    table = jnp.where(at == slot_ref[0:1, :], weight_ref[0:1, :], 0.0)
    table = table + jnp.where(at == slot_ref[1:2, :], weight_ref[1:2, :], 0.0)
    high = table.astype(BF16)
    low = (table - high.astype(F32)).astype(BF16)
    rows = rows_ref[...]
    out_ref[...] = (hidden_ref[...] + (tn_dot(rows, high) + tn_dot(rows, low))).astype(BF16)


def mix(rows, slots, weights, hidden):
    return pl.pallas_call(
        mix_kernel,
        out_shape=jax.ShapeDtypeStruct(hidden.shape, BF16),
        cost_estimate=pl.CostEstimate(flops=4 * hidden.size * rows.shape[0], bytes_accessed=rows.size * 2 + hidden.size * 6, transcendentals=0),
        compiler_params=pltpu.CompilerParams(vmem_limit_bytes=6 << 20),
        name="mix",
    )(rows, slots, weights, hidden)


def ring_pairs(axis, step):
    pairs = []
    for index in range(RING * RING):
        y, z = divmod(index, RING)
        if axis == "y":
            y = (y + step) % RING
        else:
            z = (z + step) % RING
        pairs.append((index, y * RING + z))
    return pairs


def shift(x, axis, step):
    return lax.ppermute(x, "wide", ring_pairs(axis, step))


def local(
    queries,
    new_kv,
    cache_pool,
    page_table,
    cached_len,
    residual,
    norm_gain,
    expert_ids,
    route_weight,
    w_gate_up,
    w_down,
):
    narrow_count = lax.axis_size("narrow")
    narrow_pos = lax.axis_index("narrow").astype(jnp.int32)
    _, _, width = queries.shape
    token_rows = expert_ids.shape[0]
    expert_count = w_gate_up.shape[0]
    units = w_down.shape[1]
    share = width // narrow_count

    def exchange(x):
        return lax.all_to_all(x, "narrow", 0, 0, tiled=True)

    down_all = exchange(jnp.transpose(w_down, (0, 2, 1)))
    place = narrow_pos.reshape(1)
    own, other = attend(page_table, cached_len, place, queries, cache_pool, new_kv, narrow_count)
    other = lax.ppermute(other, "narrow", [(i, i ^ 1) for i in range(narrow_count)])

    def along(x, step):
        return lax.ppermute(x, "narrow", [(i, (i + step) % narrow_count) for i in range(narrow_count)])

    merged = list(merge(place, own, other))
    w_gate_up, down_all, merged[0] = lax.optimization_barrier((w_gate_up, down_all, merged[0]))
    sums = merged[:1]
    for step in range(1, len(merged)):
        sums.append(along(merged[step], 2 * step))
    w_gate_up, sums[1] = lax.optimization_barrier((jnp.transpose(w_gate_up, (0, 2, 1, 3)), sums[1]))
    gate_up_all = exchange(w_gate_up)

    flat_ids = expert_ids.reshape(token_rows * 2)
    onehot = (flat_ids[:, None] == jnp.arange(expert_count, dtype=jnp.int32)[None, :]).astype(BF16)
    order = jnp.arange(token_rows * 2, dtype=jnp.int32)
    earlier = jnp.dot((order[:, None] > order[None, :]).astype(BF16), onehot, preferred_element_type=F32)
    position = jnp.sum(earlier * onehot.astype(F32), axis=1).astype(jnp.int32)
    slots = (flat_ids * CAP + position).reshape(token_rows, 2)

    res_share = lax.dynamic_slice_in_dim(residual, narrow_pos * share, share, 1).astype(F32).T
    gain_share = lax.dynamic_slice_in_dim(norm_gain, narrow_pos * share, share, 0)[:, None]
    *placed, hidden = join(place, sums, res_share, gain_share, slots.T, expert_count)
    for step in range(1, narrow_count):
        placed[step] = along(placed[step], step)
    rows = norm_rows(placed, share)
    down_all = down_all.reshape(width, units)

    half = CAP // 2

    def around(block, axis):
        return [block, *(shift(block, axis, step) for step in STEPS)]

    early, late = [], []
    for first, second, block in (("z", "y", rows[:half]), ("y", "z", rows[half:])):
        low, high = stack(around(block, first))
        before_low, after_high = shift(low, second, 1), shift(high, second, -1)
        before_high, after_low = shift(high, second, 1), shift(low, second, -1)
        far_low, far_high = shift(before_low, second, 1), shift(after_high, second, -1)
        early += [far_low, after_high, far_high, before_low]
        late += [low, high, after_low, before_high]
    early = list(expert(place, early, gate_up_all, down_all, 2 * CAP))
    early[0], *late = lax.optimization_barrier((early[0], *late))
    late = expert(place, late, gate_up_all, down_all, CAP)

    def back(blocks, axis):
        return [blocks[0], *(shift(block, axis, -step) for block, step in zip(blocks[1:], STEPS))]

    def joined(a, b):
        return (a.astype(F32) + b.astype(F32)).astype(BF16)

    four = []
    for color, second in enumerate(("y", "z")):
        low, high, after_low, before_high = late[4 * color : 4 * color + 4]
        got = []
        for block, step in zip(early[2 * color : 2 * color + 2], (1, -1)):
            got.append(shift(block, second, step))
        more_low, more_high = (
            shift(joined(after_low, got[0][:CAP]), second, 1),
            shift(joined(before_high, got[1][:CAP]), second, -1),
        )
        four.append(add_blocks([low, more_low, got[1]], [high, more_high, got[0]]))
    out_rows = finish([*back(four[0], "z"), *back(four[1], "y")], narrow_count)
    out_rows = exchange(out_rows)
    return mix(out_rows.reshape(expert_count * CAP, share), slots.T, route_weight.T, hidden).T


def solution(mesh):
    return jax.shard_map(
        local,
        mesh=mesh,
        in_specs=(
            P("wide", None, None),
            P("wide", None, "narrow", None),
            P("wide", "narrow", None, None, None),
            P("wide", None),
            P("wide"),
            P("wide", None),
            P(),
            P("wide", None),
            P("wide", None),
            P(None, "narrow", None, "wide"),
            P(None, "wide", "narrow"),
        ),
        out_specs=P("wide", "narrow"),
        check_vma=False,
    )
```
